128 devices in a mesh: dp: 16 (over z, y_hi, core), seq: 8 (over x, y_lo).
Axes of the slice: x: 4, y: 4 (y_hi: 2, y_lo: 2; y = y_hi * 2 + y_lo), z: 4, core: 2. Of those that a mesh axis runs over, the one named last changes fastest.
Arguments:
- streams: bfloat16 [3, 16, 2048, 512], P(None, 'dp', 'seq'), may hold values from -6 to 6
- short_filter: float32 [3, 3, 512], replicated, may hold values from -3 to 3
- long_filter: float32 [2048, 512], P('seq'), may hold values from -4 to 4
- skip_gain: float32 [512], replicated, may hold values from -4 to 4
- out_weight: bfloat16 [512, 4096], replicated, may hold values from -0.25 to 0.25
- out_grad: bfloat16 [16, 2048, 4096], P('dp', 'seq'), may hold values from -6 to 6
Outputs:
- layer_out: bfloat16 [16, 2048, 4096], P('dp', 'seq')
- grad_streams: bfloat16 [3, 16, 2048, 512], P(None, 'dp', 'seq')
- grad_filter: float32 [2048, 512], P('seq')
- grad_out_weight: float32 [512, 4096], replicated
The draws below stay inside these ranges and needn't reach their ends.
All inputs are finite; a program needn't handle non-finite values.
Results may differ from the reference program's by a relative error of at most 0.0049.
Values may be sent and summed in bfloat16 or wider, within the bound.
No kernel may reach another device: no remote copies, remote signals or barrier semaphores. Data moves between devices by JAX's collectives and lax.ppermute only.
A program may use at most 128 MiB of HBM per device.

```python
import math
import jax
import jax.numpy as jnp
from jax import lax

D = 4096
C = 512
B = 16
L = 2048


def draw_long_filter(key, part):
    key_rate = jax.random.fold_in(key, 11)
    key_noise = jax.random.fold_in(key, 23)
    steps_at = lax.broadcasted_iota(jnp.int32, (L, C), 0).astype(jnp.float32)
    lowest = math.log(0.1 / L)
    highest = math.log(1.0 / 30.0)
    rough = jnp.clip(jax.random.normal(key_noise, (L, C), jnp.float32), -4.0, 4.0)
    rates = jnp.exp(jax.random.uniform(key_rate, (1, C), jnp.float32, lowest, highest))
    norming = jnp.sqrt((1.0 - jnp.exp(-2.0 * rates)) / (1.0 - jnp.exp(-2.0 * rates * L)))
    return rough * jnp.exp(-rates * steps_at) * norming


def level_of(stream_key, shape, cuts, low, largest):
    def one(dim, blocks):
        heights = jax.random.uniform(jax.random.fold_in(jax.random.fold_in(stream_key, 6), dim), (blocks,), jnp.float32, low / len(cuts), largest / len(cuts))
        return jnp.repeat(jnp.exp(heights), shape[dim] // blocks).reshape((-1,) + (1,) * (len(shape) - dim - 1))

    factor_of = one(*cuts[0])
    for cut in cuts[1:]:
        factor_of = factor_of * one(*cut)
    return factor_of


def centred(rng, shape, width, reach, split=(), held_as=jnp.bfloat16):
    result = jax.random.normal(rng, shape, jnp.float32) * width
    if len(split) > 0:
        result = level_of(rng, shape, split, -0.22, 0.18) * result
    return jnp.clip(result, min=-reach, max=reach).astype(held_as)


def setup_inputs(seed: int = 0) -> dict:
    key_list = jax.random.split(jax.random.key(seed), 7)
    streams = centred(key_list[0], (3, B, L, C), 1.0, 6.0, ((1, 16), (2, 8)))
    short_filter = centred(key_list[1], (3, 3, C), 0.6, 3.0, (), jnp.float32)
    long_filter = draw_long_filter(jax.random.fold_in(key_list[6], 71), 0)
    skip_gain = centred(key_list[3], (C,), 1.0, 4.0, (), jnp.float32)
    out_weight = centred(key_list[4], (C, D), C ** -0.5, 0.25)
    out_grad = centred(key_list[5], (B, L, D), 1.0, 6.0, ((0, 16), (1, 8)))
    return dict(streams=streams, short_filter=short_filter, long_filter=long_filter, skip_gain=skip_gain, out_weight=out_weight, out_grad=out_grad)


def reference(streams, short_filter, long_filter, skip_gain, out_weight, out_grad):
    inputs = streams.astype(jnp.float32)
    padded = jnp.pad(inputs, ((0, 0), (0, 0), (2, 0), (0, 0)))
    shortened = sum((short_filter[:, offset, None, None, :] * padded[:, :, 2 - offset:2 - offset + L, :] for offset in range(3)))
    gate_out, gate_in, value_stream = (shortened[0], shortened[1], shortened[2])
    product = gate_in * value_stream
    padded_length = 2 * L
    product_spectrum = jnp.fft.rfft(product, n=padded_length, axis=1)
    filter_spectrum = jnp.fft.rfft(long_filter, n=padded_length, axis=0)[None]
    convolved = jnp.fft.irfft(product_spectrum * filter_spectrum, n=padded_length, axis=1)[:, :L] + skip_gain * product
    mixed_out = (gate_out * convolved).astype(jnp.bfloat16)
    mixed_flat = mixed_out.reshape(B * L, C)
    grad_flat = out_grad.reshape(B * L, D)
    layer_out = jnp.dot(mixed_flat, out_weight, preferred_element_type=jnp.float32).astype(jnp.bfloat16).reshape(B, L, D)
    grad_mixed = jnp.dot(grad_flat, out_weight.T, preferred_element_type=jnp.float32).reshape(B, L, C)
    grad_scale = 1.0 / math.sqrt(B * L)
    grad_out_weight = grad_scale * jnp.dot(mixed_flat.T, grad_flat, preferred_element_type=jnp.float32)
    grad_conv = grad_mixed * gate_out
    grad_gate_out = grad_mixed * convolved
    grad_spectrum = jnp.fft.rfft(grad_conv, n=padded_length, axis=1)
    grad_product = jnp.fft.irfft(jnp.conj(filter_spectrum) * grad_spectrum, n=padded_length, axis=1)[:, :L] + skip_gain * grad_conv
    filter_terms = lax.optimization_barrier(jnp.sum(jnp.conj(product_spectrum) * grad_spectrum, axis=0))
    grad_filter = grad_scale * jnp.fft.irfft(filter_terms, n=padded_length, axis=0)[:L]
    grad_shortened = jnp.stack([grad_gate_out, grad_product * value_stream, grad_product * gate_in])
    padded_grad = jnp.pad(grad_shortened, ((0, 0), (0, 0), (0, 2), (0, 0)))
    grad_streams = sum((short_filter[:, offset, None, None, :] * padded_grad[:, :, offset:offset + L, :] for offset in range(3)))
    return (layer_out, grad_streams.astype(jnp.bfloat16), grad_filter, grad_out_weight)
```

```python
import functools
import math

import jax
import jax.numpy as jnp
import numpy as np
from jax import lax
from jax.experimental import pallas as pl
from jax.experimental.pallas import tpu as pltpu
from jax.sharding import Mesh, PartitionSpec as P

BF = jnp.bfloat16
F32 = jnp.float32
BLOCK = 256
HALF = 64
SEQ = ("x", "yl")
DEPTH = ("z", "yh")
CHIPS = DEPTH + SEQ


@functools.lru_cache(maxsize=None)
def tables():
    order = np.concatenate([np.arange(0, BLOCK, 2), np.arange(1, BLOCK, 2)])
    angle = np.pi * ((2 * order[:, None] + 1) * np.arange(BLOCK)[None, :] % 1024) / 512.0
    ahead = np.concatenate([np.cos(angle), -np.sin(angle)], axis=0)
    back = ahead.T / BLOCK

    def two(table):
        table = table.astype(np.float32)
        high = table.astype(jnp.bfloat16)
        return high, (table - high.astype(np.float32)).astype(jnp.bfloat16)

    return two(ahead) + two(back)


def mm(a, b):
    return jnp.dot(a, b, preferred_element_type=F32)


def low_lanes(rows):
    return lax.broadcasted_iota(jnp.int32, (rows, 128), 1) < HALF


def turned(x):
    return pltpu.roll(x, HALF, 1)


def pack_kernel(streams, out_grad, weight, filt, packed, total):
    step = pl.program_id(0)

    @pl.when(step == 0)
    def _():
        total[...] = jnp.zeros_like(total)

    total[...] += lax.dot_general(
        out_grad[...], weight[...], (((1,), (1,)), ((), ())), preferred_element_type=F32
    )

    @pl.when(step == pl.num_programs(0) - 1)
    def _():
        low = low_lanes(BLOCK)
        for q in range(4):
            lanes = slice(128 * q, 128 * q + 128)
            whole = filt[:, lanes]
            high = whole.astype(BF).astype(F32)
            pairs = (
                (streams[0, :, lanes].astype(F32), streams[1, :, lanes].astype(F32)),
                (streams[2, :, lanes].astype(F32), total[:, lanes]),
                (high, whole - high),
            )
            for n, (a, b) in enumerate(pairs):
                there = slice(128 * n, 128 * n + 128)
                packed[2 * q, :, there] = jnp.where(low, a, turned(b)).astype(BF)
                packed[2 * q + 1, :, there] = jnp.where(low, turned(a), b).astype(BF)


def pack(streams, out_grad, weight, filt):
    steps = 4
    wide = out_grad.shape[1] // steps
    return pl.pallas_call(
        pack_kernel,
        grid=(steps,),
        in_specs=[
            pl.BlockSpec((3, BLOCK, 512), lambda k: (0, 0, 0)),
            pl.BlockSpec((BLOCK, wide), lambda k: (0, k)),
            pl.BlockSpec((512, wide), lambda k: (0, k)),
            pl.BlockSpec((BLOCK, 512), lambda k: (0, 0)),
        ],
        out_specs=pl.BlockSpec((8, BLOCK, 384), lambda k: (0, 0, 0)),
        out_shape=jax.ShapeDtypeStruct((8, BLOCK, 384), BF),
        scratch_shapes=[pltpu.VMEM((BLOCK, 512), F32)],
        name="pack",
    )(streams, out_grad, weight, filt)


def conv_kernel(
    place, got, short, skip, ahead_h, ahead_l, back_h, back_l,
    sent, lags,
    sa_pad, sv_pad, sa, sv, prod, spec, fspec, res, lres, time, u_pad, x_pad,
):
    low = low_lanes(BLOCK)
    low1 = low_lanes(1)
    sigma = jnp.where(low, 1.0, -1.0)
    odd = place[0] % 2 == 1

    taps = short[...]
    taps = jnp.where(odd, turned(taps), taps)
    taps_up = turned(taps)
    gain = skip[...]
    gain = jnp.where(odd, turned(gain), gain)
    gain = jnp.where(low1, gain, turned(gain))

    def tap(i, j):
        return taps[3 * i + j : 3 * i + j + 1]

    def tap_up(i, j):
        return taps_up[3 * i + j : 3 * i + j + 1]

    def unit(j):
        return jnp.full((1, 128), 1.0 if j == 0 else 0.0, F32)

    w_a = [jnp.where(low1, tap(0, j), tap_up(1, j)) for j in range(3)]
    w_v = [jnp.where(low1, tap(2, j), unit(j)) for j in range(3)]
    w_u = [jnp.where(low1, tap(1, j), tap_up(0, j)) for j in range(3)]
    w_x = [jnp.where(low1, unit(j), tap_up(2, j)) for j in range(3)]

    def split(x):
        high = x.astype(BF)
        return high, (x - high.astype(F32)).astype(BF)

    def apply(table_h, table_l, high, rest):
        both = mm(table_h[...], jnp.concatenate([high, rest], axis=1))
        return both[:, :128] + both[:, 128:] + mm(table_l[...], high)

    sa_pad[0:8] = jnp.zeros((8, 128), F32)
    sv_pad[0:8] = jnp.zeros((8, 128), F32)

    def unpack(b, carry):
        rows = pl.ds(pl.multiple_of(8 + BLOCK * b, 8), BLOCK)
        sa_pad[rows] = got[b, :, 0:128].astype(F32)
        sv_pad[rows] = got[b, :, 128:256].astype(F32)
        f = got[b, :, 256:384].astype(F32)
        g = turned(f)
        high = jnp.where(low, f, g).astype(BF)
        rest = jnp.where(low, g, f).astype(BF)
        fspec[b] = apply(ahead_h, ahead_l, high, rest)
        return carry

    lax.fori_loop(0, 8, unpack, 0)

    for b in range(8):
        start = 8 + BLOCK * b
        a = sum(w_a[j] * sa_pad[start - j : start - j + BLOCK] for j in range(3))
        v = sum(w_v[j] * sv_pad[start - j : start - j + BLOCK] for j in range(3))
        sa[b] = a
        sv[b] = v
        prod[b] = turned(a) * v

    def transform(b, carry):
        high, rest = split(jnp.where(low, prod[b], prod[7 - b]))
        out = apply(ahead_h, ahead_l, high, rest)
        spec[b, 0:BLOCK] = out[:BLOCK]
        spec[b, BLOCK:] = out[BLOCK:] * sigma
        return carry

    lax.fori_loop(0, 8, transform, 0)

    for sign, base in ((1.0, 0), (-1.0, 128)):

        def multiply(n, carry, sign=sign, base=base):
            re = pl.ds(pl.multiple_of(base + 8 * n, 8), 8)
            im = pl.ds(pl.multiple_of(BLOCK + base + 8 * n, 8), 8)
            own = [(spec[j, re], spec[j, im]) for j in range(8)]
            both = [own[0]]
            for j in range(1, 8):
                both.append(
                    (own[j][0] - sign * own[j - 1][1], own[j][1] + sign * own[j - 1][0])
                )
            filt = [(fspec[m, re], fspec[m, im]) for m in range(8)]

            def summed(pairs):
                first = True
                for (ar, ai), (br, bi) in pairs:
                    pr = ar * br - ai * bi
                    pi = ar * bi + ai * br
                    tr, ti = (pr, pi) if first else (tr + pr, ti + pi)
                    first = False
                return tr, ti

            for i in range(8):
                tr, ti = summed([(filt[m], both[i - m]) for m in range(i + 1)])
                res[i, re] = tr
                res[i, im] = ti
            moved = [(turned(r), turned(i)) for r, i in both]
            for m in range(8):
                tr, ti = summed([(own[7 - i], moved[i - m]) for i in range(m, 8)])
                lres[m, re] = tr
                lres[m, im] = ti
            return carry

        lax.fori_loop(0, 16, multiply, 0)

    def invert(b, carry):
        def one(src):
            x = jnp.concatenate([src[b, 0:BLOCK], src[b, BLOCK:] * sigma], axis=0)
            return apply(back_h, back_l, *split(x))

        time[b] = one(res)
        lag = one(lres)
        low16 = low_lanes(16)
        for k in range(8):
            a = lag[32 * k : 32 * k + 16]
            c = lag[32 * k + 16 : 32 * k + 32]
            lags[b, k] = jnp.where(low16, turned(a), c).astype(BF)
        return carry

    lax.fori_loop(0, 8, invert, 0)

    def gate(b, carry):
        t = jnp.where(low, time[b], time[7 - b]) + gain * prod[b]
        rows = pl.ds(pl.multiple_of(BLOCK * b, 8), BLOCK)
        u_pad[rows] = turned(t) * sv[b]
        x_pad[rows] = t * sa[b]
        return carry

    lax.fori_loop(0, 8, gate, 0)
    u_pad[8 * BLOCK :] = jnp.zeros((8, 128), F32)
    x_pad[8 * BLOCK :] = jnp.zeros((8, 128), F32)
    for b in range(8):
        start = BLOCK * b
        y = sum(w_u[j] * u_pad[start + j : start + j + BLOCK] for j in range(3))
        sent[b, :, 0:128] = y.astype(BF)
        y = sum(w_x[j] * x_pad[start + j : start + j + BLOCK] for j in range(3))
        sent[b, :, 128:256] = y.astype(BF)


def conv(place, got, short, skip):
    ahead_h, ahead_l, back_h, back_l = (jnp.asarray(t) for t in tables())
    full = lambda *shape: pl.BlockSpec(shape, lambda n, p: (0,) * len(shape))
    return pl.pallas_call(
        conv_kernel,
        grid_spec=pltpu.PrefetchScalarGridSpec(
            num_scalar_prefetch=1,
            grid=(1,),
            in_specs=[
                full(8, BLOCK, 384),
                pl.BlockSpec((9, 128), lambda n, p: (0, p[0] // 2)),
                pl.BlockSpec((1, 128), lambda n, p: (0, p[0] // 2)),
                full(512, BLOCK),
                full(512, BLOCK),
                full(BLOCK, 512),
                full(BLOCK, 512),
            ],
            out_specs=[full(8, BLOCK, 256), full(8, 8, 16, 128)],
            scratch_shapes=[
                pltpu.VMEM((8 + 8 * BLOCK, 128), F32),
                pltpu.VMEM((8 + 8 * BLOCK, 128), F32),
                pltpu.VMEM((8, BLOCK, 128), F32),
                pltpu.VMEM((8, BLOCK, 128), F32),
                pltpu.VMEM((8, BLOCK, 128), F32),
                pltpu.VMEM((8, 512, 128), F32),
                pltpu.VMEM((8, 512, 128), F32),
                pltpu.VMEM((8, 512, 128), F32),
                pltpu.VMEM((8, 512, 128), F32),
                pltpu.VMEM((8, BLOCK, 128), F32),
                pltpu.VMEM((8 + 8 * BLOCK, 128), F32),
                pltpu.VMEM((8 + 8 * BLOCK, 128), F32),
            ],
        ),
        out_shape=[
            jax.ShapeDtypeStruct((8, BLOCK, 256), BF),
            jax.ShapeDtypeStruct((8, 8, 16, 128), BF),
        ],
        name="conv",
    )(place, got, short, skip, ahead_h, ahead_l, back_h, back_l)


def unpack_kernel(got, mixed, grads):
    low = low_lanes(BLOCK)
    for q in range(4):
        lanes = slice(128 * q, 128 * q + 128)
        for n, (first, second) in enumerate(((grads.at[1], grads.at[0]), (mixed, grads.at[2]))):
            there = slice(128 * n, 128 * n + 128)
            a = got[2 * q, :, there].astype(F32)
            b = got[2 * q + 1, :, there].astype(F32)
            first[:, lanes] = jnp.where(low, a, turned(b)).astype(BF)
            second[:, lanes] = jnp.where(low, turned(a), b).astype(BF)


def unpack(got):
    return pl.pallas_call(
        unpack_kernel,
        out_shape=[
            jax.ShapeDtypeStruct((BLOCK, 512), BF),
            jax.ShapeDtypeStruct((3, BLOCK, 512), BF),
        ],
        name="unpack",
    )(got)


def partial_kernel(place, mine, theirs, grad_mine, grad_theirs, lags, packed):
    def term(mixed, grad):
        return lax.dot_general(
            mixed[...], grad[...], (((0,), (0,)), ((), ())), preferred_element_type=F32
        )

    part = (term(mine, grad_mine) + term(theirs, grad_theirs)).astype(BF)
    for s in range(8):
        for a in range(4):
            start = 64 * s + 16 * a
            packed[a, 0, s, :, 0:1024] = part[start : start + 16]
            packed[a, 0, s, :, 1024:1152] = lags[s, 2 * a + pl.program_id(0)]


def partial(place, mine, theirs, out_grad, grad_theirs, lags):
    return pl.pallas_call(
        partial_kernel,
        grid_spec=pltpu.PrefetchScalarGridSpec(
            num_scalar_prefetch=1,
            grid=(2,),
            in_specs=[
                pl.BlockSpec((BLOCK, 512), lambda h, p: (0, 0)),
                pl.BlockSpec((BLOCK, 512), lambda h, p: (0, 0)),
                pl.BlockSpec((BLOCK, 1024), lambda h, p: (0, 2 * p[0] + h)),
                pl.BlockSpec((BLOCK, 1024), lambda h, p: (0, h)),
                pl.BlockSpec((8, 8, 16, 128), lambda h, p: (0, 0, 0, 0)),
            ],
            out_specs=pl.BlockSpec((4, 1, 8, 16, 1152), lambda h, p: (0, h, 0, 0, 0)),
        ),
        out_shape=jax.ShapeDtypeStruct((4, 2, 8, 16, 1152), BF),
        name="partial",
    )(place, mine, theirs, out_grad, grad_theirs, lags)


def reduce_kernel(scale, got, shared):
    total = jnp.zeros((16, 1024), F32)
    for n in range(64):
        total = total + got[n, :, 0:1024].astype(F32)
    total = (total * scale).astype(BF)
    for k in range(8):
        shared[k, :, 0:1024] = total
    for s in range(8):
        lag = jnp.zeros((16, 128), F32)
        for k in range(8):
            lag = lag + got[8 * k + s, :, 1024:1152].astype(F32)
        lag = (lag * scale).astype(BF)
        for k in range(8):
            shared[k, :, 1024 + 128 * s : 1152 + 128 * s] = lag


def reduce(got, scale):
    return pl.pallas_call(
        functools.partial(reduce_kernel, scale),
        out_shape=jax.ShapeDtypeStruct((8, 16, 2048), BF),
        name="reduce",
    )(got)


def finish_kernel(place, mine, theirs, lag_mine, lag_theirs, grad_weight, grad_filter):
    core = place[0]
    for k in range(8):
        rows = slice(16 * (k // 2), 16 * (k // 2) + 16)
        for half, src in ((core, mine), (1 - core, theirs)):
            lanes = pl.ds(pl.multiple_of(2048 * half + 1024 * (k % 2), 1024), 1024)
            grad_weight[rows, lanes] = src[0, k].astype(F32)

    @pl.when(pl.program_id(0) == 0)
    def _():
        low = low_lanes(16)
        for k in range(8):
            for q in range(4):
                def both(s):
                    there = slice(128 * s, 128 * s + 128)
                    return lag_mine[k, :, there].astype(F32) + lag_theirs[k, :, there].astype(F32)

                a, b = both(2 * q), both(2 * q + 1)
                lanes = slice(128 * q, 128 * q + 128)
                grad_filter[32 * k : 32 * k + 16, lanes] = jnp.where(low, a, turned(b))
                grad_filter[32 * k + 16 : 32 * k + 32, lanes] = jnp.where(low, turned(a), b)


def finish(place, mine, theirs, lag_mine, lag_theirs):
    lag_spec = pl.BlockSpec((8, 16, 1024), lambda s, p: (0, 0, 0))
    half_spec = pl.BlockSpec((1, 8, 16, 1024), lambda s, p: (s, 0, 0, 0))
    return pl.pallas_call(
        finish_kernel,
        grid_spec=pltpu.PrefetchScalarGridSpec(
            num_scalar_prefetch=1,
            grid=(8,),
            in_specs=[half_spec, half_spec, lag_spec, lag_spec],
            out_specs=[
                pl.BlockSpec((64, 4096), lambda s, p: (s, 0)),
                pl.BlockSpec((BLOCK, 512), lambda s, p: (0, 0)),
            ],
        ),
        out_shape=[
            jax.ShapeDtypeStruct((512, 4096), F32),
            jax.ShapeDtypeStruct((BLOCK, 512), F32),
        ],
        name="finish",
    )(place, mine, theirs, lag_mine, lag_theirs)


def exchange(x, axes):
    return lax.all_to_all(x, axes, 0, 0, tiled=True)


def across(x):
    return lax.ppermute(x, "c", [(0, 1), (1, 0)])


def on_device(streams, short_filter, long_filter, skip_gain, out_weight, out_grad):
    scale = 1.0 / math.sqrt(16 * 2048)
    core = lax.axis_index("c").astype(jnp.int32)
    seq = lax.axis_index(SEQ).astype(jnp.int32)
    grad = out_grad[0]
    grad_theirs = across(lax.dynamic_slice(grad, (0, (1 - core) * 2048), (BLOCK, 2048)))
    got = exchange(pack(streams[:, 0], grad, out_weight, long_filter), SEQ)
    sent, lags = conv(
        seq[None], got, short_filter.reshape(9, 512), skip_gain.reshape(1, 512)
    )
    mixed, grad_streams = unpack(exchange(sent, SEQ))
    mixed_theirs = across(mixed)
    layer_out = jnp.dot(mixed, out_weight, preferred_element_type=F32).astype(BF)
    part = partial(core[None], mixed, mixed_theirs, grad, grad_theirs, lags)
    part = exchange(part.reshape(64, 16, 1152), CHIPS)
    shared = exchange(reduce(part, scale), DEPTH)
    lag_mine = shared[:, :, 1024:]
    rows = jnp.broadcast_to(shared[None, :, :, :1024], (8, 8, 16, 1024))
    mine = exchange(rows, SEQ)
    grad_weight, grad_filter = finish(core[None], mine, across(mine), lag_mine, across(lag_mine))
    return layer_out[None], grad_streams[:, None], grad_filter, grad_weight


def solution(mesh):
    fine = Mesh(mesh.devices.reshape(4, 2, 2, 4, 2), ("z", "yh", "c", "x", "yl"))
    dp = ("z", "yh", "c")
    placed = (P(None, dp, SEQ, None), P(), P(SEQ, None), P(), P(), P(dp, SEQ, None))
    return jax.shard_map(
        on_device,
        mesh=fine,
        in_specs=placed,
        out_specs=(P(dp, SEQ, None), P(None, dp, SEQ, None), P(SEQ, None), P()),
        check_vma=False,
    )
```

```python
import functools
import math

import jax
import jax.numpy as jnp
import numpy as np
from jax import lax
from jax.experimental import pallas as pl
from jax.experimental.pallas import tpu as pltpu
from jax.sharding import Mesh, PartitionSpec as P

BF = jnp.bfloat16
F32 = jnp.float32
BLOCK = 256
HALF = 64
SENT_ROWS = BLOCK + 64
SEQ = ("x", "yl")
DEPTH = ("z", "yh")
CHIPS = DEPTH + SEQ


@functools.lru_cache(maxsize=None)
def tables():
    order = np.concatenate([np.arange(0, BLOCK, 2), np.arange(1, BLOCK, 2)])
    angle = np.pi * ((2 * order[:, None] + 1) * np.arange(BLOCK)[None, :] % 1024) / 512.0
    ahead = np.concatenate([np.cos(angle), -np.sin(angle)], axis=0)
    back = ahead.T / BLOCK

    def two(table):
        table = table.astype(np.float32)
        high = table.astype(jnp.bfloat16)
        return high, (table - high.astype(np.float32)).astype(jnp.bfloat16)

    return two(ahead) + two(back)


def mm(a, b):
    return jnp.dot(a, b, preferred_element_type=F32)


def low_lanes(rows):
    return lax.broadcasted_iota(jnp.int32, (rows, 128), 1) < HALF


def turned(x):
    return pltpu.roll(x, HALF, 1)


def pack_kernel(streams, out_grad, weight, filt, packed, total):
    step = pl.program_id(0)
    low = low_lanes(BLOCK)

    @pl.when(step == 0)
    def _():
        total[...] = jnp.zeros_like(total)

    total[...] += lax.dot_general(
        out_grad[...], weight[...], (((1,), (1,)), ((), ())), preferred_element_type=F32
    )

    def put(q, tile, a, b):
        lanes = slice(128 * tile, 128 * tile + 128)
        packed[2 * q, 0:BLOCK, lanes] = jnp.where(low, a, turned(b)).astype(BF)
        packed[2 * q + 1, 0:BLOCK, lanes] = jnp.where(low, turned(a), b).astype(BF)

    for q in range(4):
        lanes = slice(128 * q, 128 * q + 128)

        @pl.when(step == q)
        def _(q=q, lanes=lanes):
            put(q, 0, streams[0, :, lanes].astype(F32), streams[1, :, lanes].astype(F32))
            low64 = low_lanes(64)
            for n in range(2):
                a = filt[128 * n : 128 * n + 64, lanes]
                b = filt[128 * n + 64 : 128 * n + 128, lanes]
                there = slice(128 * n, 128 * n + 128)
                packed[2 * q, BLOCK:, there] = jnp.where(low64, a, turned(b)).astype(BF)
                packed[2 * q + 1, BLOCK:, there] = jnp.where(low64, turned(a), b).astype(BF)

    @pl.when(step == pl.num_programs(0) - 1)
    def _():
        for q in range(4):
            lanes = slice(128 * q, 128 * q + 128)
            put(q, 1, streams[2, :, lanes].astype(F32), total[:, lanes])


def pack(streams, out_grad, weight, filt):
    steps = 4
    wide = out_grad.shape[1] // steps
    return pl.pallas_call(
        pack_kernel,
        grid=(steps,),
        in_specs=[
            pl.BlockSpec((3, BLOCK, 512), lambda k: (0, 0, 0)),
            pl.BlockSpec((BLOCK, wide), lambda k: (0, k)),
            pl.BlockSpec((512, wide), lambda k: (0, k)),
            pl.BlockSpec((BLOCK, 512), lambda k: (0, 0)),
        ],
        out_specs=pl.BlockSpec((8, SENT_ROWS, 256), lambda k: (0, 0, 0)),
        out_shape=jax.ShapeDtypeStruct((8, SENT_ROWS, 256), BF),
        scratch_shapes=[pltpu.VMEM((BLOCK, 512), F32)],
        name="pack",
    )(streams, out_grad, weight, filt)


def conv_kernel(
    place, got, short, skip, ahead_h, ahead_l, back_h, back_l,
    sent, lags,
    sa_pad, sv_pad, sa, sv, prod, spec, fspec, res, lres, time, u_pad, x_pad,
):
    low = low_lanes(BLOCK)
    low1 = low_lanes(1)
    sigma = jnp.where(low, 1.0, -1.0)
    odd = place[0] % 2 == 1

    taps = short[...]
    taps = jnp.where(odd, turned(taps), taps)
    taps_up = turned(taps)
    gain = skip[...]
    gain = jnp.where(odd, turned(gain), gain)
    gain = jnp.where(low1, gain, turned(gain))

    def tap(i, j):
        return taps[3 * i + j : 3 * i + j + 1]

    def tap_up(i, j):
        return taps_up[3 * i + j : 3 * i + j + 1]

    def unit(j):
        return jnp.full((1, 128), 1.0 if j == 0 else 0.0, F32)

    w_a = [jnp.where(low1, tap(0, j), tap_up(1, j)) for j in range(3)]
    w_v = [jnp.where(low1, tap(2, j), unit(j)) for j in range(3)]
    w_u = [jnp.where(low1, tap(1, j), tap_up(0, j)) for j in range(3)]
    w_x = [jnp.where(low1, unit(j), tap_up(2, j)) for j in range(3)]

    def split(x):
        high = x.astype(BF)
        return high, (x - high.astype(F32)).astype(BF)

    def apply(table_h, table_l, high, rest):
        return mm(table_h[...], high) + mm(table_h[...], rest) + mm(table_l[...], high)

    sa_pad[0:8] = jnp.zeros((8, 128), F32)
    sv_pad[0:8] = jnp.zeros((8, 128), F32)

    def load(b, carry):
        rows = pl.ds(pl.multiple_of(8 + BLOCK * b, 8), BLOCK)
        sa_pad[rows] = got[b, 0:BLOCK, 0:128].astype(F32)
        sv_pad[rows] = got[b, 0:BLOCK, 128:256].astype(F32)
        return carry

    lax.fori_loop(0, 8, load, 0)

    low64 = low_lanes(64)

    def filters(n, carry):
        def pair(b):
            parts = []
            for t in range(2):
                x = got[b, BLOCK:, 128 * t : 128 * t + 128].astype(F32)
                y = got[b + 1, BLOCK:, 128 * t : 128 * t + 128].astype(F32)
                parts.append(jnp.where(low64, x, turned(y)))
                parts.append(jnp.where(low64, turned(x), y))
            return jnp.concatenate(parts, axis=0).astype(BF)

        f = jnp.concatenate([pair(4 * n), pair(4 * n + 2)], axis=1)
        out = mm(ahead_h[...], f) + mm(ahead_l[...], f)
        low512 = low_lanes(512)
        for t in range(2):
            x = out[:, 128 * t : 128 * t + 128]
            y = turned(x)
            fspec[4 * n + 2 * t] = jnp.where(low512, x, y)
            fspec[4 * n + 2 * t + 1] = jnp.where(low512, y, x)
        return carry

    lax.fori_loop(0, 2, filters, 0)

    for b in range(8):
        start = 8 + BLOCK * b
        a = sum(w_a[j] * sa_pad[start - j : start - j + BLOCK] for j in range(3))
        v = sum(w_v[j] * sv_pad[start - j : start - j + BLOCK] for j in range(3))
        sa[b] = a
        sv[b] = v
        prod[b] = turned(a) * v

    def transform(n, carry):
        x = jnp.concatenate(
            [jnp.where(low, prod[b], prod[7 - b]) for b in (2 * n, 2 * n + 1)], axis=1
        )
        out = apply(ahead_h, ahead_l, *split(x))
        for t in range(2):
            spec[2 * n + t, 0:BLOCK] = out[:BLOCK, 128 * t : 128 * t + 128]
            spec[2 * n + t, BLOCK:] = out[BLOCK:, 128 * t : 128 * t + 128] * sigma
        return carry

    lax.fori_loop(0, 4, transform, 0)

    for sign, base in ((1.0, 0), (-1.0, 128)):

        def multiply(n, carry, sign=sign, base=base):
            re = pl.ds(pl.multiple_of(base + 8 * n, 8), 8)
            im = pl.ds(pl.multiple_of(BLOCK + base + 8 * n, 8), 8)
            own = [(spec[j, re], spec[j, im]) for j in range(8)]
            both = [own[0]]
            for j in range(1, 8):
                both.append(
                    (own[j][0] - sign * own[j - 1][1], own[j][1] + sign * own[j - 1][0])
                )
            filt = [(fspec[m, re], fspec[m, im]) for m in range(8)]

            def summed(pairs):
                first = True
                for (ar, ai), (br, bi) in pairs:
                    pr = ar * br - ai * bi
                    pi = ar * bi + ai * br
                    tr, ti = (pr, pi) if first else (tr + pr, ti + pi)
                    first = False
                return tr, ti

            for i in range(8):
                tr, ti = summed([(filt[m], both[i - m]) for m in range(i + 1)])
                res[i, re] = tr
                res[i, im] = ti
            zero = jnp.zeros((8, 128), F32)
            low8 = low_lanes(8)
            grads, shifted = [], []
            for i in range(8):
                grads.append(
                    tuple(jnp.where(low8, turned(own[7 - i][k]), own[7 - i][k]) for k in range(2))
                )
                before = both[i - 1] if i else (zero, zero)
                shifted.append(
                    tuple(jnp.where(low8, before[k], turned(both[i][k])) for k in range(2))
                )
            for a in range(4):
                tr, ti = summed([(grads[i], shifted[i - 2 * a]) for i in range(2 * a, 8)])
                lres[a, re] = tr
                lres[a, im] = ti
            return carry

        lax.fori_loop(0, 16, multiply, 0)

    def flipped(x, sign):
        return jnp.concatenate([x[0:BLOCK], x[BLOCK:] * sign], axis=0)

    def invert(n, carry):
        x = jnp.concatenate([flipped(res[b], sigma) for b in (2 * n, 2 * n + 1)], axis=1)
        out = apply(back_h, back_l, *split(x))
        time[2 * n] = out[:, :128]
        time[2 * n + 1] = out[:, 128:]
        return carry

    lax.fori_loop(0, 4, invert, 0)

    def invert_lags(n, carry):
        x = jnp.concatenate([flipped(lres[a], -1.0) for a in (2 * n, 2 * n + 1)], axis=1)
        out = apply(back_h, back_l, *split(x))
        low16 = low_lanes(16)
        for t in range(2):
            for k in range(8):
                x = out[32 * k : 32 * k + 16, 128 * t : 128 * t + 128]
                y = out[32 * k + 16 : 32 * k + 32, 128 * t : 128 * t + 128]
                m = 4 * n + 2 * t
                lags[m, k] = jnp.where(low16, turned(x), y).astype(BF)
                lags[m + 1, k] = jnp.where(low16, x, turned(y)).astype(BF)
        return carry

    lax.fori_loop(0, 2, invert_lags, 0)

    def gate(b, carry):
        t = jnp.where(low, time[b], time[7 - b]) + gain * prod[b]
        rows = pl.ds(pl.multiple_of(BLOCK * b, 8), BLOCK)
        u_pad[rows] = turned(t) * sv[b]
        x_pad[rows] = t * sa[b]
        return carry

    lax.fori_loop(0, 8, gate, 0)
    u_pad[8 * BLOCK :] = jnp.zeros((8, 128), F32)
    x_pad[8 * BLOCK :] = jnp.zeros((8, 128), F32)
    for b in range(8):
        start = BLOCK * b
        y = sum(w_u[j] * u_pad[start + j : start + j + BLOCK] for j in range(3))
        sent[b, :, 0:128] = y.astype(BF)
        y = sum(w_x[j] * x_pad[start + j : start + j + BLOCK] for j in range(3))
        sent[b, :, 128:256] = y.astype(BF)


def conv(place, got, short, skip):
    ahead_h, ahead_l, back_h, back_l = (jnp.asarray(t) for t in tables())
    full = lambda *shape: pl.BlockSpec(shape, lambda n, p: (0,) * len(shape))
    return pl.pallas_call(
        conv_kernel,
        grid_spec=pltpu.PrefetchScalarGridSpec(
            num_scalar_prefetch=1,
            grid=(1,),
            in_specs=[
                full(8, SENT_ROWS, 256),
                pl.BlockSpec((9, 128), lambda n, p: (0, p[0] // 2)),
                pl.BlockSpec((1, 128), lambda n, p: (0, p[0] // 2)),
                full(512, BLOCK),
                full(512, BLOCK),
                full(BLOCK, 512),
                full(BLOCK, 512),
            ],
            out_specs=[full(8, BLOCK, 256), full(8, 8, 16, 128)],
            scratch_shapes=[
                pltpu.VMEM((8 + 8 * BLOCK, 128), F32),
                pltpu.VMEM((8 + 8 * BLOCK, 128), F32),
                pltpu.VMEM((8, BLOCK, 128), F32),
                pltpu.VMEM((8, BLOCK, 128), F32),
                pltpu.VMEM((8, BLOCK, 128), F32),
                pltpu.VMEM((8, 512, 128), F32),
                pltpu.VMEM((8, 512, 128), F32),
                pltpu.VMEM((8, 512, 128), F32),
                pltpu.VMEM((4, 512, 128), F32),
                pltpu.VMEM((8, BLOCK, 128), F32),
                pltpu.VMEM((8 + 8 * BLOCK, 128), F32),
                pltpu.VMEM((8 + 8 * BLOCK, 128), F32),
            ],
        ),
        out_shape=[
            jax.ShapeDtypeStruct((8, BLOCK, 256), BF),
            jax.ShapeDtypeStruct((8, 8, 16, 128), BF),
        ],
        name="conv",
    )(place, got, short, skip, ahead_h, ahead_l, back_h, back_l)


def spread(got, there, first, second, low):
    for q in range(4):
        lanes = slice(128 * q, 128 * q + 128)
        a = got[2 * q, :, there].astype(F32)
        b = got[2 * q + 1, :, there].astype(F32)
        if first is not None:
            first[:, lanes] = jnp.where(low, a, turned(b)).astype(BF)
        if second is not None:
            second[:, lanes] = jnp.where(low, turned(a), b).astype(BF)


def mixed_kernel(got, mixed):
    spread(got, slice(0, 128), mixed, None, low_lanes(BLOCK))


def unpack_mixed(got):
    return pl.pallas_call(
        mixed_kernel,
        grid=(1,),
        in_specs=[pl.BlockSpec((8, BLOCK, 128), lambda n: (0, 0, 1))],
        out_specs=pl.BlockSpec((BLOCK, 512), lambda n: (0, 0)),
        out_shape=jax.ShapeDtypeStruct((BLOCK, 512), BF),
        name="unpack_mixed",
    )(got)


def grads_kernel(got, grads):
    low = low_lanes(BLOCK)
    spread(got, slice(0, 128), grads.at[1], grads.at[0], low)
    spread(got, slice(128, 256), None, grads.at[2], low)


def unpack_grads(got):
    return pl.pallas_call(
        grads_kernel,
        out_shape=jax.ShapeDtypeStruct((3, BLOCK, 512), BF),
        cost_estimate=pl.CostEstimate(flops=10**6, bytes_accessed=2 * 10**6, transcendentals=0),
        name="unpack_grads",
    )(got)


def partial_kernel(place, mine, theirs, grad_mine, grad_theirs, lags, packed):
    def term(mixed, grad):
        return lax.dot_general(
            mixed[...], grad[...], (((0,), (0,)), ((), ())), preferred_element_type=F32
        )

    part = (term(mine, grad_mine) + term(theirs, grad_theirs)).astype(BF)
    for s in range(8):
        for a in range(4):
            start = 64 * s + 16 * a
            packed[a, 0, s, :, 0:1024] = part[start : start + 16]
            packed[a, 0, s, :, 1024:1152] = lags[s, 2 * a + pl.program_id(0)]


def partial(place, mine, theirs, out_grad, grad_theirs, lags):
    return pl.pallas_call(
        partial_kernel,
        grid_spec=pltpu.PrefetchScalarGridSpec(
            num_scalar_prefetch=1,
            grid=(2,),
            in_specs=[
                pl.BlockSpec((BLOCK, 512), lambda h, p: (0, 0)),
                pl.BlockSpec((BLOCK, 512), lambda h, p: (0, 0)),
                pl.BlockSpec((BLOCK, 1024), lambda h, p: (0, 2 * p[0] + h)),
                pl.BlockSpec((BLOCK, 1024), lambda h, p: (0, h)),
                pl.BlockSpec((8, 8, 16, 128), lambda h, p: (0, 0, 0, 0)),
            ],
            out_specs=pl.BlockSpec((4, 1, 8, 16, 1152), lambda h, p: (0, h, 0, 0, 0)),
        ),
        out_shape=jax.ShapeDtypeStruct((4, 2, 8, 16, 1152), BF),
        name="partial",
    )(place, mine, theirs, out_grad, grad_theirs, lags)


def reduce_kernel(scale, got, shared):
    total = jnp.zeros((16, 1024), F32)
    for n in range(64):
        total = total + got[n, :, 0:1024].astype(F32)
    total = (total * scale).astype(BF)
    for k in range(8):
        shared[k, :, 0:1024] = total
    for s in range(8):
        lag = jnp.zeros((16, 128), F32)
        for k in range(8):
            lag = lag + got[8 * k + s, :, 1024:1152].astype(F32)
        lag = (lag * scale).astype(BF)
        for k in range(8):
            shared[k, :, 1024 + 128 * s : 1152 + 128 * s] = lag


def reduce(got, scale):
    return pl.pallas_call(
        functools.partial(reduce_kernel, scale),
        out_shape=jax.ShapeDtypeStruct((8, 16, 2048), BF),
        name="reduce",
    )(got)


def half_kernel(place, mine, *refs):
    grad_weight = refs[-1]
    for k in range(8):
        rows = slice(16 * (k // 2), 16 * (k // 2) + 16)
        lanes = slice(1024 * (k % 2), 1024 * (k % 2) + 1024)
        grad_weight[rows, lanes] = mine[0, k].astype(F32)


def write_half(half, rows, whole=None):
    more = [] if whole is None else [whole]
    return pl.pallas_call(
        half_kernel,
        grid_spec=pltpu.PrefetchScalarGridSpec(
            num_scalar_prefetch=1,
            grid=(8,),
            in_specs=[pl.BlockSpec((1, 8, 16, 1024), lambda s, p: (s, 0, 0, 0))]
            + [pl.BlockSpec(memory_space=pl.ANY)] * len(more),
            out_specs=pl.BlockSpec((64, 2048), lambda s, p: (s, p[0])),
        ),
        out_shape=jax.ShapeDtypeStruct((512, 4096), F32),
        input_output_aliases={2: 0} if more else {},
        cost_estimate=pl.CostEstimate(flops=10**6, bytes_accessed=6 * 10**6, transcendentals=0),
        name="write_half",
    )(half, rows, *more)


def filter_kernel(lag_mine, lag_theirs, grad_filter):
    low = low_lanes(16)
    for k in range(8):
        for q in range(4):
            def both(s):
                there = slice(128 * s, 128 * s + 128)
                return lag_mine[k, :, there].astype(F32) + lag_theirs[k, :, there].astype(F32)

            a, b = both(2 * q), both(2 * q + 1)
            lanes = slice(128 * q, 128 * q + 128)
            grad_filter[32 * k : 32 * k + 16, lanes] = jnp.where(low, a, turned(b))
            grad_filter[32 * k + 16 : 32 * k + 32, lanes] = jnp.where(low, turned(a), b)


def write_filter(lag_mine, lag_theirs):
    return pl.pallas_call(
        filter_kernel,
        out_shape=jax.ShapeDtypeStruct((BLOCK, 512), F32),
        cost_estimate=pl.CostEstimate(flops=10**6, bytes_accessed=2 * 10**6, transcendentals=0),
        name="write_filter",
    )(lag_mine, lag_theirs)


def exchange(x, axes):
    return lax.all_to_all(x, axes, 0, 0, tiled=True)


def across(x):
    return lax.ppermute(x, "c", [(0, 1), (1, 0)])


def on_device(streams, short_filter, long_filter, skip_gain, out_weight, out_grad):
    scale = 1.0 / math.sqrt(16 * 2048)
    core = lax.axis_index("c").astype(jnp.int32)
    seq = lax.axis_index(SEQ).astype(jnp.int32)
    grad = out_grad[0]
    grad_theirs = across(lax.dynamic_slice(grad, (0, (1 - core) * 2048), (BLOCK, 2048)))
    got = exchange(pack(streams[:, 0], grad, out_weight, long_filter), SEQ)
    sent, lags = conv(
        seq[None], got, short_filter.reshape(9, 512), skip_gain.reshape(1, 512)
    )
    back = exchange(sent, SEQ)
    mixed = unpack_mixed(back)
    mixed_theirs = across(mixed)
    part = partial(core[None], mixed, mixed_theirs, grad, grad_theirs, lags)
    part, mixed, back = lax.optimization_barrier((part, mixed, back))
    part = exchange(part.reshape(64, 16, 1152), CHIPS)
    layer_out = jnp.dot(mixed, out_weight, preferred_element_type=F32).astype(BF)
    grad_streams = unpack_grads(back)
    part, layer_out, grad_streams = lax.optimization_barrier((part, layer_out, grad_streams))
    shared = exchange(reduce(part, scale), DEPTH)
    lag_mine = shared[:, :, 1024:]
    lag_theirs = across(lag_mine)
    rows = jnp.broadcast_to(shared[None, :, :, :1024], (8, 8, 16, 1024))
    mine = exchange(rows, SEQ)
    grad_filter = write_filter(lag_mine, lag_theirs)
    theirs = across(mine)
    grad_weight = write_half(core[None], mine)
    grad_weight = write_half(1 - core[None], theirs, grad_weight)
    return layer_out[None], grad_streams[:, None], grad_filter, grad_weight


def solution(mesh):
    fine = Mesh(mesh.devices.reshape(4, 2, 2, 4, 2), ("z", "yh", "c", "x", "yl"))
    dp = ("z", "yh", "c")
    placed = (P(None, dp, SEQ, None), P(), P(SEQ, None), P(), P(), P(dp, SEQ, None))
    return jax.shard_map(
        on_device,
        mesh=fine,
        in_specs=placed,
        out_specs=(P(dp, SEQ, None), P(None, dp, SEQ, None), P(SEQ, None), P()),
        check_vma=False,
    )
```

```python
import functools
import math

import jax
import jax.numpy as jnp
import numpy as np
from jax import lax
from jax.experimental import pallas as pl
from jax.experimental.pallas import tpu as pltpu
from jax.sharding import Mesh, PartitionSpec as P

BF = jnp.bfloat16
F32 = jnp.float32
BLOCK = 256
HALF = 64
SENT_ROWS = BLOCK + 64
SEQ = ("x", "yl")
DEPTH = ("z", "yh")


@functools.lru_cache(maxsize=None)
def tables():
    order = np.concatenate([np.arange(0, BLOCK, 2), np.arange(1, BLOCK, 2)])
    angle = np.pi * ((2 * order[:, None] + 1) * np.arange(BLOCK)[None, :] % 1024) / 512.0
    ahead = np.concatenate([np.cos(angle), -np.sin(angle)], axis=0)
    back = ahead.T / BLOCK

    def two(table):
        table = table.astype(np.float32)
        high = table.astype(jnp.bfloat16)
        return high, (table - high.astype(np.float32)).astype(jnp.bfloat16)

    return two(ahead) + two(back)


def mm(a, b):
    return jnp.dot(a, b, preferred_element_type=F32)


def low_lanes(rows):
    return lax.broadcasted_iota(jnp.int32, (rows, 128), 1) < HALF


def turned(x):
    return pltpu.roll(x, HALF, 1)


def pack_kernel(streams, out_grad, weight, filt, packed, total):
    step = pl.program_id(0)
    low = low_lanes(BLOCK)

    @pl.when(step == 0)
    def _():
        total[...] = jnp.zeros_like(total)

    total[...] += lax.dot_general(
        out_grad[...], weight[...], (((1,), (1,)), ((), ())), preferred_element_type=F32
    )

    def put(q, tile, a, b):
        lanes = slice(128 * tile, 128 * tile + 128)
        packed[2 * q, 0:BLOCK, lanes] = jnp.where(low, a, turned(b)).astype(BF)
        packed[2 * q + 1, 0:BLOCK, lanes] = jnp.where(low, turned(a), b).astype(BF)

    for q in range(4):
        lanes = slice(128 * q, 128 * q + 128)

        @pl.when(step == q)
        def _(q=q, lanes=lanes):
            put(q, 0, streams[0, :, lanes].astype(F32), streams[1, :, lanes].astype(F32))
            low64 = low_lanes(64)
            for n in range(2):
                a = filt[128 * n : 128 * n + 64, lanes]
                b = filt[128 * n + 64 : 128 * n + 128, lanes]
                there = slice(128 * n, 128 * n + 128)
                packed[2 * q, BLOCK:, there] = jnp.where(low64, a, turned(b)).astype(BF)
                packed[2 * q + 1, BLOCK:, there] = jnp.where(low64, turned(a), b).astype(BF)

    @pl.when(step == pl.num_programs(0) - 1)
    def _():
        for q in range(4):
            lanes = slice(128 * q, 128 * q + 128)
            put(q, 1, streams[2, :, lanes].astype(F32), total[:, lanes])


def pack(streams, out_grad, weight, filt):
    steps = 4
    wide = out_grad.shape[1] // steps
    return pl.pallas_call(
        pack_kernel,
        grid=(steps,),
        in_specs=[
            pl.BlockSpec((3, BLOCK, 512), lambda k: (0, 0, 0)),
            pl.BlockSpec((BLOCK, wide), lambda k: (0, k)),
            pl.BlockSpec((512, wide), lambda k: (0, k)),
            pl.BlockSpec((BLOCK, 512), lambda k: (0, 0)),
        ],
        out_specs=pl.BlockSpec((8, SENT_ROWS, 256), lambda k: (0, 0, 0)),
        out_shape=jax.ShapeDtypeStruct((8, SENT_ROWS, 256), BF),
        scratch_shapes=[pltpu.VMEM((BLOCK, 512), F32)],
        name="pack",
    )(streams, out_grad, weight, filt)


def conv_kernel(
    place, got, short, skip, ahead_h, ahead_l, back_h, back_l,
    sent, lags,
    sa_pad, sv_pad, sa, sv, prod, spec, fspec, res, lres, time, u_pad, x_pad,
):
    low = low_lanes(BLOCK)
    low1 = low_lanes(1)
    sigma = jnp.where(low, 1.0, -1.0)
    odd = place[0] % 2 == 1

    taps = short[...]
    taps = jnp.where(odd, turned(taps), taps)
    taps_up = turned(taps)
    gain = skip[...]
    gain = jnp.where(odd, turned(gain), gain)
    gain = jnp.where(low1, gain, turned(gain))

    def tap(i, j):
        return taps[3 * i + j : 3 * i + j + 1]

    def tap_up(i, j):
        return taps_up[3 * i + j : 3 * i + j + 1]

    def unit(j):
        return jnp.full((1, 128), 1.0 if j == 0 else 0.0, F32)

    w_a = [jnp.where(low1, tap(0, j), tap_up(1, j)) for j in range(3)]
    w_v = [jnp.where(low1, tap(2, j), unit(j)) for j in range(3)]
    w_u = [jnp.where(low1, tap(1, j), tap_up(0, j)) for j in range(3)]
    w_x = [jnp.where(low1, unit(j), tap_up(2, j)) for j in range(3)]

    def split(x):
        high = x.astype(BF)
        return high, (x - high.astype(F32)).astype(BF)

    def apply(table_h, table_l, high, rest):
        return mm(table_h[...], high) + mm(table_h[...], rest) + mm(table_l[...], high)

    sa_pad[0:8] = jnp.zeros((8, 128), F32)
    sv_pad[0:8] = jnp.zeros((8, 128), F32)

    def load(b, carry):
        rows = pl.ds(pl.multiple_of(8 + BLOCK * b, 8), BLOCK)
        sa_pad[rows] = got[b, 0:BLOCK, 0:128].astype(F32)
        sv_pad[rows] = got[b, 0:BLOCK, 128:256].astype(F32)
        return carry

    lax.fori_loop(0, 8, load, 0)

    low64 = low_lanes(64)

    def filters(n, carry):
        def pair(b):
            parts = []
            for t in range(2):
                x = got[b, BLOCK:, 128 * t : 128 * t + 128].astype(F32)
                y = got[b + 1, BLOCK:, 128 * t : 128 * t + 128].astype(F32)
                parts.append(jnp.where(low64, x, turned(y)))
                parts.append(jnp.where(low64, turned(x), y))
            return jnp.concatenate(parts, axis=0).astype(BF)

        f = jnp.concatenate([pair(4 * n), pair(4 * n + 2)], axis=1)
        out = mm(ahead_h[...], f) + mm(ahead_l[...], f)
        low512 = low_lanes(512)
        for t in range(2):
            x = out[:, 128 * t : 128 * t + 128]
            y = turned(x)
            fspec[4 * n + 2 * t] = jnp.where(low512, x, y)
            fspec[4 * n + 2 * t + 1] = jnp.where(low512, y, x)
        return carry

    lax.fori_loop(0, 2, filters, 0)

    for b in range(8):
        start = 8 + BLOCK * b
        a = sum(w_a[j] * sa_pad[start - j : start - j + BLOCK] for j in range(3))
        v = sum(w_v[j] * sv_pad[start - j : start - j + BLOCK] for j in range(3))
        sa[b] = a
        sv[b] = v
        prod[b] = turned(a) * v

    def transform(n, carry):
        x = jnp.concatenate(
            [jnp.where(low, prod[b], prod[7 - b]) for b in (2 * n, 2 * n + 1)], axis=1
        )
        out = apply(ahead_h, ahead_l, *split(x))
        for t in range(2):
            spec[2 * n + t, 0:BLOCK] = out[:BLOCK, 128 * t : 128 * t + 128]
            spec[2 * n + t, BLOCK:] = out[BLOCK:, 128 * t : 128 * t + 128] * sigma
        return carry

    lax.fori_loop(0, 4, transform, 0)

    for sign, base in ((1.0, 0), (-1.0, 128)):

        def multiply(n, carry, sign=sign, base=base):
            re = pl.ds(pl.multiple_of(base + 8 * n, 8), 8)
            im = pl.ds(pl.multiple_of(BLOCK + base + 8 * n, 8), 8)
            own = [(spec[j, re], spec[j, im]) for j in range(8)]
            both = [own[0]]
            for j in range(1, 8):
                both.append(
                    (own[j][0] - sign * own[j - 1][1], own[j][1] + sign * own[j - 1][0])
                )
            filt = [(fspec[m, re], fspec[m, im]) for m in range(8)]

            def summed(pairs):
                first = True
                for (ar, ai), (br, bi) in pairs:
                    pr = ar * br - ai * bi
                    pi = ar * bi + ai * br
                    tr, ti = (pr, pi) if first else (tr + pr, ti + pi)
                    first = False
                return tr, ti

            for i in range(8):
                tr, ti = summed([(filt[m], both[i - m]) for m in range(i + 1)])
                res[i, re] = tr
                res[i, im] = ti
            zero = jnp.zeros((8, 128), F32)
            low8 = low_lanes(8)
            grads, shifted = [], []
            for i in range(8):
                grads.append(
                    tuple(jnp.where(low8, turned(own[7 - i][k]), own[7 - i][k]) for k in range(2))
                )
                before = both[i - 1] if i else (zero, zero)
                shifted.append(
                    tuple(jnp.where(low8, before[k], turned(both[i][k])) for k in range(2))
                )
            for a in range(4):
                tr, ti = summed([(grads[i], shifted[i - 2 * a]) for i in range(2 * a, 8)])
                lres[a, re] = tr
                lres[a, im] = ti
            return carry

        lax.fori_loop(0, 16, multiply, 0)

    def flipped(x, sign):
        return jnp.concatenate([x[0:BLOCK], x[BLOCK:] * sign], axis=0)

    def invert(n, carry):
        x = jnp.concatenate([flipped(res[b], sigma) for b in (2 * n, 2 * n + 1)], axis=1)
        out = apply(back_h, back_l, *split(x))
        time[2 * n] = out[:, :128]
        time[2 * n + 1] = out[:, 128:]
        return carry

    lax.fori_loop(0, 4, invert, 0)

    def invert_lags(n, carry):
        x = jnp.concatenate([flipped(lres[a], -1.0) for a in (2 * n, 2 * n + 1)], axis=1)
        out = apply(back_h, back_l, *split(x))
        low16 = low_lanes(16)
        for t in range(2):
            for k in range(8):
                x = out[32 * k : 32 * k + 16, 128 * t : 128 * t + 128]
                y = out[32 * k + 16 : 32 * k + 32, 128 * t : 128 * t + 128]
                m = 4 * n + 2 * t
                lags[m, k] = jnp.where(low16, turned(x), y).astype(BF)
                lags[m + 1, k] = jnp.where(low16, x, turned(y)).astype(BF)
        return carry

    lax.fori_loop(0, 2, invert_lags, 0)

    def gate(b, carry):
        t = jnp.where(low, time[b], time[7 - b]) + gain * prod[b]
        rows = pl.ds(pl.multiple_of(BLOCK * b, 8), BLOCK)
        u_pad[rows] = turned(t) * sv[b]
        x_pad[rows] = t * sa[b]
        return carry

    lax.fori_loop(0, 8, gate, 0)
    u_pad[8 * BLOCK :] = jnp.zeros((8, 128), F32)
    x_pad[8 * BLOCK :] = jnp.zeros((8, 128), F32)
    for b in range(8):
        start = BLOCK * b
        y = sum(w_u[j] * u_pad[start + j : start + j + BLOCK] for j in range(3))
        sent[b, 0:BLOCK, 0:128] = y.astype(BF)
        y = sum(w_x[j] * x_pad[start + j : start + j + BLOCK] for j in range(3))
        sent[b, 0:BLOCK, 128:256] = y.astype(BF)
        for t in range(2):
            first, second = y[128 * t : 128 * t + 64], y[128 * t + 64 : 128 * t + 128]
            there = slice(128 * t, 128 * t + 128)
            sent[b ^ 1, BLOCK:, there] = jnp.where(low64, first, turned(second)).astype(BF)


def conv(place, got, short, skip):
    ahead_h, ahead_l, back_h, back_l = (jnp.asarray(t) for t in tables())
    full = lambda *shape: pl.BlockSpec(shape, lambda n, p: (0,) * len(shape))
    return pl.pallas_call(
        conv_kernel,
        grid_spec=pltpu.PrefetchScalarGridSpec(
            num_scalar_prefetch=1,
            grid=(1,),
            in_specs=[
                full(8, SENT_ROWS, 256),
                pl.BlockSpec((9, 128), lambda n, p: (0, p[0] // 2)),
                pl.BlockSpec((1, 128), lambda n, p: (0, p[0] // 2)),
                full(512, BLOCK),
                full(512, BLOCK),
                full(BLOCK, 512),
                full(BLOCK, 512),
            ],
            out_specs=[full(8, SENT_ROWS, 256), full(8, 8, 16, 128)],
            scratch_shapes=[
                pltpu.VMEM((8 + 8 * BLOCK, 128), F32),
                pltpu.VMEM((8 + 8 * BLOCK, 128), F32),
                pltpu.VMEM((8, BLOCK, 128), F32),
                pltpu.VMEM((8, BLOCK, 128), F32),
                pltpu.VMEM((8, BLOCK, 128), F32),
                pltpu.VMEM((8, 512, 128), F32),
                pltpu.VMEM((8, 512, 128), F32),
                pltpu.VMEM((8, 512, 128), F32),
                pltpu.VMEM((4, 512, 128), F32),
                pltpu.VMEM((8, BLOCK, 128), F32),
                pltpu.VMEM((8 + 8 * BLOCK, 128), F32),
                pltpu.VMEM((8 + 8 * BLOCK, 128), F32),
            ],
        ),
        out_shape=[
            jax.ShapeDtypeStruct((8, SENT_ROWS, 256), BF),
            jax.ShapeDtypeStruct((8, 8, 16, 128), BF),
        ],
        name="conv",
    )(place, got, short, skip, ahead_h, ahead_l, back_h, back_l)


def spread(got, there, first, second, low):
    for q in range(4):
        lanes = slice(128 * q, 128 * q + 128)
        a = got[2 * q, 0:BLOCK, there].astype(F32)
        b = got[2 * q + 1, 0:BLOCK, there].astype(F32)
        if first is not None:
            first[:, lanes] = jnp.where(low, a, turned(b)).astype(BF)
        if second is not None:
            second[:, lanes] = jnp.where(low, turned(a), b).astype(BF)


def mixed_kernel(got, mixed):
    spread(got, slice(128, 256), mixed.at[0], None, low_lanes(BLOCK))
    low = low_lanes(64)
    for q in range(4):
        lanes = slice(128 * q, 128 * q + 128)
        for t in range(2):
            there = slice(128 * t, 128 * t + 128)
            a = got[2 * q, BLOCK:, there].astype(F32)
            b = got[2 * q + 1, BLOCK:, there].astype(F32)
            mixed[1, 128 * t : 128 * t + 64, lanes] = jnp.where(low, a, turned(b)).astype(BF)
            mixed[1, 128 * t + 64 : 128 * t + 128, lanes] = jnp.where(low, turned(a), b).astype(BF)


def unpack_mixed(got):
    return pl.pallas_call(
        mixed_kernel,
        out_shape=jax.ShapeDtypeStruct((2, BLOCK, 512), BF),
        name="unpack_mixed",
    )(got)


def grads_kernel(got, grads):
    low = low_lanes(BLOCK)
    spread(got, slice(0, 128), grads.at[1], grads.at[0], low)
    spread(got, slice(128, 256), None, grads.at[2], low)


def unpack_grads(got):
    return pl.pallas_call(
        grads_kernel,
        out_shape=jax.ShapeDtypeStruct((3, BLOCK, 512), BF),
        cost_estimate=pl.CostEstimate(flops=10**6, bytes_accessed=2 * 10**6, transcendentals=0),
        name="unpack_grads",
    )(got)


def partial_kernel(place, mine, theirs, g00, g01, g10, g11, lags, packed):
    def term(mixed, grad):
        return lax.dot_general(
            mixed, grad[...], (((0,), (0,)), ((), ())), preferred_element_type=F32
        )

    part = term(mine[0], g00) + term(mine[1], g01) + term(theirs[0], g10) + term(theirs[1], g11)
    part = part.astype(BF)
    for x in range(4):
        for k in range(8):
            start = 128 * x + 16 * k
            packed[4 * k + x, :, 0:1024] = part[start : start + 16]
            packed[4 * k + x, :, 1024:1152] = lags[2 * x, k]
            packed[4 * k + x, :, 1152:1280] = lags[2 * x + 1, k]


def partial(place, mine, theirs, grad, grads, lags):
    full = lambda *shape: pl.BlockSpec(shape, lambda n, p: (0,) * len(shape))
    return pl.pallas_call(
        partial_kernel,
        grid_spec=pltpu.PrefetchScalarGridSpec(
            num_scalar_prefetch=1,
            grid=(1,),
            in_specs=[
                full(2, BLOCK, 512),
                full(2, BLOCK, 512),
                pl.BlockSpec((BLOCK, 1024), lambda n, p: (0, p[0])),
                full(BLOCK, 1024),
                full(BLOCK, 1024),
                full(BLOCK, 1024),
                full(8, 8, 16, 128),
            ],
            out_specs=full(32, 16, 1280),
        ),
        out_shape=jax.ShapeDtypeStruct((32, 16, 1280), BF),
        name="partial",
    )(place, mine, theirs, grad, *grads, lags)


def reduce_kernel(scale, got, shared):
    total = jnp.zeros((16, 1024), F32)
    for n in range(32):
        total = total + got[n, :, 0:1024].astype(F32)
    total = (total * scale).astype(BF)
    for k in range(8):
        shared[k, :, 0:1024] = total
    for x in range(4):
        lag = jnp.zeros((16, 256), F32)
        for k in range(8):
            lag = lag + got[4 * k + x, :, 1024:1280].astype(F32)
        lag = (lag * scale).astype(BF)
        for k in range(8):
            for m in range(2):
                there = slice(1024 + 512 * m + 128 * x, 1152 + 512 * m + 128 * x)
                shared[k, :, there] = lag[:, 128 * m : 128 * m + 128]


def reduce(got, scale):
    return pl.pallas_call(
        functools.partial(reduce_kernel, scale),
        out_shape=jax.ShapeDtypeStruct((8, 16, 2048), BF),
        name="reduce",
    )(got)


def half_kernel(place, mine, *refs):
    grad_weight, wide, sems = refs[-3:]
    s = pl.program_id(0)

    def copy(n):
        rows = pl.ds(pl.multiple_of(128 * (n // 2), 128), 128)
        lanes = pl.ds(pl.multiple_of(2048 * place[0] + 1024 * (n % 2), 1024), 1024)
        return pltpu.make_async_copy(wide.at[n], grad_weight.at[rows, lanes], sems.at[n])

    for k in range(8):
        wide[s, 16 * k : 16 * k + 16] = mine[0, k].astype(F32)
    copy(s).start()

    @pl.when(s == 7)
    def _():
        for n in range(8):
            copy(n).wait()


def write_half(half, rows, whole=None):
    more = [] if whole is None else [whole]
    return pl.pallas_call(
        half_kernel,
        grid_spec=pltpu.PrefetchScalarGridSpec(
            num_scalar_prefetch=1,
            grid=(8,),
            in_specs=[pl.BlockSpec((1, 8, 16, 1024), lambda s, p: (s, 0, 0, 0))]
            + [pl.BlockSpec(memory_space=pltpu.HBM)] * len(more),
            out_specs=pl.BlockSpec(memory_space=pltpu.HBM),
            scratch_shapes=[
                pltpu.VMEM((8, 128, 1024), F32),
                pltpu.SemaphoreType.DMA((8,)),
            ],
        ),
        out_shape=jax.ShapeDtypeStruct((512, 4096), F32),
        input_output_aliases={2: 0} if more else {},
        cost_estimate=pl.CostEstimate(flops=10**6, bytes_accessed=6 * 10**6, transcendentals=0),
        name="write_half",
    )(half, rows, *more)


def filter_kernel(place, own, own_c, other, other_c, grad_filter):
    low = low_lanes(16)
    first = place[0] == 0
    for k in range(8):
        for q in range(4):
            there = slice(128 * q, 128 * q + 128)
            a = own[k, :, there].astype(F32) + own_c[k, :, there].astype(F32)
            b = other[k, :, there].astype(F32) + other_c[k, :, there].astype(F32)
            a, b = jnp.where(first, a, b), jnp.where(first, b, a)
            grad_filter[32 * k : 32 * k + 16, there] = jnp.where(low, a, turned(b))
            grad_filter[32 * k + 16 : 32 * k + 32, there] = jnp.where(low, turned(a), b)


def write_filter(side, own, own_c, other, other_c):
    full = lambda *shape: pl.BlockSpec(shape, lambda n, p: (0,) * len(shape))
    return pl.pallas_call(
        filter_kernel,
        grid_spec=pltpu.PrefetchScalarGridSpec(
            num_scalar_prefetch=1,
            grid=(1,),
            in_specs=[full(8, 16, 512)] * 4,
            out_specs=full(BLOCK, 512),
        ),
        out_shape=jax.ShapeDtypeStruct((BLOCK, 512), F32),
        cost_estimate=pl.CostEstimate(flops=10**6, bytes_accessed=2 * 10**6, transcendentals=0),
        name="write_filter",
    )(side, own, own_c, other, other_c)


def exchange(x, axes):
    return lax.all_to_all(x, axes, 0, 0, tiled=True)


def across(x):
    return lax.ppermute(x, "c", [(0, 1), (1, 0)])


def beside(x):
    return lax.ppermute(x, "yl", [(0, 1), (1, 0)])


def opposite(x):
    return lax.ppermute(x, ("c", "yl"), [(n, 3 - n) for n in range(4)])


def on_device(streams, short_filter, long_filter, skip_gain, out_weight, out_grad):
    scale = 1.0 / math.sqrt(16 * 2048)
    core = lax.axis_index("c").astype(jnp.int32)
    side = lax.axis_index("yl").astype(jnp.int32)
    seq = lax.axis_index(SEQ).astype(jnp.int32)
    grad = out_grad[0]

    def quarter(c, y):
        return lax.dynamic_slice(grad, (0, 1024 * (2 * c + y)), (BLOCK, 1024))

    grads = (
        beside(quarter(core, 1 - side)),
        across(quarter(1 - core, side)),
        opposite(quarter(1 - core, 1 - side)),
    )
    got = exchange(pack(streams[:, 0], grad, out_weight, long_filter), SEQ)
    sent, lags = conv(
        seq[None], got, short_filter.reshape(9, 512), skip_gain.reshape(1, 512)
    )
    back = exchange(sent, SEQ)
    mixed = unpack_mixed(back)
    mixed_theirs = across(mixed)
    part = partial((2 * core + side)[None], mixed, mixed_theirs, grad, grads, lags)
    part, mixed, back = lax.optimization_barrier((part, mixed, back))
    part = exchange(part, DEPTH + ("x",))
    layer_out = jnp.dot(mixed[0], out_weight, preferred_element_type=F32).astype(BF)
    grad_streams = unpack_grads(back)
    part, layer_out, grad_streams = lax.optimization_barrier((part, layer_out, grad_streams))
    shared = exchange(reduce(part, scale), DEPTH)
    rows = jnp.broadcast_to(shared[None, :, :, :1024], (8, 8, 16, 1024))
    rows, shared = lax.optimization_barrier((rows, shared))
    mine = exchange(rows, SEQ)
    own = lax.dynamic_slice(shared, (0, 0, 1024 + 512 * side), (8, 16, 512))
    other = beside(lax.dynamic_slice(shared, (0, 0, 1536 - 512 * side), (8, 16, 512)))
    grad_filter = write_filter(side[None], own, across(own), other, across(other))
    mine, grad_filter = lax.optimization_barrier((mine, grad_filter))
    theirs = across(mine)
    grad_weight = write_half(core[None], mine)
    grad_weight = write_half(1 - core[None], theirs, grad_weight)
    return layer_out[None], grad_streams[:, None], grad_filter, grad_weight


def solution(mesh):
    fine = Mesh(mesh.devices.reshape(4, 2, 2, 4, 2), ("z", "yh", "c", "x", "yl"))
    dp = ("z", "yh", "c")
    placed = (P(None, dp, SEQ, None), P(), P(SEQ, None), P(), P(), P(dp, SEQ, None))
    return jax.shard_map(
        on_device,
        mesh=fine,
        in_specs=placed,
        out_specs=(P(dp, SEQ, None), P(None, dp, SEQ, None), P(SEQ, None), P()),
        check_vma=False,
    )
```

```python
import functools
import math

import jax
import jax.numpy as jnp
import numpy as np
from jax import lax
from jax.experimental import pallas as pl
from jax.experimental.pallas import tpu as pltpu
from jax.sharding import Mesh, PartitionSpec as P

BF = jnp.bfloat16
F32 = jnp.float32
BLOCK = 256
HALF = 64
SENT_ROWS = BLOCK + 64
SEQ = ("x", "yl")
DEPTH = ("z", "yh")


@functools.lru_cache(maxsize=None)
def tables():
    order = np.concatenate([np.arange(0, BLOCK, 2), np.arange(1, BLOCK, 2)])
    angle = np.pi * ((2 * order[:, None] + 1) * np.arange(BLOCK)[None, :] % 1024) / 512.0
    ahead = np.concatenate([np.cos(angle), -np.sin(angle)], axis=0)
    back = ahead.T / BLOCK

    def two(table):
        table = table.astype(np.float32)
        high = table.astype(jnp.bfloat16)
        return high, (table - high.astype(np.float32)).astype(jnp.bfloat16)

    return two(ahead) + two(back)


def mm(a, b):
    return jnp.dot(a, b, preferred_element_type=F32)


def low_lanes(rows):
    return lax.broadcasted_iota(jnp.int32, (rows, 128), 1) < HALF


def turned(x):
    return pltpu.roll(x, HALF, 1)


def pack_kernel(streams, out_grad, weight, filt, packed, total):
    step = pl.program_id(0)
    low = low_lanes(BLOCK)

    @pl.when(step == 0)
    def _():
        total[...] = jnp.zeros_like(total)

    total[...] += lax.dot_general(
        out_grad[...], weight[...], (((1,), (1,)), ((), ())), preferred_element_type=F32
    )

    def put(q, tile, a, b):
        lanes = slice(128 * tile, 128 * tile + 128)
        packed[2 * q, 0:BLOCK, lanes] = jnp.where(low, a, turned(b)).astype(BF)
        packed[2 * q + 1, 0:BLOCK, lanes] = jnp.where(low, turned(a), b).astype(BF)

    for q in range(4):
        lanes = slice(128 * q, 128 * q + 128)

        @pl.when(step == q)
        def _(q=q, lanes=lanes):
            put(q, 0, streams[0, :, lanes].astype(F32), streams[1, :, lanes].astype(F32))
            low64 = low_lanes(64)
            for n in range(2):
                a = filt[128 * n : 128 * n + 64, lanes]
                b = filt[128 * n + 64 : 128 * n + 128, lanes]
                there = slice(128 * n, 128 * n + 128)
                packed[2 * q, BLOCK:, there] = jnp.where(low64, a, turned(b)).astype(BF)
                packed[2 * q + 1, BLOCK:, there] = jnp.where(low64, turned(a), b).astype(BF)

    @pl.when(step == pl.num_programs(0) - 1)
    def _():
        for q in range(4):
            lanes = slice(128 * q, 128 * q + 128)
            put(q, 1, streams[2, :, lanes].astype(F32), total[:, lanes])


def pack(streams, out_grad, weight, filt):
    steps = 4
    wide = out_grad.shape[1] // steps
    return pl.pallas_call(
        pack_kernel,
        grid=(steps,),
        in_specs=[
            pl.BlockSpec((3, BLOCK, 512), lambda k: (0, 0, 0)),
            pl.BlockSpec((BLOCK, wide), lambda k: (0, k)),
            pl.BlockSpec((512, wide), lambda k: (0, k)),
            pl.BlockSpec((BLOCK, 512), lambda k: (0, 0)),
        ],
        out_specs=pl.BlockSpec((8, SENT_ROWS, 256), lambda k: (0, 0, 0)),
        out_shape=jax.ShapeDtypeStruct((8, SENT_ROWS, 256), BF),
        scratch_shapes=[pltpu.VMEM((BLOCK, 512), F32)],
        name="pack",
    )(streams, out_grad, weight, filt)


def conv_kernel(
    place, got, short, skip, ahead_h, ahead_l, back_h, back_l,
    sent, lags,
    sa_pad, sv_pad, sa, sv, prod, spec, fspec, res, lres, time, u_pad, x_pad,
):
    low = low_lanes(BLOCK)
    low1 = low_lanes(1)
    sigma = jnp.where(low, 1.0, -1.0)
    odd = place[0] % 2 == 1

    taps = short[...]
    taps = jnp.where(odd, turned(taps), taps)
    taps_up = turned(taps)
    gain = skip[...]
    gain = jnp.where(odd, turned(gain), gain)
    gain = jnp.where(low1, gain, turned(gain))

    def tap(i, j):
        return taps[3 * i + j : 3 * i + j + 1]

    def tap_up(i, j):
        return taps_up[3 * i + j : 3 * i + j + 1]

    def unit(j):
        return jnp.full((1, 128), 1.0 if j == 0 else 0.0, F32)

    w_a = [jnp.where(low1, tap(0, j), tap_up(1, j)) for j in range(3)]
    w_v = [jnp.where(low1, tap(2, j), unit(j)) for j in range(3)]
    w_u = [jnp.where(low1, tap(1, j), tap_up(0, j)) for j in range(3)]
    w_x = [jnp.where(low1, unit(j), tap_up(2, j)) for j in range(3)]

    def split(x):
        high = x.astype(BF)
        return high, (x - high.astype(F32)).astype(BF)

    def apply(table_h, table_l, high, rest):
        return mm(table_h[...], high) + mm(table_h[...], rest) + mm(table_l[...], high)

    sa_pad[0:8] = jnp.zeros((8, 128), F32)
    sv_pad[0:8] = jnp.zeros((8, 128), F32)

    def load(b, carry):
        rows = pl.ds(pl.multiple_of(8 + BLOCK * b, 8), BLOCK)
        sa_pad[rows] = got[b, 0:BLOCK, 0:128].astype(F32)
        sv_pad[rows] = got[b, 0:BLOCK, 128:256].astype(F32)
        return carry

    lax.fori_loop(0, 8, load, 0)

    low64 = low_lanes(64)

    def filters(n, carry):
        def pair(b):
            parts = []
            for t in range(2):
                x = got[b, BLOCK:, 128 * t : 128 * t + 128].astype(F32)
                y = got[b + 1, BLOCK:, 128 * t : 128 * t + 128].astype(F32)
                parts.append(jnp.where(low64, x, turned(y)))
                parts.append(jnp.where(low64, turned(x), y))
            return jnp.concatenate(parts, axis=0).astype(BF)

        f = jnp.concatenate([pair(4 * n), pair(4 * n + 2)], axis=1)
        out = mm(ahead_h[...], f) + mm(ahead_l[...], f)
        low512 = low_lanes(512)
        for t in range(2):
            x = out[:, 128 * t : 128 * t + 128]
            y = turned(x)
            fspec[4 * n + 2 * t] = jnp.where(low512, x, y)
            fspec[4 * n + 2 * t + 1] = jnp.where(low512, y, x)
        return carry

    lax.fori_loop(0, 2, filters, 0)

    for b in range(8):
        start = 8 + BLOCK * b
        a = sum(w_a[j] * sa_pad[start - j : start - j + BLOCK] for j in range(3))
        v = sum(w_v[j] * sv_pad[start - j : start - j + BLOCK] for j in range(3))
        sa[b] = a
        sv[b] = v
        prod[b] = turned(a) * v

    def transform(n, carry):
        x = jnp.concatenate(
            [jnp.where(low, prod[b], prod[7 - b]) for b in (2 * n, 2 * n + 1)], axis=1
        )
        out = apply(ahead_h, ahead_l, *split(x))
        for t in range(2):
            spec[2 * n + t, 0:BLOCK] = out[:BLOCK, 128 * t : 128 * t + 128]
            spec[2 * n + t, BLOCK:] = out[BLOCK:, 128 * t : 128 * t + 128] * sigma
        return carry

    lax.fori_loop(0, 4, transform, 0)

    for sign, base in ((1.0, 0), (-1.0, 128)):

        def multiply(n, carry, sign=sign, base=base):
            re = pl.ds(pl.multiple_of(base + 8 * n, 8), 8)
            im = pl.ds(pl.multiple_of(BLOCK + base + 8 * n, 8), 8)
            own = [(spec[j, re], spec[j, im]) for j in range(8)]
            both = [own[0]]
            for j in range(1, 8):
                both.append(
                    (own[j][0] - sign * own[j - 1][1], own[j][1] + sign * own[j - 1][0])
                )
            filt = [(fspec[m, re], fspec[m, im]) for m in range(8)]

            def summed(pairs):
                first = True
                for (ar, ai), (br, bi) in pairs:
                    pr = ar * br - ai * bi
                    pi = ar * bi + ai * br
                    tr, ti = (pr, pi) if first else (tr + pr, ti + pi)
                    first = False
                return tr, ti

            for i in range(8):
                tr, ti = summed([(filt[m], both[i - m]) for m in range(i + 1)])
                res[i, re] = tr
                res[i, im] = ti
            zero = jnp.zeros((8, 128), F32)
            low8 = low_lanes(8)
            grads, shifted = [], []
            for i in range(8):
                grads.append(
                    tuple(jnp.where(low8, turned(own[7 - i][k]), own[7 - i][k]) for k in range(2))
                )
                before = both[i - 1] if i else (zero, zero)
                shifted.append(
                    tuple(jnp.where(low8, before[k], turned(both[i][k])) for k in range(2))
                )
            for a in range(4):
                tr, ti = summed([(grads[i], shifted[i - 2 * a]) for i in range(2 * a, 8)])
                lres[a, re] = tr
                lres[a, im] = ti
            return carry

        lax.fori_loop(0, 16, multiply, 0)

    def flipped(x, sign):
        return jnp.concatenate([x[0:BLOCK], x[BLOCK:] * sign], axis=0)

    def invert(n, carry):
        x = jnp.concatenate([flipped(res[b], sigma) for b in (2 * n, 2 * n + 1)], axis=1)
        out = apply(back_h, back_l, *split(x))
        time[2 * n] = out[:, :128]
        time[2 * n + 1] = out[:, 128:]
        return carry

    lax.fori_loop(0, 4, invert, 0)

    def invert_lags(n, carry):
        x = jnp.concatenate([flipped(lres[a], -1.0) for a in (2 * n, 2 * n + 1)], axis=1)
        out = apply(back_h, back_l, *split(x))
        low16 = low_lanes(16)
        for t in range(2):
            for k in range(8):
                x = out[32 * k : 32 * k + 16, 128 * t : 128 * t + 128]
                y = out[32 * k + 16 : 32 * k + 32, 128 * t : 128 * t + 128]
                m = 4 * n + 2 * t
                lags[m, k] = jnp.where(low16, turned(x), y).astype(BF)
                lags[m + 1, k] = jnp.where(low16, x, turned(y)).astype(BF)
        return carry

    lax.fori_loop(0, 2, invert_lags, 0)

    def gate(b, carry):
        t = jnp.where(low, time[b], time[7 - b]) + gain * prod[b]
        rows = pl.ds(pl.multiple_of(BLOCK * b, 8), BLOCK)
        u_pad[rows] = turned(t) * sv[b]
        x_pad[rows] = t * sa[b]
        return carry

    lax.fori_loop(0, 8, gate, 0)
    u_pad[8 * BLOCK :] = jnp.zeros((8, 128), F32)
    x_pad[8 * BLOCK :] = jnp.zeros((8, 128), F32)
    for b in range(8):
        start = BLOCK * b
        y = sum(w_u[j] * u_pad[start + j : start + j + BLOCK] for j in range(3))
        sent[b, 0:BLOCK, 0:128] = y.astype(BF)
        y = sum(w_x[j] * x_pad[start + j : start + j + BLOCK] for j in range(3))
        sent[b, 0:BLOCK, 128:256] = y.astype(BF)
        for t in range(2):
            first, second = y[128 * t : 128 * t + 64], y[128 * t + 64 : 128 * t + 128]
            there = slice(128 * t, 128 * t + 128)
            sent[b ^ 1, BLOCK:, there] = jnp.where(low64, first, turned(second)).astype(BF)


def conv(place, got, short, skip):
    ahead_h, ahead_l, back_h, back_l = (jnp.asarray(t) for t in tables())
    full = lambda *shape: pl.BlockSpec(shape, lambda n, p: (0,) * len(shape))
    return pl.pallas_call(
        conv_kernel,
        grid_spec=pltpu.PrefetchScalarGridSpec(
            num_scalar_prefetch=1,
            grid=(1,),
            in_specs=[
                full(8, SENT_ROWS, 256),
                pl.BlockSpec((9, 128), lambda n, p: (0, p[0] // 2)),
                pl.BlockSpec((1, 128), lambda n, p: (0, p[0] // 2)),
                full(512, BLOCK),
                full(512, BLOCK),
                full(BLOCK, 512),
                full(BLOCK, 512),
            ],
            out_specs=[full(8, SENT_ROWS, 256), full(8, 8, 16, 128)],
            scratch_shapes=[
                pltpu.VMEM((8 + 8 * BLOCK, 128), F32),
                pltpu.VMEM((8 + 8 * BLOCK, 128), F32),
                pltpu.VMEM((8, BLOCK, 128), F32),
                pltpu.VMEM((8, BLOCK, 128), F32),
                pltpu.VMEM((8, BLOCK, 128), F32),
                pltpu.VMEM((8, 512, 128), F32),
                pltpu.VMEM((8, 512, 128), F32),
                pltpu.VMEM((8, 512, 128), F32),
                pltpu.VMEM((4, 512, 128), F32),
                pltpu.VMEM((8, BLOCK, 128), F32),
                pltpu.VMEM((8 + 8 * BLOCK, 128), F32),
                pltpu.VMEM((8 + 8 * BLOCK, 128), F32),
            ],
        ),
        out_shape=[
            jax.ShapeDtypeStruct((8, SENT_ROWS, 256), BF),
            jax.ShapeDtypeStruct((8, 8, 16, 128), BF),
        ],
        name="conv",
    )(place, got, short, skip, ahead_h, ahead_l, back_h, back_l)


def spread(got, there, first, second, low):
    for q in range(4):
        lanes = slice(128 * q, 128 * q + 128)
        a = got[2 * q, 0:BLOCK, there].astype(F32)
        b = got[2 * q + 1, 0:BLOCK, there].astype(F32)
        if first is not None:
            first[:, lanes] = jnp.where(low, a, turned(b)).astype(BF)
        if second is not None:
            second[:, lanes] = jnp.where(low, turned(a), b).astype(BF)


def mixed_kernel(got, mixed):
    spread(got, slice(128, 256), mixed.at[0], None, low_lanes(BLOCK))
    low = low_lanes(64)
    for q in range(4):
        lanes = slice(128 * q, 128 * q + 128)
        for t in range(2):
            there = slice(128 * t, 128 * t + 128)
            a = got[2 * q, BLOCK:, there].astype(F32)
            b = got[2 * q + 1, BLOCK:, there].astype(F32)
            mixed[1, 128 * t : 128 * t + 64, lanes] = jnp.where(low, a, turned(b)).astype(BF)
            mixed[1, 128 * t + 64 : 128 * t + 128, lanes] = jnp.where(low, turned(a), b).astype(BF)


def unpack_mixed(got):
    return pl.pallas_call(
        mixed_kernel,
        out_shape=jax.ShapeDtypeStruct((2, BLOCK, 512), BF),
        name="unpack_mixed",
    )(got)


def grads_kernel(got, grads):
    low = low_lanes(BLOCK)
    spread(got, slice(0, 128), grads.at[1], grads.at[0], low)
    spread(got, slice(128, 256), None, grads.at[2], low)


def unpack_grads(got):
    return pl.pallas_call(
        grads_kernel,
        out_shape=jax.ShapeDtypeStruct((3, BLOCK, 512), BF),
        cost_estimate=pl.CostEstimate(flops=10**6, bytes_accessed=2 * 10**6, transcendentals=0),
        name="unpack_grads",
    )(got)


def partial_kernel(place, mine, theirs, g00, g01, g10, g11, lags, lags_beside, packed):
    def term(mixed, grad):
        return lax.dot_general(
            mixed, grad[...], (((0,), (0,)), ((), ())), preferred_element_type=F32
        )

    part = term(mine[0], g00) + term(mine[1], g01) + term(theirs[0], g10) + term(theirs[1], g11)
    part = part.astype(BF)
    for x in range(4):
        for k in range(8):
            start = 128 * x + 16 * k
            packed[4 * k + x, :, 0:1024] = part[start : start + 16]
            packed[4 * k + x, :, 1024:1152] = lags[x, k]
            packed[4 * k + x, :, 1152:1280] = lags_beside[x, k]


def partial(place, mine, theirs, grad, grads, lags, lags_beside):
    full = lambda *shape: pl.BlockSpec(shape, lambda n, p: (0,) * len(shape))
    return pl.pallas_call(
        partial_kernel,
        grid_spec=pltpu.PrefetchScalarGridSpec(
            num_scalar_prefetch=1,
            grid=(1,),
            in_specs=[
                full(2, BLOCK, 512),
                full(2, BLOCK, 512),
                pl.BlockSpec((BLOCK, 1024), lambda n, p: (0, p[0])),
                full(BLOCK, 1024),
                full(BLOCK, 1024),
                full(BLOCK, 1024),
                full(4, 8, 16, 128),
                full(4, 8, 16, 128),
            ],
            out_specs=full(32, 16, 1280),
        ),
        out_shape=jax.ShapeDtypeStruct((32, 16, 1280), BF),
        name="partial",
    )(place, mine, theirs, grad, *grads, lags, lags_beside)


def reduce_kernel(scale, got, shared):
    total = jnp.zeros((16, 1024), F32)
    for n in range(32):
        total = total + got[n, :, 0:1024].astype(F32)
    total = (total * scale).astype(BF)
    for k in range(8):
        shared[k, :, 0:1024] = total
    for x in range(4):
        lag = jnp.zeros((16, 256), F32)
        for k in range(8):
            lag = lag + got[4 * k + x, :, 1024:1280].astype(F32)
        lag = (lag * scale).astype(BF)
        for k in range(8):
            for m in range(2):
                there = slice(1024 + 512 * m + 128 * x, 1152 + 512 * m + 128 * x)
                shared[k, :, there] = lag[:, 128 * m : 128 * m + 128]


def reduce(got, scale):
    return pl.pallas_call(
        functools.partial(reduce_kernel, scale),
        out_shape=jax.ShapeDtypeStruct((8, 16, 2048), BF),
        name="reduce",
    )(got)


def half_kernel(place, mine, *refs):
    grad_weight, wide, sems = refs[-3:]

    def copy(n):
        rows = slice(128 * (n // 2), 128 * (n // 2) + 128)
        lanes = pl.ds(pl.multiple_of(2048 * place[0] + 1024 * (n % 2), 1024), 1024)
        return pltpu.make_async_copy(wide.at[n], grad_weight.at[rows, lanes], sems.at[n])

    for n in range(8):
        for k in range(8):
            wide[n, 16 * k : 16 * k + 16] = mine[n, k].astype(F32)
        copy(n).start()
    for n in range(8):
        copy(n).wait()


def write_half(half, rows, whole=None):
    more = [] if whole is None else [whole]
    return pl.pallas_call(
        half_kernel,
        grid_spec=pltpu.PrefetchScalarGridSpec(
            num_scalar_prefetch=1,
            grid=(1,),
            in_specs=[pl.BlockSpec((8, 8, 16, 1024), lambda n, p: (0, 0, 0, 0))]
            + [pl.BlockSpec(memory_space=pltpu.HBM)] * len(more),
            out_specs=pl.BlockSpec(memory_space=pltpu.HBM),
            scratch_shapes=[
                pltpu.VMEM((8, 128, 1024), F32),
                pltpu.SemaphoreType.DMA((8,)),
            ],
        ),
        out_shape=jax.ShapeDtypeStruct((512, 4096), F32),
        input_output_aliases={2: 0} if more else {},
        cost_estimate=pl.CostEstimate(flops=10**6, bytes_accessed=6 * 10**6, transcendentals=0),
        name="write_half",
    )(half, rows, *more)


def filter_kernel(place, lags, lags_c, grad_filter):
    low = low_lanes(16)
    first = place[0] == 0
    for k in range(8):
        for q in range(4):
            def both(start):
                there = slice(start + 128 * q, start + 128 * q + 128)
                return lags[k, :, there].astype(F32) + lags_c[k, :, there].astype(F32)

            own, other = both(0), both(512)
            a, b = jnp.where(first, own, other), jnp.where(first, other, own)
            lanes = slice(128 * q, 128 * q + 128)
            grad_filter[32 * k : 32 * k + 16, lanes] = jnp.where(low, a, turned(b))
            grad_filter[32 * k + 16 : 32 * k + 32, lanes] = jnp.where(low, turned(a), b)


def write_filter(side, lags, lags_c):
    full = lambda *shape: pl.BlockSpec(shape, lambda n, p: (0,) * len(shape))
    return pl.pallas_call(
        filter_kernel,
        grid_spec=pltpu.PrefetchScalarGridSpec(
            num_scalar_prefetch=1,
            grid=(1,),
            in_specs=[full(8, 16, 1024)] * 2,
            out_specs=full(BLOCK, 512),
        ),
        out_shape=jax.ShapeDtypeStruct((BLOCK, 512), F32),
        cost_estimate=pl.CostEstimate(flops=10**6, bytes_accessed=2 * 10**6, transcendentals=0),
        name="write_filter",
    )(side, lags, lags_c)


def exchange(x, axes):
    return lax.all_to_all(x, axes, 0, 0, tiled=True)


def across(x):
    return lax.ppermute(x, "c", [(0, 1), (1, 0)])


def beside(x):
    return lax.ppermute(x, "yl", [(0, 1), (1, 0)])


def opposite(x):
    return lax.ppermute(x, ("c", "yl"), [(n, 3 - n) for n in range(4)])


def on_device(streams, short_filter, long_filter, skip_gain, out_weight, out_grad):
    scale = 1.0 / math.sqrt(16 * 2048)
    core = lax.axis_index("c").astype(jnp.int32)
    side = lax.axis_index("yl").astype(jnp.int32)
    seq = lax.axis_index(SEQ).astype(jnp.int32)
    grad = out_grad[0]

    def quarter(c, y):
        return lax.dynamic_slice(grad, (0, 1024 * (2 * c + y)), (BLOCK, 1024))

    grads = (
        beside(quarter(core, 1 - side)),
        across(quarter(1 - core, side)),
        opposite(quarter(1 - core, 1 - side)),
    )
    got = exchange(pack(streams[:, 0], grad, out_weight, long_filter), SEQ)
    sent, lags = conv(
        seq[None], got, short_filter.reshape(9, 512), skip_gain.reshape(1, 512)
    )
    sent, grads = lax.optimization_barrier((sent, grads))
    lags = lags.reshape(4, 2, 8, 16, 128)
    lags_own = lax.dynamic_index_in_dim(lags, side, 1, False)
    lags_beside = beside(lax.dynamic_index_in_dim(lags, 1 - side, 1, False))
    back = exchange(sent, SEQ)
    back, lags_own, lags_beside = lax.optimization_barrier((back, lags_own, lags_beside))
    mixed = unpack_mixed(back)
    mixed_theirs = across(mixed)
    part = partial(
        (2 * core + side)[None], mixed, mixed_theirs, grad, grads, lags_own, lags_beside
    )
    part, mixed, back = lax.optimization_barrier((part, mixed, back))
    part = exchange(part, DEPTH + ("x",))
    layer_out = jnp.dot(mixed[0], out_weight, preferred_element_type=F32).astype(BF)
    grad_streams = unpack_grads(back)
    part, layer_out, grad_streams = lax.optimization_barrier((part, layer_out, grad_streams))
    shared = exchange(reduce(part, scale), DEPTH)
    rows = jnp.broadcast_to(shared[None, :, :, :1024], (8, 8, 16, 1024))
    rows, shared = lax.optimization_barrier((rows, shared))
    mine = exchange(rows, SEQ)
    shared_lags = shared[:, :, 1024:]
    grad_filter = write_filter(side[None], shared_lags, across(shared_lags))
    mine, grad_filter = lax.optimization_barrier((mine, grad_filter))
    theirs = across(mine)
    grad_weight = write_half(core[None], mine)
    grad_weight = write_half(1 - core[None], theirs, grad_weight)
    return layer_out[None], grad_streams[:, None], grad_filter, grad_weight


def solution(mesh):
    fine = Mesh(mesh.devices.reshape(4, 2, 2, 4, 2), ("z", "yh", "c", "x", "yl"))
    dp = ("z", "yh", "c")
    placed = (P(None, dp, SEQ, None), P(), P(SEQ, None), P(), P(), P(dp, SEQ, None))
    return jax.shard_map(
        on_device,
        mesh=fine,
        in_specs=placed,
        out_specs=(P(dp, SEQ, None), P(None, dp, SEQ, None), P(SEQ, None), P()),
        check_vma=False,
    )
```

```python
import functools
import math

import jax
import jax.numpy as jnp
import numpy as np
from jax import lax
from jax.experimental import pallas as pl
from jax.experimental.pallas import tpu as pltpu
from jax.sharding import Mesh, PartitionSpec as P

BF = jnp.bfloat16
F32 = jnp.float32
BLOCK = 256
HALF = 64
SENT_ROWS = BLOCK + 64
SEQ = ("x", "yl")
MOST = ("zh", "yh") + SEQ
CHIPS = ("zh", "zl", "yh") + SEQ


@functools.lru_cache(maxsize=None)
def tables():
    order = np.concatenate([np.arange(0, BLOCK, 2), np.arange(1, BLOCK, 2)])
    angle = np.pi * ((2 * order[:, None] + 1) * np.arange(BLOCK)[None, :] % 1024) / 512.0
    ahead = np.concatenate([np.cos(angle), -np.sin(angle)], axis=0)
    back = ahead.T / BLOCK

    def two(table):
        table = table.astype(np.float32)
        high = table.astype(jnp.bfloat16)
        return high, (table - high.astype(np.float32)).astype(jnp.bfloat16)

    return two(ahead) + two(back)


def mm(a, b):
    return jnp.dot(a, b, preferred_element_type=F32)


def low_lanes(rows):
    return lax.broadcasted_iota(jnp.int32, (rows, 128), 1) < HALF


def turned(x):
    return pltpu.roll(x, HALF, 1)


def pack_kernel(streams, out_grad, weight, filt, packed, total):
    step = pl.program_id(0)
    low = low_lanes(BLOCK)

    @pl.when(step == 0)
    def _():
        total[...] = jnp.zeros_like(total)

    total[...] += lax.dot_general(
        out_grad[...], weight[...], (((1,), (1,)), ((), ())), preferred_element_type=F32
    )

    def put(q, tile, a, b):
        lanes = slice(128 * tile, 128 * tile + 128)
        packed[2 * q, 0:BLOCK, lanes] = jnp.where(low, a, turned(b)).astype(BF)
        packed[2 * q + 1, 0:BLOCK, lanes] = jnp.where(low, turned(a), b).astype(BF)

    for q in range(4):
        lanes = slice(128 * q, 128 * q + 128)

        @pl.when(step == q)
        def _(q=q, lanes=lanes):
            put(q, 0, streams[0, :, lanes].astype(F32), streams[1, :, lanes].astype(F32))
            low64 = low_lanes(64)
            for n in range(2):
                a = filt[128 * n : 128 * n + 64, lanes]
                b = filt[128 * n + 64 : 128 * n + 128, lanes]
                there = slice(128 * n, 128 * n + 128)
                packed[2 * q, BLOCK:, there] = jnp.where(low64, a, turned(b)).astype(BF)
                packed[2 * q + 1, BLOCK:, there] = jnp.where(low64, turned(a), b).astype(BF)

    @pl.when(step == pl.num_programs(0) - 1)
    def _():
        for q in range(4):
            lanes = slice(128 * q, 128 * q + 128)
            put(q, 1, streams[2, :, lanes].astype(F32), total[:, lanes])


def pack(streams, out_grad, weight, filt):
    steps = 4
    wide = out_grad.shape[1] // steps
    return pl.pallas_call(
        pack_kernel,
        grid=(steps,),
        in_specs=[
            pl.BlockSpec((3, BLOCK, 512), lambda k: (0, 0, 0)),
            pl.BlockSpec((BLOCK, wide), lambda k: (0, k)),
            pl.BlockSpec((512, wide), lambda k: (0, k)),
            pl.BlockSpec((BLOCK, 512), lambda k: (0, 0)),
        ],
        out_specs=pl.BlockSpec((8, SENT_ROWS, 256), lambda k: (0, 0, 0)),
        out_shape=jax.ShapeDtypeStruct((8, SENT_ROWS, 256), BF),
        scratch_shapes=[pltpu.VMEM((BLOCK, 512), F32)],
        name="pack",
    )(streams, out_grad, weight, filt)


def conv_kernel(
    place, got, short, skip, ahead_h, ahead_l, back_h, back_l,
    sent, lags,
    sa_pad, sv_pad, sa, sv, prod, spec, fspec, res, lres, time, u_pad, x_pad,
):
    low = low_lanes(BLOCK)
    low1 = low_lanes(1)
    sigma = jnp.where(low, 1.0, -1.0)
    odd = place[0] % 2 == 1

    taps = short[...]
    taps = jnp.where(odd, turned(taps), taps)
    taps_up = turned(taps)
    gain = skip[...]
    gain = jnp.where(odd, turned(gain), gain)
    gain = jnp.where(low1, gain, turned(gain))

    def tap(i, j):
        return taps[3 * i + j : 3 * i + j + 1]

    def tap_up(i, j):
        return taps_up[3 * i + j : 3 * i + j + 1]

    def unit(j):
        return jnp.full((1, 128), 1.0 if j == 0 else 0.0, F32)

    w_a = [jnp.where(low1, tap(0, j), tap_up(1, j)) for j in range(3)]
    w_v = [jnp.where(low1, tap(2, j), unit(j)) for j in range(3)]
    w_u = [jnp.where(low1, tap(1, j), tap_up(0, j)) for j in range(3)]
    w_x = [jnp.where(low1, unit(j), tap_up(2, j)) for j in range(3)]

    def split(x):
        high = x.astype(BF)
        return high, (x - high.astype(F32)).astype(BF)

    def apply(table_h, table_l, high, rest):
        return mm(table_h[...], high) + mm(table_h[...], rest) + mm(table_l[...], high)

    sa_pad[0:8] = jnp.zeros((8, 128), F32)
    sv_pad[0:8] = jnp.zeros((8, 128), F32)

    def load(b, carry):
        rows = pl.ds(pl.multiple_of(8 + BLOCK * b, 8), BLOCK)
        sa_pad[rows] = got[b, 0:BLOCK, 0:128].astype(F32)
        sv_pad[rows] = got[b, 0:BLOCK, 128:256].astype(F32)
        return carry

    lax.fori_loop(0, 8, load, 0)

    low64 = low_lanes(64)

    def filters(n, carry):
        def pair(b):
            parts = []
            for t in range(2):
                x = got[b, BLOCK:, 128 * t : 128 * t + 128].astype(F32)
                y = got[b + 1, BLOCK:, 128 * t : 128 * t + 128].astype(F32)
                parts.append(jnp.where(low64, x, turned(y)))
                parts.append(jnp.where(low64, turned(x), y))
            return jnp.concatenate(parts, axis=0).astype(BF)

        f = jnp.concatenate([pair(4 * n), pair(4 * n + 2)], axis=1)
        out = mm(ahead_h[...], f) + mm(ahead_l[...], f)
        low512 = low_lanes(512)
        for t in range(2):
            x = out[:, 128 * t : 128 * t + 128]
            y = turned(x)
            fspec[4 * n + 2 * t] = jnp.where(low512, x, y)
            fspec[4 * n + 2 * t + 1] = jnp.where(low512, y, x)
        return carry

    lax.fori_loop(0, 2, filters, 0)

    for b in range(8):
        start = 8 + BLOCK * b
        a = sum(w_a[j] * sa_pad[start - j : start - j + BLOCK] for j in range(3))
        v = sum(w_v[j] * sv_pad[start - j : start - j + BLOCK] for j in range(3))
        sa[b] = a
        sv[b] = v
        prod[b] = turned(a) * v

    def transform(n, carry):
        x = jnp.concatenate(
            [jnp.where(low, prod[b], prod[7 - b]) for b in (2 * n, 2 * n + 1)], axis=1
        )
        out = apply(ahead_h, ahead_l, *split(x))
        for t in range(2):
            spec[2 * n + t, 0:BLOCK] = out[:BLOCK, 128 * t : 128 * t + 128]
            spec[2 * n + t, BLOCK:] = out[BLOCK:, 128 * t : 128 * t + 128] * sigma
        return carry

    lax.fori_loop(0, 4, transform, 0)

    for sign, base in ((1.0, 0), (-1.0, 128)):

        def multiply(n, carry, sign=sign, base=base):
            re = pl.ds(pl.multiple_of(base + 8 * n, 8), 8)
            im = pl.ds(pl.multiple_of(BLOCK + base + 8 * n, 8), 8)
            own = [(spec[j, re], spec[j, im]) for j in range(8)]
            both = [own[0]]
            for j in range(1, 8):
                both.append(
                    (own[j][0] - sign * own[j - 1][1], own[j][1] + sign * own[j - 1][0])
                )
            filt = [(fspec[m, re], fspec[m, im]) for m in range(8)]

            def summed(pairs):
                first = True
                for (ar, ai), (br, bi) in pairs:
                    pr = ar * br - ai * bi
                    pi = ar * bi + ai * br
                    tr, ti = (pr, pi) if first else (tr + pr, ti + pi)
                    first = False
                return tr, ti

            for i in range(8):
                tr, ti = summed([(filt[m], both[i - m]) for m in range(i + 1)])
                res[i, re] = tr
                res[i, im] = ti
            zero = jnp.zeros((8, 128), F32)
            low8 = low_lanes(8)
            grads, shifted = [], []
            for i in range(8):
                grads.append(
                    tuple(jnp.where(low8, turned(own[7 - i][k]), own[7 - i][k]) for k in range(2))
                )
                before = both[i - 1] if i else (zero, zero)
                shifted.append(
                    tuple(jnp.where(low8, before[k], turned(both[i][k])) for k in range(2))
                )
            for a in range(4):
                tr, ti = summed([(grads[i], shifted[i - 2 * a]) for i in range(2 * a, 8)])
                lres[a, re] = tr
                lres[a, im] = ti
            return carry

        lax.fori_loop(0, 16, multiply, 0)

    def flipped(x, sign):
        return jnp.concatenate([x[0:BLOCK], x[BLOCK:] * sign], axis=0)

    def invert(n, carry):
        x = jnp.concatenate([flipped(res[b], sigma) for b in (2 * n, 2 * n + 1)], axis=1)
        out = apply(back_h, back_l, *split(x))
        time[2 * n] = out[:, :128]
        time[2 * n + 1] = out[:, 128:]
        return carry

    lax.fori_loop(0, 4, invert, 0)

    def invert_lags(n, carry):
        x = jnp.concatenate([flipped(lres[a], -1.0) for a in (2 * n, 2 * n + 1)], axis=1)
        out = apply(back_h, back_l, *split(x))
        low16 = low_lanes(16)
        for t in range(2):
            for k in range(8):
                x = out[32 * k : 32 * k + 16, 128 * t : 128 * t + 128]
                y = out[32 * k + 16 : 32 * k + 32, 128 * t : 128 * t + 128]
                m = 4 * n + 2 * t
                lags[m, k] = jnp.where(low16, turned(x), y).astype(BF)
                lags[m + 1, k] = jnp.where(low16, x, turned(y)).astype(BF)
        return carry

    lax.fori_loop(0, 2, invert_lags, 0)

    def gate(b, carry):
        t = jnp.where(low, time[b], time[7 - b]) + gain * prod[b]
        rows = pl.ds(pl.multiple_of(BLOCK * b, 8), BLOCK)
        u_pad[rows] = turned(t) * sv[b]
        x_pad[rows] = t * sa[b]
        return carry

    lax.fori_loop(0, 8, gate, 0)
    u_pad[8 * BLOCK :] = jnp.zeros((8, 128), F32)
    x_pad[8 * BLOCK :] = jnp.zeros((8, 128), F32)
    for b in range(8):
        start = BLOCK * b
        y = sum(w_u[j] * u_pad[start + j : start + j + BLOCK] for j in range(3))
        sent[b, 0:BLOCK, 0:128] = y.astype(BF)
        y = sum(w_x[j] * x_pad[start + j : start + j + BLOCK] for j in range(3))
        sent[b, 0:BLOCK, 128:256] = y.astype(BF)


def conv(place, got, short, skip):
    ahead_h, ahead_l, back_h, back_l = (jnp.asarray(t) for t in tables())
    full = lambda *shape: pl.BlockSpec(shape, lambda n, p: (0,) * len(shape))
    return pl.pallas_call(
        conv_kernel,
        grid_spec=pltpu.PrefetchScalarGridSpec(
            num_scalar_prefetch=1,
            grid=(1,),
            in_specs=[
                full(8, SENT_ROWS, 256),
                pl.BlockSpec((9, 128), lambda n, p: (0, p[0] // 2)),
                pl.BlockSpec((1, 128), lambda n, p: (0, p[0] // 2)),
                full(512, BLOCK),
                full(512, BLOCK),
                full(BLOCK, 512),
                full(BLOCK, 512),
            ],
            out_specs=[full(8, BLOCK, 256), full(8, 8, 16, 128)],
            scratch_shapes=[
                pltpu.VMEM((8 + 8 * BLOCK, 128), F32),
                pltpu.VMEM((8 + 8 * BLOCK, 128), F32),
                pltpu.VMEM((8, BLOCK, 128), F32),
                pltpu.VMEM((8, BLOCK, 128), F32),
                pltpu.VMEM((8, BLOCK, 128), F32),
                pltpu.VMEM((8, 512, 128), F32),
                pltpu.VMEM((8, 512, 128), F32),
                pltpu.VMEM((8, 512, 128), F32),
                pltpu.VMEM((4, 512, 128), F32),
                pltpu.VMEM((8, BLOCK, 128), F32),
                pltpu.VMEM((8 + 8 * BLOCK, 128), F32),
                pltpu.VMEM((8 + 8 * BLOCK, 128), F32),
            ],
        ),
        out_shape=[
            jax.ShapeDtypeStruct((8, BLOCK, 256), BF),
            jax.ShapeDtypeStruct((8, 8, 16, 128), BF),
        ],
        name="conv",
    )(place, got, short, skip, ahead_h, ahead_l, back_h, back_l)


def spread(got, there, first, second, low):
    for q in range(4):
        lanes = slice(128 * q, 128 * q + 128)
        a = got[2 * q, 0:BLOCK, there].astype(F32)
        b = got[2 * q + 1, 0:BLOCK, there].astype(F32)
        if first is not None:
            first[:, lanes] = jnp.where(low, a, turned(b)).astype(BF)
        if second is not None:
            second[:, lanes] = jnp.where(low, turned(a), b).astype(BF)


def mixed_kernel(got, mixed):
    spread(got, slice(0, 128), mixed, None, low_lanes(BLOCK))


def unpack_mixed(got):
    return pl.pallas_call(
        mixed_kernel,
        grid=(1,),
        in_specs=[pl.BlockSpec((8, BLOCK, 128), lambda n: (0, 0, 1))],
        out_specs=pl.BlockSpec((BLOCK, 512), lambda n: (0, 0)),
        out_shape=jax.ShapeDtypeStruct((BLOCK, 512), BF),
        name="unpack_mixed",
    )(got)


def grads_kernel(got, grads):
    low = low_lanes(BLOCK)
    spread(got, slice(0, 128), grads.at[1], grads.at[0], low)
    spread(got, slice(128, 256), None, grads.at[2], low)


def unpack_grads(got):
    return pl.pallas_call(
        grads_kernel,
        out_shape=jax.ShapeDtypeStruct((3, BLOCK, 512), BF),
        cost_estimate=pl.CostEstimate(flops=10**6, bytes_accessed=2 * 10**6, transcendentals=0),
        name="unpack_grads",
    )(got)


def partial_kernel(place, m00, m01, m10, m11, g00, g01, g10, g11, lags, lags_z, packed):
    def term(mixed, grad):
        return lax.dot_general(
            mixed[...], grad[...], (((0,), (0,)), ((), ())), preferred_element_type=F32
        )

    part = term(m00, g00) + term(m01, g01) + term(m10, g10) + term(m11, g11)
    part = part.astype(BF)
    for n in range(32):
        packed[n, :, 0:1024] = part[16 * n : 16 * n + 16]
        s, k = n % 8, n // 8
        lag = lags[s, k].astype(F32) + lags_z[s, k].astype(F32)
        packed[n, :, 1024:1152] = lag.astype(BF)


def partial(place, mixed, grad, grads, lags, lags_z):
    full = lambda *shape: pl.BlockSpec(shape, lambda n, p: (0,) * len(shape))
    return pl.pallas_call(
        partial_kernel,
        grid_spec=pltpu.PrefetchScalarGridSpec(
            num_scalar_prefetch=1,
            grid=(1,),
            in_specs=[full(BLOCK, 512)] * 4
            + [pl.BlockSpec((BLOCK, 1024), lambda n, p: (0, p[0]))]
            + [full(BLOCK, 1024)] * 3
            + [full(8, 4, 16, 128)] * 2,
            out_specs=full(32, 16, 1152),
        ),
        out_shape=jax.ShapeDtypeStruct((32, 16, 1152), BF),
        name="partial",
    )(place, *mixed, grad, *grads, lags, lags_z)


def reduce_kernel(scale, got, shared, lags):
    total = jnp.zeros((16, 1024), F32)
    for n in range(32):
        total = total + got[n, :, 0:1024].astype(F32)
    total = (total * scale).astype(BF)
    for n in range(64):
        shared[n] = total
    for s in range(8):
        lag = jnp.zeros((16, 128), F32)
        for k in range(4):
            lag = lag + got[8 * k + s, :, 1024:1152].astype(F32)
        lags[:, 128 * s : 128 * s + 128] = lag * scale


def reduce(got, scale):
    return pl.pallas_call(
        functools.partial(reduce_kernel, scale),
        out_shape=[
            jax.ShapeDtypeStruct((64, 16, 1024), BF),
            jax.ShapeDtypeStruct((16, 1024), F32),
        ],
        name="reduce",
    )(got)


def half_kernel(place, mine, *refs):
    grad_weight, wide, sems = refs[-3:]

    def copy(n):
        zh, zl, yh = n // 4, n // 2 % 2, n % 2
        rows = slice(128 * (2 * zh + yh), 128 * (2 * zh + yh) + 128)
        lanes = pl.ds(pl.multiple_of(2048 * place[0] + 1024 * zl, 1024), 1024)
        return pltpu.make_async_copy(wide.at[n], grad_weight.at[rows, lanes], sems.at[n])

    for n in range(8):
        for k in range(8):
            wide[n, 16 * k : 16 * k + 16] = mine[8 * n + k].astype(F32)
        copy(n).start()
    for n in range(8):
        copy(n).wait()


def write_half(half, rows, whole=None):
    more = [] if whole is None else [whole]
    return pl.pallas_call(
        half_kernel,
        grid_spec=pltpu.PrefetchScalarGridSpec(
            num_scalar_prefetch=1,
            grid=(1,),
            in_specs=[pl.BlockSpec((64, 16, 1024), lambda n, p: (0, 0, 0))]
            + [pl.BlockSpec(memory_space=pltpu.HBM)] * len(more),
            out_specs=pl.BlockSpec(memory_space=pltpu.HBM),
            scratch_shapes=[
                pltpu.VMEM((8, 128, 1024), F32),
                pltpu.SemaphoreType.DMA((8,)),
            ],
        ),
        out_shape=jax.ShapeDtypeStruct((512, 4096), F32),
        input_output_aliases={2: 0} if more else {},
        cost_estimate=pl.CostEstimate(flops=10**6, bytes_accessed=6 * 10**6, transcendentals=0),
        name="write_half",
    )(half, rows, *more)


def filter_kernel(place, *refs):
    grad_filter = refs[-1]
    low = low_lanes(16)
    for d in range(4):
        z = (place[0] + 4 - d) % 4
        for n in range(2):
            yh = place[1] if n == 0 else 1 - place[1]
            row = pl.multiple_of(32 * (2 * z + yh), 32)
            lags = refs[2 * d + n]
            for q in range(4):
                a = lags[:, 256 * q : 256 * q + 128].astype(F32)
                b = lags[:, 256 * q + 128 : 256 * q + 256].astype(F32)
                lanes = slice(128 * q, 128 * q + 128)
                grad_filter[pl.ds(row, 16), lanes] = jnp.where(low, a, turned(b))
                grad_filter[pl.ds(row + 16, 16), lanes] = jnp.where(low, turned(a), b)


def write_filter(place, lags):
    full = lambda *shape: pl.BlockSpec(shape, lambda n, p: (0,) * len(shape))
    return pl.pallas_call(
        filter_kernel,
        grid_spec=pltpu.PrefetchScalarGridSpec(
            num_scalar_prefetch=1,
            grid=(1,),
            in_specs=[full(16, 1024)] * 8,
            out_specs=full(BLOCK, 512),
        ),
        out_shape=jax.ShapeDtypeStruct((BLOCK, 512), F32),
        cost_estimate=pl.CostEstimate(flops=10**6, bytes_accessed=2 * 10**6, transcendentals=0),
        name="write_filter",
    )(place, *lags)


def exchange(x, axes):
    return lax.all_to_all(x, axes, 0, 0, tiled=True)


def across(x):
    return lax.ppermute(x, "c", [(0, 1), (1, 0)])


def above(x):
    return lax.ppermute(x, "zl", [(0, 1), (1, 0)])


def opposite(x):
    return lax.ppermute(x, ("zl", "c"), [(n, 3 - n) for n in range(4)])


def gathered(lags):
    pair = (lags, lax.ppermute(lags, "yh", [(0, 1), (1, 0)]))
    out = list(pair)
    for d in range(1, 4):
        route = [(n, (n + d) % 4) for n in range(4)]
        out += [lax.ppermute(part, ("zh", "zl"), route) for part in pair]
    return out


def on_device(streams, short_filter, long_filter, skip_gain, out_weight, out_grad):
    scale = 1.0 / math.sqrt(16 * 2048)
    core = lax.axis_index("c").astype(jnp.int32)
    side = lax.axis_index("zl").astype(jnp.int32)
    seq = lax.axis_index(SEQ).astype(jnp.int32)
    grad = out_grad[0]

    def quarter(c, z):
        return lax.dynamic_slice(grad, (0, 1024 * (2 * c + z)), (BLOCK, 1024))

    grads = (
        above(quarter(core, 1 - side)),
        across(quarter(1 - core, side)),
        opposite(quarter(1 - core, 1 - side)),
    )
    got = exchange(pack(streams[:, 0], grad, out_weight, long_filter), SEQ)
    sent, lags = conv(
        seq[None], got, short_filter.reshape(9, 512), skip_gain.reshape(1, 512)
    )
    sent, grads = lax.optimization_barrier((sent, grads))
    lags = lags.reshape(8, 2, 2, 2, 16, 128)

    def of_side(z):
        return lax.dynamic_index_in_dim(lags, z, 2, False).reshape(8, 4, 16, 128)

    lags_own, lags_z = of_side(side), above(of_side(1 - side))
    back = exchange(sent, SEQ)
    back, lags_own, lags_z = lax.optimization_barrier((back, lags_own, lags_z))
    m00 = unpack_mixed(back)
    m01, m10 = above(m00), across(m00)
    mixed = (m00, m01, m10, across(m01))
    part = partial((2 * core + side)[None], mixed, grad, grads, lags_own, lags_z)
    part, m00, back = lax.optimization_barrier((part, m00, back))
    part = exchange(part, MOST)
    layer_out = jnp.dot(m00, out_weight, preferred_element_type=F32).astype(BF)
    grad_streams = unpack_grads(back)
    part, layer_out, grad_streams = lax.optimization_barrier((part, layer_out, grad_streams))
    rows, lags = reduce(part, scale)
    rows, lags = lax.optimization_barrier((rows, lags))
    mine = exchange(rows, CHIPS)
    lags = (lags + across(lags)).astype(BF)
    place = jnp.stack([lax.axis_index(("zh", "zl")), lax.axis_index("yh")]).astype(jnp.int32)
    grad_filter = write_filter(place, gathered(lags))
    mine, grad_filter = lax.optimization_barrier((mine, grad_filter))
    theirs = across(mine)
    grad_weight = write_half(core[None], mine)
    grad_weight = write_half(1 - core[None], theirs, grad_weight)
    return layer_out[None], grad_streams[:, None], grad_filter, grad_weight


def solution(mesh):
    fine = Mesh(
        mesh.devices.reshape(2, 2, 2, 2, 4, 2), ("zh", "zl", "yh", "c", "x", "yl")
    )
    dp = ("zh", "zl", "yh", "c")
    placed = (P(None, dp, SEQ, None), P(), P(SEQ, None), P(), P(), P(dp, SEQ, None))
    return jax.shard_map(
        on_device,
        mesh=fine,
        in_specs=placed,
        out_specs=(P(dp, SEQ, None), P(None, dp, SEQ, None), P(SEQ, None), P()),
        check_vma=False,
    )
```

```python
import functools
import math

import jax
import jax.numpy as jnp
import numpy as np
from jax import lax
from jax.experimental import pallas as pl
from jax.experimental.pallas import tpu as pltpu
from jax.sharding import Mesh, PartitionSpec as P

BF = jnp.bfloat16
F32 = jnp.float32
BLOCK = 256
HALF = 64
SENT_ROWS = BLOCK + 64
SEQ = ("x", "yl")
MOST = ("zh", "yh") + SEQ
CHIPS = ("zh", "zl", "yh") + SEQ


@functools.lru_cache(maxsize=None)
def tables():
    order = np.concatenate([np.arange(0, BLOCK, 2), np.arange(1, BLOCK, 2)])
    angle = np.pi * ((2 * order[:, None] + 1) * np.arange(BLOCK)[None, :] % 1024) / 512.0
    ahead = np.concatenate([np.cos(angle), -np.sin(angle)], axis=0)
    back = ahead.T / BLOCK

    def two(table):
        table = table.astype(np.float32)
        high = table.astype(jnp.bfloat16)
        return high, (table - high.astype(np.float32)).astype(jnp.bfloat16)

    return two(ahead) + two(back)


def mm(a, b):
    return jnp.dot(a, b, preferred_element_type=F32)


def low_lanes(rows):
    return lax.broadcasted_iota(jnp.int32, (rows, 128), 1) < HALF


def turned(x):
    return pltpu.roll(x, HALF, 1)


def pack_kernel(streams, out_grad, weight, filt, packed, total):
    step = pl.program_id(0)
    low = low_lanes(BLOCK)

    @pl.when(step == 0)
    def _():
        total[...] = jnp.zeros_like(total)

    total[...] += lax.dot_general(
        out_grad[...], weight[...], (((1,), (1,)), ((), ())), preferred_element_type=F32
    )

    def put(q, tile, a, b):
        lanes = slice(128 * tile, 128 * tile + 128)
        packed[2 * q, 0:BLOCK, lanes] = jnp.where(low, a, turned(b)).astype(BF)
        packed[2 * q + 1, 0:BLOCK, lanes] = jnp.where(low, turned(a), b).astype(BF)

    for q in range(4):
        lanes = slice(128 * q, 128 * q + 128)

        @pl.when(step == q)
        def _(q=q, lanes=lanes):
            put(q, 0, streams[0, :, lanes].astype(F32), streams[1, :, lanes].astype(F32))
            low64 = low_lanes(64)
            for n in range(2):
                a = filt[128 * n : 128 * n + 64, lanes]
                b = filt[128 * n + 64 : 128 * n + 128, lanes]
                there = slice(128 * n, 128 * n + 128)
                packed[2 * q, BLOCK:, there] = jnp.where(low64, a, turned(b)).astype(BF)
                packed[2 * q + 1, BLOCK:, there] = jnp.where(low64, turned(a), b).astype(BF)

    @pl.when(step == pl.num_programs(0) - 1)
    def _():
        for q in range(4):
            lanes = slice(128 * q, 128 * q + 128)
            put(q, 1, streams[2, :, lanes].astype(F32), total[:, lanes])


def pack(streams, out_grad, weight, filt):
    steps = 4
    wide = out_grad.shape[1] // steps
    return pl.pallas_call(
        pack_kernel,
        grid=(steps,),
        in_specs=[
            pl.BlockSpec((3, BLOCK, 512), lambda k: (0, 0, 0)),
            pl.BlockSpec((BLOCK, wide), lambda k: (0, k)),
            pl.BlockSpec((512, wide), lambda k: (0, k)),
            pl.BlockSpec((BLOCK, 512), lambda k: (0, 0)),
        ],
        out_specs=pl.BlockSpec((8, SENT_ROWS, 256), lambda k: (0, 0, 0)),
        out_shape=jax.ShapeDtypeStruct((8, SENT_ROWS, 256), BF),
        scratch_shapes=[pltpu.VMEM((BLOCK, 512), F32)],
        name="pack",
    )(streams, out_grad, weight, filt)


def split(x):
    high = x.astype(BF)
    return high, (x - high.astype(F32)).astype(BF)


def apply(table_h, table_l, high, rest):
    return mm(table_h[...], high) + mm(table_h[...], rest) + mm(table_l[...], high)


def weights(place, short, skip):
    low1 = low_lanes(1)
    odd = place[0] % 2 == 1
    taps = short[...]
    taps = jnp.where(odd, turned(taps), taps)
    taps_up = turned(taps)
    gain = skip[...]
    gain = jnp.where(odd, turned(gain), gain)
    gain = jnp.where(low1, gain, turned(gain))

    def pair(first, second):
        def row(table, i, j):
            if i is None:
                return jnp.full((1, 128), 1.0 if j == 0 else 0.0, F32)
            return table[3 * i + j : 3 * i + j + 1]

        return [
            jnp.where(low1, row(taps, first, j), row(taps_up, second, j)) for j in range(3)
        ]

    return pair, gain


def shorten(got, pair, sa_pad, sv_pad, use):
    w_a, w_v = pair(0, 1), pair(2, None)
    sa_pad[0:8] = jnp.zeros((8, 128), F32)
    sv_pad[0:8] = jnp.zeros((8, 128), F32)

    def load(b, carry):
        rows = pl.ds(pl.multiple_of(8 + BLOCK * b, 8), BLOCK)
        sa_pad[rows] = got[b, 0:BLOCK, 0:128].astype(F32)
        sv_pad[rows] = got[b, 0:BLOCK, 128:256].astype(F32)
        return carry

    lax.fori_loop(0, 8, load, 0)
    for b in range(8):
        start = 8 + BLOCK * b
        a = sum(w_a[j] * sa_pad[start - j : start - j + BLOCK] for j in range(3))
        v = sum(w_v[j] * sv_pad[start - j : start - j + BLOCK] for j in range(3))
        use(b, a, v)


def spectra(prod, ahead_h, ahead_l, spec):
    low = low_lanes(BLOCK)
    sigma = jnp.where(low, 1.0, -1.0)

    def transform(n, carry):
        x = jnp.concatenate(
            [jnp.where(low, prod[b], prod[7 - b]) for b in (2 * n, 2 * n + 1)], axis=1
        )
        out = apply(ahead_h, ahead_l, *split(x))
        for t in range(2):
            spec[2 * n + t, 0:BLOCK] = out[:BLOCK, 128 * t : 128 * t + 128]
            spec[2 * n + t, BLOCK:] = out[BLOCK:, 128 * t : 128 * t + 128] * sigma
        return carry

    lax.fori_loop(0, 4, transform, 0)


def over_bins(spec, use):
    for sign, base in ((1.0, 0), (-1.0, 128)):

        def step(n, carry, sign=sign, base=base):
            re = pl.ds(pl.multiple_of(base + 8 * n, 8), 8)
            im = pl.ds(pl.multiple_of(BLOCK + base + 8 * n, 8), 8)
            own = [(spec[j, re], spec[j, im]) for j in range(8)]
            both = [own[0]]
            for j in range(1, 8):
                both.append(
                    (own[j][0] - sign * own[j - 1][1], own[j][1] + sign * own[j - 1][0])
                )
            use(re, im, own, both)
            return carry

        lax.fori_loop(0, 16, step, 0)


def summed(pairs):
    first = True
    for (ar, ai), (br, bi) in pairs:
        pr = ar * br - ai * bi
        pi = ar * bi + ai * br
        tr, ti = (pr, pi) if first else (tr + pr, ti + pi)
        first = False
    return tr, ti


def flipped(x, sign):
    return jnp.concatenate([x[0:BLOCK], x[BLOCK:] * sign], axis=0)


def conv_kernel(
    place, got, short, skip, ahead_h, ahead_l, back_h, back_l,
    sent, whole,
    sa_pad, sv_pad, sa, prod, spec, fspec, res, time,
):
    low = low_lanes(BLOCK)
    low64 = low_lanes(64)
    sigma = jnp.where(low, 1.0, -1.0)
    pair, gain = weights(place, short, skip)

    def filters(n, carry):
        def blocks(b):
            parts = []
            for t in range(2):
                x = got[b, BLOCK:, 128 * t : 128 * t + 128].astype(F32)
                y = got[b + 1, BLOCK:, 128 * t : 128 * t + 128].astype(F32)
                parts.append(jnp.where(low64, x, turned(y)))
                parts.append(jnp.where(low64, turned(x), y))
            return jnp.concatenate(parts, axis=0).astype(BF)

        f = jnp.concatenate([blocks(4 * n), blocks(4 * n + 2)], axis=1)
        out = mm(ahead_h[...], f) + mm(ahead_l[...], f)
        low512 = low_lanes(512)
        for t in range(2):
            x = out[:, 128 * t : 128 * t + 128]
            y = turned(x)
            fspec[4 * n + 2 * t] = jnp.where(low512, x, y)
            fspec[4 * n + 2 * t + 1] = jnp.where(low512, y, x)
        return carry

    lax.fori_loop(0, 2, filters, 0)

    def keep(b, a, v):
        sa[b] = a
        prod[b] = turned(a) * v

    shorten(got, pair, sa_pad, sv_pad, keep)
    spectra(prod, ahead_h, ahead_l, spec)

    def multiply(re, im, own, both):
        filt = [(fspec[m, re], fspec[m, im]) for m in range(8)]
        for i in range(8):
            tr, ti = summed([(filt[m], both[i - m]) for m in range(i + 1)])
            res[i, re] = tr
            res[i, im] = ti

    over_bins(spec, multiply)

    def invert(n, carry):
        x = jnp.concatenate([flipped(res[b], sigma) for b in (2 * n, 2 * n + 1)], axis=1)
        out = apply(back_h, back_l, *split(x))
        time[2 * n] = out[:, :128]
        time[2 * n + 1] = out[:, 128:]
        return carry

    lax.fori_loop(0, 4, invert, 0)

    def gate(b, carry):
        t = jnp.where(low, time[b], time[7 - b]) + gain * prod[b]
        whole[b] = t
        y = t * sa[b]
        for n in range(2):
            first, second = y[128 * n : 128 * n + 64], y[128 * n + 64 : 128 * n + 128]
            there = slice(128 * n, 128 * n + 128)
            sent[b, :, there] = jnp.where(low64, first, turned(second)).astype(BF)
        return carry

    lax.fori_loop(0, 8, gate, 0)


def lag_kernel(
    place, got, short, skip, ahead_h, ahead_l, back_h, back_l,
    lags,
    sa_pad, sv_pad, prod, spec, lres,
):
    pair, _ = weights(place, short, skip)

    def keep(b, a, v):
        prod[b] = turned(a) * v

    shorten(got, pair, sa_pad, sv_pad, keep)
    spectra(prod, ahead_h, ahead_l, spec)
    zero = jnp.zeros((8, 128), F32)
    low8 = low_lanes(8)

    def multiply(re, im, own, both):
        grads, shifted = [], []
        for i in range(8):
            grads.append(
                tuple(jnp.where(low8, turned(own[7 - i][k]), own[7 - i][k]) for k in range(2))
            )
            before = both[i - 1] if i else (zero, zero)
            shifted.append(
                tuple(jnp.where(low8, before[k], turned(both[i][k])) for k in range(2))
            )
        for a in range(4):
            tr, ti = summed([(grads[i], shifted[i - 2 * a]) for i in range(2 * a, 8)])
            lres[a, re] = tr
            lres[a, im] = ti

    over_bins(spec, multiply)

    def invert(n, carry):
        x = jnp.concatenate([flipped(lres[a], -1.0) for a in (2 * n, 2 * n + 1)], axis=1)
        out = apply(back_h, back_l, *split(x))
        low16 = low_lanes(16)
        for t in range(2):
            for k in range(8):
                x = out[32 * k : 32 * k + 16, 128 * t : 128 * t + 128]
                y = out[32 * k + 16 : 32 * k + 32, 128 * t : 128 * t + 128]
                m = 4 * n + 2 * t
                lags[m, k] = jnp.where(low16, turned(x), y).astype(BF)
                lags[m + 1, k] = jnp.where(low16, x, turned(y)).astype(BF)
        return carry

    lax.fori_loop(0, 2, invert, 0)


def stream_kernel(place, got, short, skip, whole, *refs):
    outs, (sa_pad, sv_pad, u_pad, x_pad, wide) = refs[:8], refs[8:]
    pair, _ = weights(place, short, skip)

    def keep(b, a, v):
        t = whole[b]
        u_pad[BLOCK * b : BLOCK * b + BLOCK] = turned(t) * v
        x_pad[BLOCK * b : BLOCK * b + BLOCK] = t * a

    shorten(got, pair, sa_pad, sv_pad, keep)
    u_pad[8 * BLOCK :] = jnp.zeros((8, 128), F32)
    x_pad[8 * BLOCK :] = jnp.zeros((8, 128), F32)
    w_u, w_x = pair(1, 0), pair(None, 2)
    low128 = low_lanes(128)
    for b in range(8):
        start = BLOCK * b
        y = sum(w_u[j] * u_pad[start + j : start + j + BLOCK] for j in range(3))
        wide[b, 0:BLOCK] = y.astype(BF)
        y = sum(w_x[j] * x_pad[start + j : start + j + BLOCK] for j in range(3))
        wide[b, BLOCK:] = jnp.where(low128, turned(y[:128]), y[128:]).astype(BF)
    for n in range(8):
        outs[n][...] = wide[place[0] ^ n]


def on_channels(kernel, name, inputs, in_shapes, outputs, scratch, cost):
    full = lambda *shape: pl.BlockSpec(shape, lambda n, p: (0,) * len(shape))
    return pl.pallas_call(
        kernel,
        grid_spec=pltpu.PrefetchScalarGridSpec(
            num_scalar_prefetch=1,
            grid=(1,),
            in_specs=[
                full(8, SENT_ROWS, 256),
                pl.BlockSpec((9, 128), lambda n, p: (0, p[0] // 2)),
                pl.BlockSpec((1, 128), lambda n, p: (0, p[0] // 2)),
            ]
            + [full(*shape) for shape in in_shapes],
            out_specs=[full(*shape) for shape, _ in outputs],
            scratch_shapes=[
                pltpu.VMEM(shape, dtype)
                for shape, dtype in [((8 + 8 * BLOCK, 128), F32)] * 2 + scratch
            ],
        ),
        out_shape=[jax.ShapeDtypeStruct(shape, dtype) for shape, dtype in outputs],
        cost_estimate=cost,
        name=name,
    )(*inputs)


TABLES = [(512, BLOCK), (512, BLOCK), (BLOCK, 512), (BLOCK, 512)]
BLOCKS = ((8, BLOCK, 128), F32)
BINS = ((8, 512, 128), F32)


def spent(flops):
    return pl.CostEstimate(flops=flops, bytes_accessed=3 * 10**6, transcendentals=0)


def conv(place, got, short, skip):
    inputs = (place, got, short, skip, *(jnp.asarray(t) for t in tables()))
    outputs = [((8, 64, 256), BF), BLOCKS]
    scratch = [BLOCKS, BLOCKS, BINS, BINS, BINS, BLOCKS]
    return on_channels(conv_kernel, "conv", inputs, TABLES, outputs, scratch, None)


def lag_sums(place, got, short, skip):
    inputs = (place, got, short, skip, *(jnp.asarray(t) for t in tables()))
    outputs = [((8, 8, 16, 128), BF)]
    scratch = [BLOCKS, BINS, ((4, 512, 128), F32)]
    cost = spent(2 * 10**9)
    return on_channels(lag_kernel, "lag_sums", inputs, TABLES, outputs, scratch, cost)[0]


def stream_grads(place, got, short, skip, whole):
    outputs = [((384, 128), BF)] * 8
    pad = ((8 * BLOCK + 8, 128), F32)
    scratch = [pad, pad, ((8, 384, 128), BF)]
    inputs = (place, got, short, skip, whole)
    cost = spent(10**9)
    return on_channels(
        stream_kernel, "stream_grads", inputs, [BLOCKS[0]], outputs, scratch, cost
    )


def mixed_kernel(got, mixed):
    low = low_lanes(64)
    for q in range(4):
        lanes = slice(128 * q, 128 * q + 128)
        for t in range(2):
            there = slice(128 * t, 128 * t + 128)
            a = got[2 * q, :, there].astype(F32)
            b = got[2 * q + 1, :, there].astype(F32)
            mixed[128 * t : 128 * t + 64, lanes] = jnp.where(low, a, turned(b)).astype(BF)
            mixed[128 * t + 64 : 128 * t + 128, lanes] = jnp.where(low, turned(a), b).astype(BF)


def unpack_mixed(got):
    return pl.pallas_call(
        mixed_kernel,
        out_shape=jax.ShapeDtypeStruct((BLOCK, 512), BF),
        name="unpack_mixed",
    )(got)


def grads_kernel(place, *refs):
    parts, grads = refs[:8], refs[8]
    low, low128 = low_lanes(BLOCK), low_lanes(128)
    even = place[0] % 2 == 0
    for n in range(4):
        lanes = pl.ds(pl.multiple_of(128 * ((place[0] // 2) ^ n), 128), 128)
        first, second = parts[2 * n][...].astype(F32), parts[2 * n + 1][...].astype(F32)
        a, b = jnp.where(even, first, second), jnp.where(even, second, first)
        grads[1, :, lanes] = jnp.where(low, a[:BLOCK], turned(b[:BLOCK])).astype(BF)
        grads[0, :, lanes] = jnp.where(low, turned(a[:BLOCK]), b[:BLOCK]).astype(BF)
        a, b = a[BLOCK:], b[BLOCK:]
        grads[2, 0:128, lanes] = jnp.where(low128, a, turned(b)).astype(BF)
        grads[2, 128:256, lanes] = jnp.where(low128, turned(a), b).astype(BF)


def unpack_grads(place, parts):
    full = lambda *shape: pl.BlockSpec(shape, lambda n, p: (0,) * len(shape))
    return pl.pallas_call(
        grads_kernel,
        grid_spec=pltpu.PrefetchScalarGridSpec(
            num_scalar_prefetch=1,
            grid=(1,),
            in_specs=[full(384, 128)] * 8,
            out_specs=full(3, BLOCK, 512),
        ),
        out_shape=jax.ShapeDtypeStruct((3, BLOCK, 512), BF),
        cost_estimate=pl.CostEstimate(flops=10**6, bytes_accessed=2 * 10**6, transcendentals=0),
        name="unpack_grads",
    )(place, *parts)


def partial_kernel(place, m00, m01, m10, m11, g00, g01, g10, g11, lags, lags_z, packed):
    def term(mixed, grad):
        return lax.dot_general(
            mixed[...], grad[...], (((0,), (0,)), ((), ())), preferred_element_type=F32
        )

    part = term(m00, g00) + term(m01, g01) + term(m10, g10) + term(m11, g11)
    part = part.astype(BF)
    for n in range(32):
        packed[n, :, 0:1024] = part[16 * n : 16 * n + 16]
        s, k = n % 8, n // 8
        lag = lags[s, k].astype(F32) + lags_z[s, k].astype(F32)
        packed[n, :, 1024:1152] = lag.astype(BF)


def partial(place, mixed, grad, grads, lags, lags_z):
    full = lambda *shape: pl.BlockSpec(shape, lambda n, p: (0,) * len(shape))
    return pl.pallas_call(
        partial_kernel,
        grid_spec=pltpu.PrefetchScalarGridSpec(
            num_scalar_prefetch=1,
            grid=(1,),
            in_specs=[full(BLOCK, 512)] * 4
            + [pl.BlockSpec((BLOCK, 1024), lambda n, p: (0, p[0]))]
            + [full(BLOCK, 1024)] * 3
            + [full(8, 4, 16, 128)] * 2,
            out_specs=full(32, 16, 1152),
        ),
        out_shape=jax.ShapeDtypeStruct((32, 16, 1152), BF),
        name="partial",
    )(place, *mixed, grad, *grads, lags, lags_z)


def reduce_kernel(scale, got, shared, lags):
    total = jnp.zeros((16, 1024), F32)
    for n in range(32):
        total = total + got[n, :, 0:1024].astype(F32)
    total = (total * scale).astype(BF)
    for n in range(64):
        shared[n] = total
    for s in range(8):
        lag = jnp.zeros((16, 128), F32)
        for k in range(4):
            lag = lag + got[8 * k + s, :, 1024:1152].astype(F32)
        lags[:, 128 * s : 128 * s + 128] = lag * scale


def reduce(got, scale):
    return pl.pallas_call(
        functools.partial(reduce_kernel, scale),
        out_shape=[
            jax.ShapeDtypeStruct((64, 16, 1024), BF),
            jax.ShapeDtypeStruct((16, 1024), F32),
        ],
        name="reduce",
    )(got)


def half_kernel(place, mine, *refs):
    grad_weight, wide, sems = refs[-3:]

    def copy(n):
        zh, zl, yh = n // 4, n // 2 % 2, n % 2
        rows = slice(128 * (2 * zh + yh), 128 * (2 * zh + yh) + 128)
        lanes = pl.ds(pl.multiple_of(2048 * place[0] + 1024 * zl, 1024), 1024)
        return pltpu.make_async_copy(wide.at[n], grad_weight.at[rows, lanes], sems.at[n])

    for n in range(8):
        for k in range(8):
            wide[n, 16 * k : 16 * k + 16] = mine[8 * n + k].astype(F32)
        copy(n).start()
    for n in range(8):
        copy(n).wait()


def write_half(half, rows, whole=None):
    more = [] if whole is None else [whole]
    return pl.pallas_call(
        half_kernel,
        grid_spec=pltpu.PrefetchScalarGridSpec(
            num_scalar_prefetch=1,
            grid=(1,),
            in_specs=[pl.BlockSpec((64, 16, 1024), lambda n, p: (0, 0, 0))]
            + [pl.BlockSpec(memory_space=pltpu.HBM)] * len(more),
            out_specs=pl.BlockSpec(memory_space=pltpu.HBM),
            scratch_shapes=[
                pltpu.VMEM((8, 128, 1024), F32),
                pltpu.SemaphoreType.DMA((8,)),
            ],
        ),
        out_shape=jax.ShapeDtypeStruct((512, 4096), F32),
        input_output_aliases={2: 0} if more else {},
        cost_estimate=pl.CostEstimate(flops=10**6, bytes_accessed=6 * 10**6, transcendentals=0),
        name="write_half",
    )(half, rows, *more)


def filter_kernel(place, *refs):
    grad_filter = refs[-1]
    low = low_lanes(16)
    for d in range(4):
        z = (place[0] + 4 - d) % 4
        for n in range(2):
            yh = place[1] if n == 0 else 1 - place[1]
            row = pl.multiple_of(32 * (2 * z + yh), 32)
            lags = refs[2 * d + n]
            for q in range(4):
                a = lags[:, 256 * q : 256 * q + 128].astype(F32)
                b = lags[:, 256 * q + 128 : 256 * q + 256].astype(F32)
                lanes = slice(128 * q, 128 * q + 128)
                grad_filter[pl.ds(row, 16), lanes] = jnp.where(low, a, turned(b))
                grad_filter[pl.ds(row + 16, 16), lanes] = jnp.where(low, turned(a), b)


def write_filter(place, lags):
    full = lambda *shape: pl.BlockSpec(shape, lambda n, p: (0,) * len(shape))
    return pl.pallas_call(
        filter_kernel,
        grid_spec=pltpu.PrefetchScalarGridSpec(
            num_scalar_prefetch=1,
            grid=(1,),
            in_specs=[full(16, 1024)] * 8,
            out_specs=full(BLOCK, 512),
        ),
        out_shape=jax.ShapeDtypeStruct((BLOCK, 512), F32),
        cost_estimate=pl.CostEstimate(flops=10**6, bytes_accessed=2 * 10**6, transcendentals=0),
        name="write_filter",
    )(place, *lags)


def exchange(x, axes):
    return lax.all_to_all(x, axes, 0, 0, tiled=True)


def across(x):
    return lax.ppermute(x, "c", [(0, 1), (1, 0)])


def above(x):
    return lax.ppermute(x, "zl", [(0, 1), (1, 0)])


def opposite(x):
    return lax.ppermute(x, ("zl", "c"), [(n, 3 - n) for n in range(4)])


def gathered(lags):
    pair = (lags, lax.ppermute(lags, "yh", [(0, 1), (1, 0)]))
    out = list(pair)
    for d in range(1, 4):
        route = [(n, (n + d) % 4) for n in range(4)]
        out += [lax.ppermute(part, ("zh", "zl"), route) for part in pair]
    return out


def on_device(streams, short_filter, long_filter, skip_gain, out_weight, out_grad):
    scale = 1.0 / math.sqrt(16 * 2048)
    core = lax.axis_index("c").astype(jnp.int32)
    side = lax.axis_index("zl").astype(jnp.int32)
    seq = lax.axis_index(SEQ).astype(jnp.int32)
    grad = out_grad[0]

    def quarter(c, z):
        return lax.dynamic_slice(grad, (0, 1024 * (2 * c + z)), (BLOCK, 1024))

    grads = (
        above(quarter(core, 1 - side)),
        across(quarter(1 - core, side)),
        opposite(quarter(1 - core, 1 - side)),
    )
    got = exchange(pack(streams[:, 0], grad, out_weight, long_filter), SEQ)
    channels = (seq[None], got, short_filter.reshape(9, 512), skip_gain.reshape(1, 512))
    sent, whole = conv(*channels)
    sent, whole, got, grads = lax.optimization_barrier((sent, whole, got, grads))
    channels = (channels[0], got) + channels[2:]
    lags = lag_sums(*channels).reshape(8, 2, 2, 2, 16, 128)

    def of_side(z):
        return lax.dynamic_index_in_dim(lags, z, 2, False).reshape(8, 4, 16, 128)

    lags_own, lags_z = of_side(side), above(of_side(1 - side))
    back = exchange(sent, SEQ)
    back, lags_own = lax.optimization_barrier((back, lags_own))
    m00 = unpack_mixed(back)
    m01, m10 = above(m00), across(m00)
    mixed = (m00, m01, m10, across(m01))
    part = partial((2 * core + side)[None], mixed, grad, grads, lags_own, lags_z)
    part, m00, whole, got = lax.optimization_barrier((part, m00, whole, got))
    part = exchange(part, MOST)
    channels = (channels[0], got) + channels[2:]
    parts = stream_grads(*channels, whole)
    parts = [parts[0]] + [
        lax.ppermute(parts[n], SEQ, [(i, i ^ n) for i in range(8)]) for n in range(1, 8)
    ]
    part, parts, m00 = lax.optimization_barrier((part, parts, m00))
    rows, lags = reduce(part, scale)
    rows, lags, parts, m00 = lax.optimization_barrier((rows, lags, parts, m00))
    mine = exchange(rows, CHIPS)
    layer_out = jnp.dot(m00, out_weight, preferred_element_type=F32).astype(BF)
    grad_streams = unpack_grads(seq[None], parts)
    lags = (lags + across(lags)).astype(BF)
    place = jnp.stack([lax.axis_index(("zh", "zl")), lax.axis_index("yh")]).astype(jnp.int32)
    grad_filter = write_filter(place, gathered(lags))
    mine, grad_filter, layer_out, grad_streams = lax.optimization_barrier(
        (mine, grad_filter, layer_out, grad_streams)
    )
    theirs = across(mine)
    grad_weight = write_half(core[None], mine)
    grad_weight = write_half(1 - core[None], theirs, grad_weight)
    return layer_out[None], grad_streams[:, None], grad_filter, grad_weight


def solution(mesh):
    fine = Mesh(
        mesh.devices.reshape(2, 2, 2, 2, 4, 2), ("zh", "zl", "yh", "c", "x", "yl")
    )
    dp = ("zh", "zl", "yh", "c")
    placed = (P(None, dp, SEQ, None), P(), P(SEQ, None), P(), P(), P(dp, SEQ, None))
    return jax.shard_map(
        on_device,
        mesh=fine,
        in_specs=placed,
        out_specs=(P(dp, SEQ, None), P(None, dp, SEQ, None), P(SEQ, None), P()),
        check_vma=False,
    )
```

```python
import functools
import math

import jax
import jax.numpy as jnp
import numpy as np
from jax import lax
from jax.experimental import pallas as pl
from jax.experimental.pallas import tpu as pltpu
from jax.sharding import Mesh, PartitionSpec as P

BF = jnp.bfloat16
F32 = jnp.float32
BLOCK = 256
HALF = 64
SENT_ROWS = BLOCK + 64
SEQ = ("x", "yl")
MOST = ("zh", "yh") + SEQ
CHIPS = ("zh", "zl", "yh") + SEQ


@functools.lru_cache(maxsize=None)
def tables():
    order = np.concatenate([np.arange(0, BLOCK, 2), np.arange(1, BLOCK, 2)])
    angle = np.pi * ((2 * order[:, None] + 1) * np.arange(BLOCK)[None, :] % 1024) / 512.0
    ahead = np.concatenate([np.cos(angle), -np.sin(angle)], axis=0)
    back = ahead.T / BLOCK

    def two(table):
        table = table.astype(np.float32)
        high = table.astype(jnp.bfloat16)
        return high, (table - high.astype(np.float32)).astype(jnp.bfloat16)

    return two(ahead) + two(back)


def mm(a, b):
    return jnp.dot(a, b, preferred_element_type=F32)


def low_lanes(rows):
    return lax.broadcasted_iota(jnp.int32, (rows, 128), 1) < HALF


def turned(x):
    return pltpu.roll(x, HALF, 1)


def pack_kernel(streams, out_grad, weight, filt, packed, total):
    step = pl.program_id(0)
    low = low_lanes(BLOCK)

    @pl.when(step == 0)
    def _():
        total[...] = jnp.zeros_like(total)

    total[...] += lax.dot_general(
        out_grad[...], weight[...], (((1,), (1,)), ((), ())), preferred_element_type=F32
    )

    def put(q, tile, a, b):
        lanes = slice(128 * tile, 128 * tile + 128)
        packed[2 * q, 0:BLOCK, lanes] = jnp.where(low, a, turned(b)).astype(BF)
        packed[2 * q + 1, 0:BLOCK, lanes] = jnp.where(low, turned(a), b).astype(BF)

    for q in range(4):
        lanes = slice(128 * q, 128 * q + 128)

        @pl.when(step == q)
        def _(q=q, lanes=lanes):
            put(q, 0, streams[0, :, lanes].astype(F32), streams[1, :, lanes].astype(F32))
            low64 = low_lanes(64)
            for n in range(2):
                a = filt[128 * n : 128 * n + 64, lanes]
                b = filt[128 * n + 64 : 128 * n + 128, lanes]
                there = slice(128 * n, 128 * n + 128)
                packed[2 * q, BLOCK:, there] = jnp.where(low64, a, turned(b)).astype(BF)
                packed[2 * q + 1, BLOCK:, there] = jnp.where(low64, turned(a), b).astype(BF)

    @pl.when(step == pl.num_programs(0) - 1)
    def _():
        for q in range(4):
            lanes = slice(128 * q, 128 * q + 128)
            put(q, 1, streams[2, :, lanes].astype(F32), total[:, lanes])


def pack(streams, out_grad, weight, filt):
    steps = 4
    wide = out_grad.shape[1] // steps
    return pl.pallas_call(
        pack_kernel,
        grid=(steps,),
        in_specs=[
            pl.BlockSpec((3, BLOCK, 512), lambda k: (0, 0, 0)),
            pl.BlockSpec((BLOCK, wide), lambda k: (0, k)),
            pl.BlockSpec((512, wide), lambda k: (0, k)),
            pl.BlockSpec((BLOCK, 512), lambda k: (0, 0)),
        ],
        out_specs=pl.BlockSpec((8, SENT_ROWS, 256), lambda k: (0, 0, 0)),
        out_shape=jax.ShapeDtypeStruct((8, SENT_ROWS, 256), BF),
        scratch_shapes=[pltpu.VMEM((BLOCK, 512), F32)],
        name="pack",
    )(streams, out_grad, weight, filt)


def split(x):
    high = x.astype(BF)
    return high, (x - high.astype(F32)).astype(BF)


def apply(table_h, table_l, high, rest):
    return mm(table_h[...], high) + mm(table_h[...], rest) + mm(table_l[...], high)


def weights(place, short, skip):
    low1 = low_lanes(1)
    odd = place[0] % 2 == 1
    taps = short[...]
    taps = jnp.where(odd, turned(taps), taps)
    taps_up = turned(taps)
    gain = skip[...]
    gain = jnp.where(odd, turned(gain), gain)
    gain = jnp.where(low1, gain, turned(gain))

    def pair(first, second):
        def row(table, i, j):
            if i is None:
                return jnp.full((1, 128), 1.0 if j == 0 else 0.0, F32)
            return table[3 * i + j : 3 * i + j + 1]

        return [
            jnp.where(low1, row(taps, first, j), row(taps_up, second, j)) for j in range(3)
        ]

    return pair, gain


def shorten(got, pair, sa_pad, sv_pad, use):
    w_a, w_v = pair(0, 1), pair(2, None)
    sa_pad[0:8] = jnp.zeros((8, 128), F32)
    sv_pad[0:8] = jnp.zeros((8, 128), F32)

    def load(b, carry):
        rows = pl.ds(pl.multiple_of(8 + BLOCK * b, 8), BLOCK)
        sa_pad[rows] = got[b, 0:BLOCK, 0:128].astype(F32)
        sv_pad[rows] = got[b, 0:BLOCK, 128:256].astype(F32)
        return carry

    lax.fori_loop(0, 8, load, 0)
    for b in range(8):
        start = 8 + BLOCK * b
        a = sum(w_a[j] * sa_pad[start - j : start - j + BLOCK] for j in range(3))
        v = sum(w_v[j] * sv_pad[start - j : start - j + BLOCK] for j in range(3))
        use(b, a, v)


def spectra(prod, ahead_h, ahead_l, spec):
    low = low_lanes(BLOCK)
    sigma = jnp.where(low, 1.0, -1.0)

    def transform(n, carry):
        x = jnp.concatenate(
            [jnp.where(low, prod[b], prod[7 - b]) for b in (2 * n, 2 * n + 1)], axis=1
        )
        out = apply(ahead_h, ahead_l, *split(x))
        for t in range(2):
            spec[2 * n + t, 0:BLOCK] = out[:BLOCK, 128 * t : 128 * t + 128]
            spec[2 * n + t, BLOCK:] = out[BLOCK:, 128 * t : 128 * t + 128] * sigma
        return carry

    lax.fori_loop(0, 4, transform, 0)


def over_bins(spec, use):
    for sign, base in ((1.0, 0), (-1.0, 128)):

        def step(n, carry, sign=sign, base=base):
            re = pl.ds(pl.multiple_of(base + 8 * n, 8), 8)
            im = pl.ds(pl.multiple_of(BLOCK + base + 8 * n, 8), 8)
            own = [(spec[j, re], spec[j, im]) for j in range(8)]
            both = [own[0]]
            for j in range(1, 8):
                both.append(
                    (own[j][0] - sign * own[j - 1][1], own[j][1] + sign * own[j - 1][0])
                )
            use(re, im, own, both)
            return carry

        lax.fori_loop(0, 16, step, 0)


def summed(pairs):
    first = True
    for (ar, ai), (br, bi) in pairs:
        pr = ar * br - ai * bi
        pi = ar * bi + ai * br
        tr, ti = (pr, pi) if first else (tr + pr, ti + pi)
        first = False
    return tr, ti


def flipped(x, sign):
    return jnp.concatenate([x[0:BLOCK], x[BLOCK:] * sign], axis=0)


def conv_kernel(
    place, got, short, skip, ahead_h, ahead_l, back_h, back_l,
    sent,
    sa_pad, sv_pad, sa, sv, prod, spec, fspec, res, time, u_pad, x_pad,
):
    low = low_lanes(BLOCK)
    low64 = low_lanes(64)
    sigma = jnp.where(low, 1.0, -1.0)
    pair, gain = weights(place, short, skip)

    def filters(n, carry):
        def blocks(b):
            parts = []
            for t in range(2):
                x = got[b, BLOCK:, 128 * t : 128 * t + 128].astype(F32)
                y = got[b + 1, BLOCK:, 128 * t : 128 * t + 128].astype(F32)
                parts.append(jnp.where(low64, x, turned(y)))
                parts.append(jnp.where(low64, turned(x), y))
            return jnp.concatenate(parts, axis=0).astype(BF)

        f = jnp.concatenate([blocks(4 * n), blocks(4 * n + 2)], axis=1)
        out = mm(ahead_h[...], f) + mm(ahead_l[...], f)
        low512 = low_lanes(512)
        for t in range(2):
            x = out[:, 128 * t : 128 * t + 128]
            y = turned(x)
            fspec[4 * n + 2 * t] = jnp.where(low512, x, y)
            fspec[4 * n + 2 * t + 1] = jnp.where(low512, y, x)
        return carry

    lax.fori_loop(0, 2, filters, 0)

    def keep(b, a, v):
        sa[b] = a
        sv[b] = v
        prod[b] = turned(a) * v

    shorten(got, pair, sa_pad, sv_pad, keep)
    spectra(prod, ahead_h, ahead_l, spec)

    def multiply(re, im, own, both):
        filt = [(fspec[m, re], fspec[m, im]) for m in range(8)]
        for i in range(8):
            tr, ti = summed([(filt[m], both[i - m]) for m in range(i + 1)])
            res[i, re] = tr
            res[i, im] = ti

    over_bins(spec, multiply)

    def invert(n, carry):
        x = jnp.concatenate([flipped(res[b], sigma) for b in (2 * n, 2 * n + 1)], axis=1)
        out = apply(back_h, back_l, *split(x))
        time[2 * n] = out[:, :128]
        time[2 * n + 1] = out[:, 128:]
        return carry

    lax.fori_loop(0, 4, invert, 0)

    def gate(b, carry):
        t = jnp.where(low, time[b], time[7 - b]) + gain * prod[b]
        rows = pl.ds(pl.multiple_of(BLOCK * b, 8), BLOCK)
        u_pad[rows] = turned(t) * sv[b]
        x_pad[rows] = t * sa[b]
        return carry

    lax.fori_loop(0, 8, gate, 0)
    u_pad[8 * BLOCK :] = jnp.zeros((8, 128), F32)
    x_pad[8 * BLOCK :] = jnp.zeros((8, 128), F32)
    w_u, w_x = pair(1, 0), pair(None, 2)
    for b in range(8):
        start = BLOCK * b
        y = sum(w_u[j] * u_pad[start + j : start + j + BLOCK] for j in range(3))
        sent[b, :, 0:128] = y.astype(BF)
        y = sum(w_x[j] * x_pad[start + j : start + j + BLOCK] for j in range(3))
        sent[b, :, 128:256] = y.astype(BF)


def lag_kernel(
    place, got, short, skip, ahead_h, ahead_l, back_h, back_l,
    lags,
    sa_pad, sv_pad, prod, spec, lres,
):
    pair, _ = weights(place, short, skip)

    def keep(b, a, v):
        prod[b] = turned(a) * v

    shorten(got, pair, sa_pad, sv_pad, keep)
    spectra(prod, ahead_h, ahead_l, spec)
    zero = jnp.zeros((8, 128), F32)
    low8 = low_lanes(8)

    def multiply(re, im, own, both):
        grads, shifted = [], []
        for i in range(8):
            grads.append(
                tuple(jnp.where(low8, turned(own[7 - i][k]), own[7 - i][k]) for k in range(2))
            )
            before = both[i - 1] if i else (zero, zero)
            shifted.append(
                tuple(jnp.where(low8, before[k], turned(both[i][k])) for k in range(2))
            )
        for a in range(4):
            tr, ti = summed([(grads[i], shifted[i - 2 * a]) for i in range(2 * a, 8)])
            lres[a, re] = tr
            lres[a, im] = ti

    over_bins(spec, multiply)

    def invert(n, carry):
        x = jnp.concatenate([flipped(lres[a], -1.0) for a in (2 * n, 2 * n + 1)], axis=1)
        out = apply(back_h, back_l, *split(x))
        low16 = low_lanes(16)
        for t in range(2):
            for k in range(8):
                x = out[32 * k : 32 * k + 16, 128 * t : 128 * t + 128]
                y = out[32 * k + 16 : 32 * k + 32, 128 * t : 128 * t + 128]
                m = 4 * n + 2 * t
                lags[m, k] = jnp.where(low16, turned(x), y).astype(BF)
                lags[m + 1, k] = jnp.where(low16, x, turned(y)).astype(BF)
        return carry

    lax.fori_loop(0, 2, invert, 0)


def on_channels(kernel, name, inputs, in_shapes, outputs, scratch, cost):
    full = lambda *shape: pl.BlockSpec(shape, lambda n, p: (0,) * len(shape))
    return pl.pallas_call(
        kernel,
        grid_spec=pltpu.PrefetchScalarGridSpec(
            num_scalar_prefetch=1,
            grid=(1,),
            in_specs=[
                full(8, SENT_ROWS, 256),
                pl.BlockSpec((9, 128), lambda n, p: (0, p[0] // 2)),
                pl.BlockSpec((1, 128), lambda n, p: (0, p[0] // 2)),
            ]
            + [full(*shape) for shape in in_shapes],
            out_specs=[full(*shape) for shape, _ in outputs],
            scratch_shapes=[
                pltpu.VMEM(shape, dtype)
                for shape, dtype in [((8 + 8 * BLOCK, 128), F32)] * 2 + scratch
            ],
        ),
        out_shape=[jax.ShapeDtypeStruct(shape, dtype) for shape, dtype in outputs],
        cost_estimate=cost,
        name=name,
    )(*inputs)


TABLES = [(512, BLOCK), (512, BLOCK), (BLOCK, 512), (BLOCK, 512)]
BLOCKS = ((8, BLOCK, 128), F32)
BINS = ((8, 512, 128), F32)


def spent(flops):
    return pl.CostEstimate(flops=flops, bytes_accessed=3 * 10**6, transcendentals=0)


def conv(place, got, short, skip):
    inputs = (place, got, short, skip, *(jnp.asarray(t) for t in tables()))
    outputs = [((8, BLOCK, 256), BF)]
    pad = ((8 * BLOCK + 8, 128), F32)
    scratch = [BLOCKS, BLOCKS, BLOCKS, BINS, BINS, BINS, BLOCKS, pad, pad]
    return on_channels(conv_kernel, "conv", inputs, TABLES, outputs, scratch, None)[0]


def lag_sums(place, got, short, skip):
    inputs = (place, got, short, skip, *(jnp.asarray(t) for t in tables()))
    outputs = [((8, 8, 16, 128), BF)]
    scratch = [BLOCKS, BINS, ((4, 512, 128), F32)]
    cost = spent(2 * 10**9)
    return on_channels(lag_kernel, "lag_sums", inputs, TABLES, outputs, scratch, cost)[0]


def spread(got, there, first, second, low):
    for q in range(4):
        lanes = slice(128 * q, 128 * q + 128)
        a = got[2 * q, 0:BLOCK, there].astype(F32)
        b = got[2 * q + 1, 0:BLOCK, there].astype(F32)
        if first is not None:
            first[:, lanes] = jnp.where(low, a, turned(b)).astype(BF)
        if second is not None:
            second[:, lanes] = jnp.where(low, turned(a), b).astype(BF)


def mixed_kernel(got, mixed):
    spread(got, slice(0, 128), mixed, None, low_lanes(BLOCK))


def unpack_mixed(got):
    return pl.pallas_call(
        mixed_kernel,
        grid=(1,),
        in_specs=[pl.BlockSpec((8, BLOCK, 128), lambda n: (0, 0, 1))],
        out_specs=pl.BlockSpec((BLOCK, 512), lambda n: (0, 0)),
        out_shape=jax.ShapeDtypeStruct((BLOCK, 512), BF),
        name="unpack_mixed",
    )(got)


def grads_kernel(got, grads):
    low = low_lanes(BLOCK)
    spread(got, slice(0, 128), grads.at[1], grads.at[0], low)
    spread(got, slice(128, 256), None, grads.at[2], low)


def unpack_grads(got):
    return pl.pallas_call(
        grads_kernel,
        out_shape=jax.ShapeDtypeStruct((3, BLOCK, 512), BF),
        cost_estimate=pl.CostEstimate(flops=10**6, bytes_accessed=2 * 10**6, transcendentals=0),
        name="unpack_grads",
    )(got)


def partial_kernel(place, m00, m01, m10, m11, g00, g01, g10, g11, lags, lags_z, packed):
    def term(mixed, grad):
        return lax.dot_general(
            mixed[...], grad[...], (((0,), (0,)), ((), ())), preferred_element_type=F32
        )

    part = term(m00, g00) + term(m01, g01) + term(m10, g10) + term(m11, g11)
    part = part.astype(BF)
    for n in range(32):
        packed[n, :, 0:1024] = part[16 * n : 16 * n + 16]
        s, k = n % 8, n // 8
        lag = lags[s, k].astype(F32) + lags_z[s, k].astype(F32)
        packed[n, :, 1024:1152] = lag.astype(BF)


def partial(place, mixed, grad, grads, lags, lags_z):
    full = lambda *shape: pl.BlockSpec(shape, lambda n, p: (0,) * len(shape))
    return pl.pallas_call(
        partial_kernel,
        grid_spec=pltpu.PrefetchScalarGridSpec(
            num_scalar_prefetch=1,
            grid=(1,),
            in_specs=[full(BLOCK, 512)] * 4
            + [pl.BlockSpec((BLOCK, 1024), lambda n, p: (0, p[0]))]
            + [full(BLOCK, 1024)] * 3
            + [full(8, 4, 16, 128)] * 2,
            out_specs=full(32, 16, 1152),
        ),
        out_shape=jax.ShapeDtypeStruct((32, 16, 1152), BF),
        name="partial",
    )(place, *mixed, grad, *grads, lags, lags_z)


def reduce_kernel(scale, got, shared, lags):
    total = jnp.zeros((16, 1024), F32)
    for n in range(32):
        total = total + got[n, :, 0:1024].astype(F32)
    total = (total * scale).astype(BF)
    for n in range(64):
        shared[n] = total
    for s in range(8):
        lag = jnp.zeros((16, 128), F32)
        for k in range(4):
            lag = lag + got[8 * k + s, :, 1024:1152].astype(F32)
        lags[:, 128 * s : 128 * s + 128] = lag * scale


def reduce(got, scale):
    return pl.pallas_call(
        functools.partial(reduce_kernel, scale),
        out_shape=[
            jax.ShapeDtypeStruct((64, 16, 1024), BF),
            jax.ShapeDtypeStruct((16, 1024), F32),
        ],
        name="reduce",
    )(got)


def half_kernel(place, mine, *refs):
    grad_weight, wide, sems = refs[-3:]

    def copy(n):
        zh, zl, yh = n // 4, n // 2 % 2, n % 2
        rows = slice(128 * (2 * zh + yh), 128 * (2 * zh + yh) + 128)
        lanes = pl.ds(pl.multiple_of(2048 * place[0] + 1024 * zl, 1024), 1024)
        return pltpu.make_async_copy(wide.at[n], grad_weight.at[rows, lanes], sems.at[n])

    for n in range(8):
        for k in range(8):
            wide[n, 16 * k : 16 * k + 16] = mine[8 * n + k].astype(F32)
        copy(n).start()
    for n in range(8):
        copy(n).wait()


def write_half(half, rows, whole=None):
    more = [] if whole is None else [whole]
    return pl.pallas_call(
        half_kernel,
        grid_spec=pltpu.PrefetchScalarGridSpec(
            num_scalar_prefetch=1,
            grid=(1,),
            in_specs=[pl.BlockSpec((64, 16, 1024), lambda n, p: (0, 0, 0))]
            + [pl.BlockSpec(memory_space=pltpu.HBM)] * len(more),
            out_specs=pl.BlockSpec(memory_space=pltpu.HBM),
            scratch_shapes=[
                pltpu.VMEM((8, 128, 1024), F32),
                pltpu.SemaphoreType.DMA((8,)),
            ],
        ),
        out_shape=jax.ShapeDtypeStruct((512, 4096), F32),
        input_output_aliases={2: 0} if more else {},
        cost_estimate=pl.CostEstimate(flops=10**6, bytes_accessed=6 * 10**6, transcendentals=0),
        name="write_half",
    )(half, rows, *more)


def filter_kernel(place, *refs):
    grad_filter = refs[-1]
    low = low_lanes(16)
    for d in range(4):
        z = (place[0] + 4 - d) % 4
        for n in range(2):
            yh = place[1] if n == 0 else 1 - place[1]
            row = pl.multiple_of(32 * (2 * z + yh), 32)
            lags = refs[2 * d + n]
            for q in range(4):
                a = lags[:, 256 * q : 256 * q + 128].astype(F32)
                b = lags[:, 256 * q + 128 : 256 * q + 256].astype(F32)
                lanes = slice(128 * q, 128 * q + 128)
                grad_filter[pl.ds(row, 16), lanes] = jnp.where(low, a, turned(b))
                grad_filter[pl.ds(row + 16, 16), lanes] = jnp.where(low, turned(a), b)


def write_filter(place, lags):
    full = lambda *shape: pl.BlockSpec(shape, lambda n, p: (0,) * len(shape))
    return pl.pallas_call(
        filter_kernel,
        grid_spec=pltpu.PrefetchScalarGridSpec(
            num_scalar_prefetch=1,
            grid=(1,),
            in_specs=[full(16, 1024)] * 8,
            out_specs=full(BLOCK, 512),
        ),
        out_shape=jax.ShapeDtypeStruct((BLOCK, 512), F32),
        cost_estimate=pl.CostEstimate(flops=10**6, bytes_accessed=2 * 10**6, transcendentals=0),
        name="write_filter",
    )(place, *lags)


def exchange(x, axes):
    return lax.all_to_all(x, axes, 0, 0, tiled=True)


def across(x):
    return lax.ppermute(x, "c", [(0, 1), (1, 0)])


def above(x):
    return lax.ppermute(x, "zl", [(0, 1), (1, 0)])


def opposite(x):
    return lax.ppermute(x, ("zl", "c"), [(n, 3 - n) for n in range(4)])


def gathered(lags):
    pair = (lags, lax.ppermute(lags, "yh", [(0, 1), (1, 0)]))
    out = list(pair)
    for d in range(1, 4):
        route = [(n, (n + d) % 4) for n in range(4)]
        out += [lax.ppermute(part, ("zh", "zl"), route) for part in pair]
    return out


def on_device(streams, short_filter, long_filter, skip_gain, out_weight, out_grad):
    scale = 1.0 / math.sqrt(16 * 2048)
    core = lax.axis_index("c").astype(jnp.int32)
    side = lax.axis_index("zl").astype(jnp.int32)
    seq = lax.axis_index(SEQ).astype(jnp.int32)
    grad = out_grad[0]

    def quarter(c, z):
        return lax.dynamic_slice(grad, (0, 1024 * (2 * c + z)), (BLOCK, 1024))

    grads = (
        above(quarter(core, 1 - side)),
        across(quarter(1 - core, side)),
        opposite(quarter(1 - core, 1 - side)),
    )
    got = exchange(pack(streams[:, 0], grad, out_weight, long_filter), SEQ)
    channels = (seq[None], got, short_filter.reshape(9, 512), skip_gain.reshape(1, 512))
    sent = conv(*channels)
    sent, got, grads = lax.optimization_barrier((sent, got, grads))
    channels = (channels[0], got) + channels[2:]
    lags = lag_sums(*channels).reshape(8, 2, 2, 2, 16, 128)

    def of_side(z):
        return lax.dynamic_index_in_dim(lags, z, 2, False).reshape(8, 4, 16, 128)

    lags_own, lags_z = of_side(side), above(of_side(1 - side))
    back = exchange(sent, SEQ)
    back, lags_own, lags_z = lax.optimization_barrier((back, lags_own, lags_z))
    m00 = unpack_mixed(back)
    m01, m10 = above(m00), across(m00)
    mixed = (m00, m01, m10, across(m01))
    part = partial((2 * core + side)[None], mixed, grad, grads, lags_own, lags_z)
    part, m00, back = lax.optimization_barrier((part, m00, back))
    part = exchange(part, MOST)
    layer_out = jnp.dot(m00, out_weight, preferred_element_type=F32).astype(BF)
    grad_streams = unpack_grads(back)
    part, layer_out, grad_streams = lax.optimization_barrier((part, layer_out, grad_streams))
    rows, lags = reduce(part, scale)
    rows, lags = lax.optimization_barrier((rows, lags))
    mine = exchange(rows, CHIPS)
    lags = (lags + across(lags)).astype(BF)
    place = jnp.stack([lax.axis_index(("zh", "zl")), lax.axis_index("yh")]).astype(jnp.int32)
    grad_filter = write_filter(place, gathered(lags))
    mine, grad_filter = lax.optimization_barrier((mine, grad_filter))
    theirs = across(mine)
    grad_weight = write_half(core[None], mine)
    grad_weight = write_half(1 - core[None], theirs, grad_weight)
    return layer_out[None], grad_streams[:, None], grad_filter, grad_weight


def solution(mesh):
    fine = Mesh(
        mesh.devices.reshape(2, 2, 2, 2, 4, 2), ("zh", "zl", "yh", "c", "x", "yl")
    )
    dp = ("zh", "zl", "yh", "c")
    placed = (P(None, dp, SEQ, None), P(), P(SEQ, None), P(), P(), P(dp, SEQ, None))
    return jax.shard_map(
        on_device,
        mesh=fine,
        in_specs=placed,
        out_specs=(P(dp, SEQ, None), P(None, dp, SEQ, None), P(SEQ, None), P()),
        check_vma=False,
    )
```

```python
import functools
import math

import jax
import jax.numpy as jnp
import numpy as np
from jax import lax
from jax.experimental import pallas as pl
from jax.experimental.pallas import tpu as pltpu
from jax.sharding import Mesh, PartitionSpec as P

BF = jnp.bfloat16
F32 = jnp.float32
BLOCK = 256
HALF = 64
SEQ = ("x", "yl")
MOST = ("zh", "yh") + SEQ
CHIPS = ("zh", "zl", "yh") + SEQ


@functools.lru_cache(maxsize=None)
def tables():
    order = np.concatenate([np.arange(0, BLOCK, 2), np.arange(1, BLOCK, 2)])
    angle = np.pi * ((2 * order[:, None] + 1) * np.arange(BLOCK)[None, :] % 1024) / 512.0
    ahead = np.concatenate([np.cos(angle), -np.sin(angle)], axis=0)
    back = ahead.T / BLOCK

    def two(table):
        table = table.astype(np.float32)
        high = table.astype(jnp.bfloat16)
        return high, (table - high.astype(np.float32)).astype(jnp.bfloat16)

    return two(ahead) + two(back)


def mm(a, b):
    return jnp.dot(a, b, preferred_element_type=F32)


def low_lanes(rows):
    return lax.broadcasted_iota(jnp.int32, (rows, 128), 1) < HALF


def turned(x):
    return pltpu.roll(x, HALF, 1)


def grad_kernel(out_grad, weight, total):
    @pl.when(pl.program_id(0) == 0)
    def _():
        total[...] = jnp.zeros_like(total)

    total[...] += lax.dot_general(
        out_grad[...], weight[...], (((1,), (1,)), ((), ())), preferred_element_type=F32
    )


def grad_of_mixed(out_grad, weight):
    steps = 4
    wide = out_grad.shape[1] // steps
    return pl.pallas_call(
        grad_kernel,
        grid=(steps,),
        in_specs=[
            pl.BlockSpec((BLOCK, wide), lambda k: (0, k)),
            pl.BlockSpec((512, wide), lambda k: (0, k)),
        ],
        out_specs=pl.BlockSpec((BLOCK, 512), lambda k: (0, 0)),
        out_shape=jax.ShapeDtypeStruct((BLOCK, 512), F32),
        cost_estimate=pl.CostEstimate(flops=10**9, bytes_accessed=7 * 10**6, transcendentals=0),
        name="grad_of_mixed",
    )(out_grad, weight)


def pack_kernel(streams, edge, grad, filt, short, packed, gate_out, pad):
    low = low_lanes(BLOCK)
    pad[0:8] = edge[...].astype(F32)
    pad[8:] = streams[0].astype(F32)
    for q in range(4):
        lanes = slice(128 * q, 128 * q + 128)
        gate = sum(
            short[j : j + 1, lanes] * pad[8 - j : 8 - j + BLOCK, lanes] for j in range(3)
        )
        gate_out[:, lanes] = gate
        pairs = (
            (streams[1, :, lanes].astype(F32), streams[2, :, lanes].astype(F32)),
            (grad[:, lanes] * gate, filt[:, lanes]),
        )
        for n, (a, b) in enumerate(pairs):
            there = slice(128 * n, 128 * n + 128)
            packed[2 * q, :, there] = jnp.where(low, a, turned(b)).astype(BF)
            packed[2 * q + 1, :, there] = jnp.where(low, turned(a), b).astype(BF)


def pack(streams, edge, grad, filt, short):
    return pl.pallas_call(
        pack_kernel,
        out_shape=[
            jax.ShapeDtypeStruct((8, BLOCK, 256), BF),
            jax.ShapeDtypeStruct((BLOCK, 512), F32),
        ],
        scratch_shapes=[pltpu.VMEM((8 + BLOCK, 512), F32)],
        name="pack",
    )(streams, edge, grad, filt, short)


def split(x):
    high = x.astype(BF)
    return high, (x - high.astype(F32)).astype(BF)


def apply(table_h, table_l, high, rest):
    return mm(table_h[...], high) + mm(table_h[...], rest) + mm(table_l[...], high)


def weights(place, short, skip):
    low1 = low_lanes(1)
    odd = place[0] % 2 == 1
    taps = short[...]
    taps = jnp.where(odd, turned(taps), taps)
    taps_up = turned(taps)
    gain = skip[...]
    gain = jnp.where(odd, turned(gain), gain)
    gain = jnp.where(low1, gain, turned(gain))

    def pair(first, second):
        def row(table, i, j):
            if i is None:
                return jnp.full((1, 128), 1.0 if j == 0 else 0.0, F32)
            return table[3 * i + j : 3 * i + j + 1]

        return [
            jnp.where(low1, row(taps, first, j), row(taps_up, second, j)) for j in range(3)
        ]

    return pair, gain


def prepare(got, pair, pad, prod, gates=None):
    taps = pair(1, 2)
    low = low_lanes(BLOCK)
    pad[0:8] = jnp.zeros((8, 128), F32)

    def load(b, carry):
        rows = pl.ds(pl.multiple_of(8 + BLOCK * b, 8), BLOCK)
        pad[rows] = got[b, :, 0:128].astype(F32)
        return carry

    lax.fori_loop(0, 8, load, 0)
    for b in range(8):
        start = 8 + BLOCK * b
        s = sum(taps[j] * pad[start - j : start - j + BLOCK] for j in range(3))
        if gates is not None:
            gates[b] = s
        prod[b] = jnp.where(low, s * turned(s), turned(got[b, :, 128:256].astype(F32)))


def spectra(prod, ahead_h, ahead_l, spec):
    low = low_lanes(BLOCK)
    sigma = jnp.where(low, 1.0, -1.0)

    def transform(n, carry):
        x = jnp.concatenate(
            [jnp.where(low, prod[b], prod[7 - b]) for b in (2 * n, 2 * n + 1)], axis=1
        )
        out = apply(ahead_h, ahead_l, *split(x))
        for t in range(2):
            spec[2 * n + t, 0:BLOCK] = out[:BLOCK, 128 * t : 128 * t + 128]
            spec[2 * n + t, BLOCK:] = out[BLOCK:, 128 * t : 128 * t + 128] * sigma
        return carry

    lax.fori_loop(0, 4, transform, 0)


def over_bins(spec, use):
    for sign, base in ((1.0, 0), (-1.0, 128)):

        def step(n, carry, sign=sign, base=base):
            re = pl.ds(pl.multiple_of(base + 8 * n, 8), 8)
            im = pl.ds(pl.multiple_of(BLOCK + base + 8 * n, 8), 8)
            own = [(spec[j, re], spec[j, im]) for j in range(8)]
            both = [own[0]]
            for j in range(1, 8):
                both.append(
                    (own[j][0] - sign * own[j - 1][1], own[j][1] + sign * own[j - 1][0])
                )
            use(re, im, own, both)
            return carry

        lax.fori_loop(0, 16, step, 0)


def summed(pairs):
    first = True
    for (ar, ai), (br, bi) in pairs:
        pr = ar * br - ai * bi
        pi = ar * bi + ai * br
        tr, ti = (pr, pi) if first else (tr + pr, ti + pi)
        first = False
    return tr, ti


def flipped(x, sign):
    return jnp.concatenate([x[0:BLOCK], x[BLOCK:] * sign], axis=0)


def conv_kernel(
    place, got, short, skip, ahead_h, ahead_l, back_h, back_l,
    sent,
    pad, prod, gates, spec, fspec, res, time, after,
):
    low = low_lanes(BLOCK)
    sigma = jnp.where(low, 1.0, -1.0)
    pair, gain = weights(place, short, skip)

    def filters(n, carry):
        def blocks(b):
            x, y = got[b, :, 128:256].astype(F32), got[b + 1, :, 128:256].astype(F32)
            return jnp.where(low, turned(x), y).astype(BF)

        f = jnp.concatenate([blocks(4 * n), blocks(4 * n + 2)], axis=1)
        out = mm(ahead_h[...], f) + mm(ahead_l[...], f)
        low512 = low_lanes(512)
        for t in range(2):
            x = out[:, 128 * t : 128 * t + 128]
            y = turned(x)
            fspec[4 * n + 2 * t] = jnp.where(low512, x, y)
            fspec[4 * n + 2 * t + 1] = jnp.where(low512, y, x)
        return carry

    lax.fori_loop(0, 2, filters, 0)
    prepare(got, pair, pad, prod, gates)
    spectra(prod, ahead_h, ahead_l, spec)

    def multiply(re, im, own, both):
        filt = [(fspec[m, re], fspec[m, im]) for m in range(8)]
        for i in range(8):
            tr, ti = summed([(filt[m], both[i - m]) for m in range(i + 1)])
            res[i, re] = tr
            res[i, im] = ti

    over_bins(spec, multiply)

    def invert(n, carry):
        x = jnp.concatenate([flipped(res[b], sigma) for b in (2 * n, 2 * n + 1)], axis=1)
        out = apply(back_h, back_l, *split(x))
        time[2 * n] = out[:, :128]
        time[2 * n + 1] = out[:, 128:]
        return carry

    lax.fori_loop(0, 4, invert, 0)

    low128 = low_lanes(128)

    def gate(b, carry):
        t = jnp.where(low, time[b], time[7 - b]) + gain * prod[b]
        rows = pl.ds(pl.multiple_of(BLOCK * b, 8), BLOCK)
        after[rows] = jnp.where(low, turned(t), t) * turned(gates[b])
        sent[b, BLOCK:] = jnp.where(low128, t[0:128], turned(t[128:256])).astype(BF)
        return carry

    lax.fori_loop(0, 8, gate, 0)
    after[8 * BLOCK :] = jnp.zeros((8, 128), F32)
    taps = pair(1, 2)
    for b in range(8):
        start = BLOCK * b
        y = sum(taps[j] * after[start + j : start + j + BLOCK] for j in range(3))
        sent[b, 0:BLOCK] = y.astype(BF)


def lag_kernel(
    place, got, short, skip, ahead_h, ahead_l, back_h, back_l,
    lags,
    pad, prod, spec, lres,
):
    pair, _ = weights(place, short, skip)
    prepare(got, pair, pad, prod)
    spectra(prod, ahead_h, ahead_l, spec)
    zero = jnp.zeros((8, 128), F32)
    low8 = low_lanes(8)

    def multiply(re, im, own, both):
        grads, shifted = [], []
        for i in range(8):
            grads.append(
                tuple(jnp.where(low8, turned(own[7 - i][k]), own[7 - i][k]) for k in range(2))
            )
            before = both[i - 1] if i else (zero, zero)
            shifted.append(
                tuple(jnp.where(low8, before[k], turned(both[i][k])) for k in range(2))
            )
        for a in range(4):
            tr, ti = summed([(grads[i], shifted[i - 2 * a]) for i in range(2 * a, 8)])
            lres[a, re] = tr
            lres[a, im] = ti

    over_bins(spec, multiply)

    def invert(n, carry):
        x = jnp.concatenate([flipped(lres[a], -1.0) for a in (2 * n, 2 * n + 1)], axis=1)
        out = apply(back_h, back_l, *split(x))
        low16 = low_lanes(16)
        for t in range(2):
            for k in range(8):
                x = out[32 * k : 32 * k + 16, 128 * t : 128 * t + 128]
                y = out[32 * k + 16 : 32 * k + 32, 128 * t : 128 * t + 128]
                m = 4 * n + 2 * t
                lags[m, k] = jnp.where(low16, turned(x), y).astype(BF)
                lags[m + 1, k] = jnp.where(low16, x, turned(y)).astype(BF)
        return carry

    lax.fori_loop(0, 2, invert, 0)


def on_channels(kernel, name, inputs, in_shapes, outputs, scratch, cost):
    full = lambda *shape: pl.BlockSpec(shape, lambda n, p: (0,) * len(shape))
    return pl.pallas_call(
        kernel,
        grid_spec=pltpu.PrefetchScalarGridSpec(
            num_scalar_prefetch=1,
            grid=(1,),
            in_specs=[
                full(8, BLOCK, 256),
                pl.BlockSpec((9, 128), lambda n, p: (0, p[0] // 2)),
                pl.BlockSpec((1, 128), lambda n, p: (0, p[0] // 2)),
            ]
            + [full(*shape) for shape in in_shapes],
            out_specs=[full(*shape) for shape, _ in outputs],
            scratch_shapes=[
                pltpu.VMEM(shape, dtype)
                for shape, dtype in [((8 + 8 * BLOCK, 128), F32)] + scratch
            ],
        ),
        out_shape=[jax.ShapeDtypeStruct(shape, dtype) for shape, dtype in outputs],
        cost_estimate=cost,
        name=name,
    )(*inputs)


TABLES = [(512, BLOCK), (512, BLOCK), (BLOCK, 512), (BLOCK, 512)]
BLOCKS = ((8, BLOCK, 128), F32)
BINS = ((8, 512, 128), F32)


def spent(flops):
    return pl.CostEstimate(flops=flops, bytes_accessed=3 * 10**6, transcendentals=0)


def conv(place, got, short, skip):
    inputs = (place, got, short, skip, *(jnp.asarray(t) for t in tables()))
    outputs = [((8, 384, 128), BF)]
    scratch = [BLOCKS, BLOCKS, BINS, BINS, BINS, BLOCKS, ((8 * BLOCK + 8, 128), F32)]
    return on_channels(conv_kernel, "conv", inputs, TABLES, outputs, scratch, None)[0]


def lag_sums(place, got, short, skip):
    inputs = (place, got, short, skip, *(jnp.asarray(t) for t in tables()))
    outputs = [((8, 8, 16, 128), BF)]
    scratch = [BLOCKS, BINS, ((4, 512, 128), F32)]
    cost = spent(2 * 10**9)
    return on_channels(lag_kernel, "lag_sums", inputs, TABLES, outputs, scratch, cost)[0]


def convolved(got, q, low128):
    a, b = got[2 * q, -128:].astype(F32), got[2 * q + 1, -128:].astype(F32)
    return jnp.where(low128, a, turned(b)), jnp.where(low128, turned(a), b)


def mixed_kernel(got, gate_out, grad, mixed, head):
    low128 = low_lanes(128)
    for q in range(4):
        lanes = slice(128 * q, 128 * q + 128)
        first, second = convolved(got, q, low128)
        mixed[0:128, lanes] = (gate_out[0:128, lanes] * first).astype(BF)
        mixed[128:256, lanes] = (gate_out[128:256, lanes] * second).astype(BF)
        head[:, lanes] = grad[:, lanes] * first[0:8]


def unpack_mixed(got, gate_out, grad):
    return pl.pallas_call(
        mixed_kernel,
        grid=(1,),
        in_specs=[
            pl.BlockSpec((8, 128, 128), lambda n: (0, 2, 0)),
            pl.BlockSpec((BLOCK, 512), lambda n: (0, 0)),
            pl.BlockSpec((8, 512), lambda n: (0, 0)),
        ],
        out_specs=[
            pl.BlockSpec((BLOCK, 512), lambda n: (0, 0)),
            pl.BlockSpec((8, 512), lambda n: (0, 0)),
        ],
        out_shape=[
            jax.ShapeDtypeStruct((BLOCK, 512), BF),
            jax.ShapeDtypeStruct((8, 512), F32),
        ],
        name="unpack_mixed",
    )(got, gate_out, grad)


def grads_kernel(got, grad, tail, short, grads, pad):
    low, low128 = low_lanes(BLOCK), low_lanes(128)
    pad[BLOCK:] = tail[...]
    for q in range(4):
        lanes = slice(128 * q, 128 * q + 128)
        first, second = convolved(got, q, low128)
        pad[0:128, lanes] = grad[0:128, lanes] * first
        pad[128:256, lanes] = grad[128:256, lanes] * second
        a, b = got[2 * q, 0:BLOCK].astype(F32), got[2 * q + 1, 0:BLOCK].astype(F32)
        grads[1, :, lanes] = jnp.where(low, a, turned(b)).astype(BF)
        grads[2, :, lanes] = jnp.where(low, turned(a), b).astype(BF)
        grads[0, :, lanes] = sum(
            short[j : j + 1, lanes] * pad[j : j + BLOCK, lanes] for j in range(3)
        ).astype(BF)


def unpack_grads(got, grad, tail, short):
    return pl.pallas_call(
        grads_kernel,
        out_shape=jax.ShapeDtypeStruct((3, BLOCK, 512), BF),
        scratch_shapes=[pltpu.VMEM((BLOCK + 8, 512), F32)],
        cost_estimate=pl.CostEstimate(flops=10**6, bytes_accessed=2 * 10**6, transcendentals=0),
        name="unpack_grads",
    )(got, grad, tail, short)


def partial_kernel(place, m00, m01, m10, m11, g00, g01, g10, g11, lags, lags_z, packed):
    def term(mixed, grad):
        return lax.dot_general(
            mixed[...], grad[...], (((0,), (0,)), ((), ())), preferred_element_type=F32
        )

    part = term(m00, g00) + term(m01, g01) + term(m10, g10) + term(m11, g11)
    part = part.astype(BF)
    for n in range(32):
        packed[n, :, 0:1024] = part[16 * n : 16 * n + 16]
        s, k = n % 8, n // 8
        lag = lags[s, k].astype(F32) + lags_z[s, k].astype(F32)
        packed[n, :, 1024:1152] = lag.astype(BF)


def partial(place, mixed, grad, grads, lags, lags_z):
    full = lambda *shape: pl.BlockSpec(shape, lambda n, p: (0,) * len(shape))
    return pl.pallas_call(
        partial_kernel,
        grid_spec=pltpu.PrefetchScalarGridSpec(
            num_scalar_prefetch=1,
            grid=(1,),
            in_specs=[full(BLOCK, 512)] * 4
            + [pl.BlockSpec((BLOCK, 1024), lambda n, p: (0, p[0]))]
            + [full(BLOCK, 1024)] * 3
            + [full(8, 4, 16, 128)] * 2,
            out_specs=full(32, 16, 1152),
        ),
        out_shape=jax.ShapeDtypeStruct((32, 16, 1152), BF),
        name="partial",
    )(place, *mixed, grad, *grads, lags, lags_z)


def reduce_kernel(scale, got, shared, lags):
    total = jnp.zeros((16, 1024), F32)
    for n in range(32):
        total = total + got[n, :, 0:1024].astype(F32)
    total = (total * scale).astype(BF)
    for n in range(64):
        shared[n] = total
    for s in range(8):
        lag = jnp.zeros((16, 128), F32)
        for k in range(4):
            lag = lag + got[8 * k + s, :, 1024:1152].astype(F32)
        lags[:, 128 * s : 128 * s + 128] = lag * scale


def reduce(got, scale):
    return pl.pallas_call(
        functools.partial(reduce_kernel, scale),
        out_shape=[
            jax.ShapeDtypeStruct((64, 16, 1024), BF),
            jax.ShapeDtypeStruct((16, 1024), F32),
        ],
        name="reduce",
    )(got)


def half_kernel(place, mine, *refs):
    grad_weight, wide, sems = refs[-3:]

    def copy(n):
        zh, zl, yh = n // 4, n // 2 % 2, n % 2
        rows = slice(128 * (2 * zh + yh), 128 * (2 * zh + yh) + 128)
        lanes = pl.ds(pl.multiple_of(2048 * place[0] + 1024 * zl, 1024), 1024)
        return pltpu.make_async_copy(wide.at[n], grad_weight.at[rows, lanes], sems.at[n])

    for n in range(8):
        for k in range(8):
            wide[n, 16 * k : 16 * k + 16] = mine[8 * n + k].astype(F32)
        copy(n).start()
    for n in range(8):
        copy(n).wait()


def write_half(half, rows, whole=None):
    more = [] if whole is None else [whole]
    return pl.pallas_call(
        half_kernel,
        grid_spec=pltpu.PrefetchScalarGridSpec(
            num_scalar_prefetch=1,
            grid=(1,),
            in_specs=[pl.BlockSpec((64, 16, 1024), lambda n, p: (0, 0, 0))]
            + [pl.BlockSpec(memory_space=pltpu.HBM)] * len(more),
            out_specs=pl.BlockSpec(memory_space=pltpu.HBM),
            scratch_shapes=[
                pltpu.VMEM((8, 128, 1024), F32),
                pltpu.SemaphoreType.DMA((8,)),
            ],
        ),
        out_shape=jax.ShapeDtypeStruct((512, 4096), F32),
        input_output_aliases={2: 0} if more else {},
        cost_estimate=pl.CostEstimate(flops=10**6, bytes_accessed=6 * 10**6, transcendentals=0),
        name="write_half",
    )(half, rows, *more)


def filter_kernel(place, *refs):
    grad_filter = refs[-1]
    low = low_lanes(16)
    for d in range(4):
        z = (place[0] + 4 - d) % 4
        for n in range(2):
            yh = place[1] if n == 0 else 1 - place[1]
            row = pl.multiple_of(32 * (2 * z + yh), 32)
            lags = refs[2 * d + n]
            for q in range(4):
                a = lags[:, 256 * q : 256 * q + 128].astype(F32)
                b = lags[:, 256 * q + 128 : 256 * q + 256].astype(F32)
                lanes = slice(128 * q, 128 * q + 128)
                grad_filter[pl.ds(row, 16), lanes] = jnp.where(low, a, turned(b))
                grad_filter[pl.ds(row + 16, 16), lanes] = jnp.where(low, turned(a), b)


def write_filter(place, lags):
    full = lambda *shape: pl.BlockSpec(shape, lambda n, p: (0,) * len(shape))
    return pl.pallas_call(
        filter_kernel,
        grid_spec=pltpu.PrefetchScalarGridSpec(
            num_scalar_prefetch=1,
            grid=(1,),
            in_specs=[full(16, 1024)] * 8,
            out_specs=full(BLOCK, 512),
        ),
        out_shape=jax.ShapeDtypeStruct((BLOCK, 512), F32),
        cost_estimate=pl.CostEstimate(flops=10**6, bytes_accessed=2 * 10**6, transcendentals=0),
        name="write_filter",
    )(place, *lags)


def exchange(x, axes):
    return lax.all_to_all(x, axes, 0, 0, tiled=True)


def across(x):
    return lax.ppermute(x, "c", [(0, 1), (1, 0)])


def along(x, step):
    return lax.ppermute(x, SEQ, [(n, n + step) for n in range(8) if 0 <= n + step < 8])


def above(x):
    return lax.ppermute(x, "zl", [(0, 1), (1, 0)])


def opposite(x):
    return lax.ppermute(x, ("zl", "c"), [(n, 3 - n) for n in range(4)])


def gathered(lags):
    pair = (lags, lax.ppermute(lags, "yh", [(0, 1), (1, 0)]))
    out = list(pair)
    for d in range(1, 4):
        route = [(n, (n + d) % 4) for n in range(4)]
        out += [lax.ppermute(part, ("zh", "zl"), route) for part in pair]
    return out


def on_device(streams, short_filter, long_filter, skip_gain, out_weight, out_grad):
    scale = 1.0 / math.sqrt(16 * 2048)
    core = lax.axis_index("c").astype(jnp.int32)
    side = lax.axis_index("zl").astype(jnp.int32)
    seq = lax.axis_index(SEQ).astype(jnp.int32)
    grad = out_grad[0]

    def quarter(c, z):
        return lax.dynamic_slice(grad, (0, 1024 * (2 * c + z)), (BLOCK, 1024))

    grads = (
        above(quarter(core, 1 - side)),
        across(quarter(1 - core, side)),
        opposite(quarter(1 - core, 1 - side)),
    )
    short = short_filter.reshape(9, 512)
    edge = along(streams[0, 0, BLOCK - 8 :], 1)
    grad_mixed = grad_of_mixed(grad, out_weight)
    edge, grad_mixed = lax.optimization_barrier((edge, grad_mixed))
    packed, gate_out = pack(streams[:, 0], edge, grad_mixed, long_filter, short)
    got = exchange(packed, SEQ)
    channels = (seq[None], got, short, skip_gain.reshape(1, 512))
    sent = conv(*channels)
    sent, got, grads = lax.optimization_barrier((sent, got, grads))
    channels = (channels[0], got) + channels[2:]
    lags = lag_sums(*channels).reshape(8, 2, 2, 2, 16, 128)

    def of_side(z):
        return lax.dynamic_index_in_dim(lags, z, 2, False).reshape(8, 4, 16, 128)

    lags_own, lags_z = of_side(side), above(of_side(1 - side))
    back = exchange(sent, SEQ)
    back, lags_own, lags_z = lax.optimization_barrier((back, lags_own, lags_z))
    m00, head = unpack_mixed(back, gate_out, grad_mixed)
    m01, m10 = above(m00), across(m00)
    mixed = (m00, m01, m10, across(m01))
    part = partial((2 * core + side)[None], mixed, grad, grads, lags_own, lags_z)
    part, m00, back, head = lax.optimization_barrier((part, m00, back, head))
    part = exchange(part, MOST)
    layer_out = jnp.dot(m00, out_weight, preferred_element_type=F32).astype(BF)
    grad_streams = unpack_grads(back, grad_mixed, along(head, -1), short)
    part, layer_out, grad_streams = lax.optimization_barrier((part, layer_out, grad_streams))
    rows, lags = reduce(part, scale)
    rows, lags = lax.optimization_barrier((rows, lags))
    mine = exchange(rows, CHIPS)
    lags = (lags + across(lags)).astype(BF)
    place = jnp.stack([lax.axis_index(("zh", "zl")), lax.axis_index("yh")]).astype(jnp.int32)
    grad_filter = write_filter(place, gathered(lags))
    mine, grad_filter = lax.optimization_barrier((mine, grad_filter))
    theirs = across(mine)
    grad_weight = write_half(core[None], mine)
    grad_weight = write_half(1 - core[None], theirs, grad_weight)
    return layer_out[None], grad_streams[:, None], grad_filter, grad_weight


def solution(mesh):
    fine = Mesh(
        mesh.devices.reshape(2, 2, 2, 2, 4, 2), ("zh", "zl", "yh", "c", "x", "yl")
    )
    dp = ("zh", "zl", "yh", "c")
    placed = (P(None, dp, SEQ, None), P(), P(SEQ, None), P(), P(), P(dp, SEQ, None))
    return jax.shard_map(
        on_device,
        mesh=fine,
        in_specs=placed,
        out_specs=(P(dp, SEQ, None), P(None, dp, SEQ, None), P(SEQ, None), P()),
        check_vma=False,
    )
```

```python
import functools
import math

import jax
import jax.numpy as jnp
import numpy as np
from jax import lax
from jax.experimental import pallas as pl
from jax.experimental.pallas import tpu as pltpu
from jax.sharding import Mesh, PartitionSpec as P

BF = jnp.bfloat16
F32 = jnp.float32
BLOCK = 256
HALF = 64
SENT_ROWS = BLOCK + 16
SEQ = ("x", "yl")
MOST = ("zh", "yh") + SEQ
DEPTH = ("zh", "zl", "yh")
CHIPS = DEPTH + SEQ


@functools.lru_cache(maxsize=None)
def tables():
    order = np.concatenate([np.arange(0, BLOCK, 2), np.arange(1, BLOCK, 2)])
    angle = np.pi * ((2 * order[:, None] + 1) * np.arange(BLOCK)[None, :] % 1024) / 512.0
    ahead = np.concatenate([np.cos(angle), -np.sin(angle)], axis=0)
    back = ahead.T / BLOCK

    def two(table):
        table = table.astype(np.float32)
        high = table.astype(jnp.bfloat16)
        return high, (table - high.astype(np.float32)).astype(jnp.bfloat16)

    return two(ahead) + two(back)


def mm(a, b):
    return jnp.dot(a, b, preferred_element_type=F32)


def low_lanes(rows):
    return lax.broadcasted_iota(jnp.int32, (rows, 128), 1) < HALF


def turned(x):
    return pltpu.roll(x, HALF, 1)


def pack_kernel(streams, out_grad, weight, filt, short, packed, grad, gate_out, pad):
    step = pl.program_id(0)
    low, low16 = low_lanes(BLOCK), low_lanes(16)

    @pl.when(step == 0)
    def _():
        grad[...] = jnp.zeros_like(grad)

    grad[...] += lax.dot_general(
        out_grad[...], weight[...], (((1,), (1,)), ((), ())), preferred_element_type=F32
    )

    for q in range(4):

        @pl.when(step == q)
        def _(q=q):
            lanes = slice(128 * q, 128 * q + 128)
            a, b = streams[1, :, lanes].astype(F32), streams[2, :, lanes].astype(F32)
            packed[2 * q, 0:BLOCK, 0:128] = jnp.where(low, a, turned(b)).astype(BF)
            packed[2 * q + 1, 0:BLOCK, 0:128] = jnp.where(low, turned(a), b).astype(BF)
            pad[0:8] = jnp.zeros((8, 128), F32)
            pad[8:] = streams[0, :, lanes].astype(F32)
            gate_out[:, lanes] = sum(
                short[j : j + 1, lanes] * pad[8 - j : 8 - j + BLOCK] for j in range(3)
            )

    @pl.when(step == pl.num_programs(0) - 1)
    def _():
        for q in range(4):
            lanes = slice(128 * q, 128 * q + 128)
            a, b = grad[:, lanes] * gate_out[:, lanes], filt[:, lanes]
            packed[2 * q, 0:BLOCK, 128:256] = jnp.where(low, a, turned(b)).astype(BF)
            packed[2 * q + 1, 0:BLOCK, 128:256] = jnp.where(low, turned(a), b).astype(BF)
            ends = streams[0, :, lanes].astype(F32)
            a = jnp.concatenate([ends[0:8], ends[BLOCK - 8 :]], axis=0)
            b = grad[0:16, lanes]
            packed[2 * q, BLOCK:, 0:128] = jnp.where(low16, a, turned(b)).astype(BF)
            packed[2 * q + 1, BLOCK:, 0:128] = jnp.where(low16, turned(a), b).astype(BF)
            packed[2 * q, BLOCK:, 128:256] = jnp.zeros((16, 128), BF)
            packed[2 * q + 1, BLOCK:, 128:256] = jnp.zeros((16, 128), BF)


def pack(streams, out_grad, weight, filt, short):
    steps = 4
    wide = out_grad.shape[1] // steps
    full = lambda *shape: pl.BlockSpec(shape, lambda k: (0,) * len(shape))
    return pl.pallas_call(
        pack_kernel,
        grid=(steps,),
        in_specs=[
            full(3, BLOCK, 512),
            pl.BlockSpec((BLOCK, wide), lambda k: (0, k)),
            pl.BlockSpec((512, wide), lambda k: (0, k)),
            full(BLOCK, 512),
            full(9, 512),
        ],
        out_specs=[full(8, SENT_ROWS, 256), full(BLOCK, 512), full(BLOCK, 512)],
        out_shape=[
            jax.ShapeDtypeStruct((8, SENT_ROWS, 256), BF),
            jax.ShapeDtypeStruct((BLOCK, 512), F32),
            jax.ShapeDtypeStruct((BLOCK, 512), F32),
        ],
        scratch_shapes=[pltpu.VMEM((8 + BLOCK, 128), F32)],
        name="pack",
    )(streams, out_grad, weight, filt, short)


def split(x):
    high = x.astype(BF)
    return high, (x - high.astype(F32)).astype(BF)


def apply(table_h, table_l, high, rest):
    return mm(table_h[...], high) + mm(table_h[...], rest) + mm(table_l[...], high)


def weights(place, short, skip):
    low1 = low_lanes(1)
    odd = place[0] % 2 == 1
    taps = short[...]
    taps = jnp.where(odd, turned(taps), taps)
    taps_up = turned(taps)
    gain = skip[...]
    gain = jnp.where(odd, turned(gain), gain)
    gain = jnp.where(low1, gain, turned(gain))

    def pair(first, second):
        def row(table, i, j):
            if i is None:
                return jnp.full((1, 128), 1.0 if j == 0 else 0.0, F32)
            return table[3 * i + j : 3 * i + j + 1]

        return [
            jnp.where(low1, row(taps, first, j), row(taps_up, second, j)) for j in range(3)
        ]

    return pair, gain


def prepare(got, pair, pad, prod, gates=None):
    taps = pair(1, 2)
    low = low_lanes(BLOCK)
    pad[0:8] = jnp.zeros((8, 128), F32)

    def load(b, carry):
        rows = pl.ds(pl.multiple_of(8 + BLOCK * b, 8), BLOCK)
        pad[rows] = got[b, 0:BLOCK, 0:128].astype(F32)
        return carry

    lax.fori_loop(0, 8, load, 0)
    for b in range(8):
        start = 8 + BLOCK * b
        s = sum(taps[j] * pad[start - j : start - j + BLOCK] for j in range(3))
        if gates is not None:
            gates[b] = s
        prod[b] = jnp.where(low, s * turned(s), turned(got[b, 0:BLOCK, 128:256].astype(F32)))
    low8 = low_lanes(8)
    gate = pair(0, None)
    for b in range(8):
        ends = got[b, BLOCK:, 0:128].astype(F32)
        first = got[b - 1, BLOCK:, 0:128].astype(F32)[8:] if b else jnp.zeros((8, 128), F32)
        pad[0:8] = first
        pad[8:16] = ends[0:8]
        out = sum(gate[j] * pad[8 - j : 16 - j] for j in range(3))
        prod[b, 0:8] = jnp.where(low8, prod[b, 0:8], turned(out) * ends[0:8])


def spectra(prod, ahead_h, ahead_l, spec):
    low = low_lanes(BLOCK)
    sigma = jnp.where(low, 1.0, -1.0)

    def transform(n, carry):
        x = jnp.concatenate(
            [jnp.where(low, prod[b], prod[7 - b]) for b in (2 * n, 2 * n + 1)], axis=1
        )
        out = apply(ahead_h, ahead_l, *split(x))
        for t in range(2):
            spec[2 * n + t, 0:BLOCK] = out[:BLOCK, 128 * t : 128 * t + 128]
            spec[2 * n + t, BLOCK:] = out[BLOCK:, 128 * t : 128 * t + 128] * sigma
        return carry

    lax.fori_loop(0, 4, transform, 0)


def over_bins(spec, use):
    for sign, base in ((1.0, 0), (-1.0, 128)):

        def step(n, carry, sign=sign, base=base):
            re = pl.ds(pl.multiple_of(base + 8 * n, 8), 8)
            im = pl.ds(pl.multiple_of(BLOCK + base + 8 * n, 8), 8)
            own = [(spec[j, re], spec[j, im]) for j in range(8)]
            both = [own[0]]
            for j in range(1, 8):
                both.append(
                    (own[j][0] - sign * own[j - 1][1], own[j][1] + sign * own[j - 1][0])
                )
            use(re, im, own, both)
            return carry

        lax.fori_loop(0, 16, step, 0)


def summed(pairs):
    first = True
    for (ar, ai), (br, bi) in pairs:
        pr = ar * br - ai * bi
        pi = ar * bi + ai * br
        tr, ti = (pr, pi) if first else (tr + pr, ti + pi)
        first = False
    return tr, ti


def flipped(x, sign):
    return jnp.concatenate([x[0:BLOCK], x[BLOCK:] * sign], axis=0)


def conv_kernel(
    place, got, short, skip, ahead_h, ahead_l, back_h, back_l,
    sent,
    pad, prod, gates, spec, fspec, res, time, after,
):
    low = low_lanes(BLOCK)
    sigma = jnp.where(low, 1.0, -1.0)
    pair, gain = weights(place, short, skip)

    def filters(n, carry):
        def blocks(b):
            x, y = (got[n, 0:BLOCK, 128:256].astype(F32) for n in (b, b + 1))
            return jnp.where(low, turned(x), y).astype(BF)

        f = jnp.concatenate([blocks(4 * n), blocks(4 * n + 2)], axis=1)
        out = mm(ahead_h[...], f) + mm(ahead_l[...], f)
        low512 = low_lanes(512)
        for t in range(2):
            x = out[:, 128 * t : 128 * t + 128]
            y = turned(x)
            fspec[4 * n + 2 * t] = jnp.where(low512, x, y)
            fspec[4 * n + 2 * t + 1] = jnp.where(low512, y, x)
        return carry

    lax.fori_loop(0, 2, filters, 0)
    prepare(got, pair, pad, prod, gates)
    spectra(prod, ahead_h, ahead_l, spec)

    def multiply(re, im, own, both):
        filt = [(fspec[m, re], fspec[m, im]) for m in range(8)]
        for i in range(8):
            tr, ti = summed([(filt[m], both[i - m]) for m in range(i + 1)])
            res[i, re] = tr
            res[i, im] = ti

    over_bins(spec, multiply)

    def invert(n, carry):
        x = jnp.concatenate([flipped(res[b], sigma) for b in (2 * n, 2 * n + 1)], axis=1)
        out = apply(back_h, back_l, *split(x))
        time[2 * n] = out[:, :128]
        time[2 * n + 1] = out[:, 128:]
        return carry

    lax.fori_loop(0, 4, invert, 0)

    low128 = low_lanes(128)

    def gate(b, carry):
        t = jnp.where(low, time[b], time[7 - b]) + gain * prod[b]
        rows = pl.ds(pl.multiple_of(BLOCK * b, 8), BLOCK)
        after[rows] = jnp.where(low, turned(t), t) * turned(gates[b])
        sent[b, BLOCK:] = jnp.where(low128, t[0:128], turned(t[128:256])).astype(BF)
        return carry

    lax.fori_loop(0, 8, gate, 0)
    after[8 * BLOCK :] = jnp.zeros((8, 128), F32)
    taps = pair(1, 2)
    for b in range(8):
        start = BLOCK * b
        y = sum(taps[j] * after[start + j : start + j + BLOCK] for j in range(3))
        sent[b, 0:BLOCK] = y.astype(BF)


def lag_kernel(
    place, got, short, skip, ahead_h, ahead_l, back_h, back_l,
    lags,
    pad, prod, spec, lres,
):
    pair, _ = weights(place, short, skip)
    prepare(got, pair, pad, prod)
    spectra(prod, ahead_h, ahead_l, spec)
    zero = jnp.zeros((8, 128), F32)
    low8 = low_lanes(8)

    def multiply(re, im, own, both):
        grads, shifted = [], []
        for i in range(8):
            grads.append(
                tuple(jnp.where(low8, turned(own[7 - i][k]), own[7 - i][k]) for k in range(2))
            )
            before = both[i - 1] if i else (zero, zero)
            shifted.append(
                tuple(jnp.where(low8, before[k], turned(both[i][k])) for k in range(2))
            )
        for a in range(4):
            tr, ti = summed([(grads[i], shifted[i - 2 * a]) for i in range(2 * a, 8)])
            lres[a, re] = tr
            lres[a, im] = ti

    over_bins(spec, multiply)

    def invert(n, carry):
        x = jnp.concatenate([flipped(lres[a], -1.0) for a in (2 * n, 2 * n + 1)], axis=1)
        out = apply(back_h, back_l, *split(x))
        low16 = low_lanes(16)
        for t in range(2):
            for k in range(8):
                x = out[32 * k : 32 * k + 16, 128 * t : 128 * t + 128]
                y = out[32 * k + 16 : 32 * k + 32, 128 * t : 128 * t + 128]
                m = 4 * n + 2 * t
                lags[m, k] = jnp.where(low16, turned(x), y).astype(BF)
                lags[m + 1, k] = jnp.where(low16, x, turned(y)).astype(BF)
        return carry

    lax.fori_loop(0, 2, invert, 0)


def on_channels(kernel, name, inputs, in_shapes, outputs, scratch, cost):
    full = lambda *shape: pl.BlockSpec(shape, lambda n, p: (0,) * len(shape))
    return pl.pallas_call(
        kernel,
        grid_spec=pltpu.PrefetchScalarGridSpec(
            num_scalar_prefetch=1,
            grid=(1,),
            in_specs=[
                full(8, SENT_ROWS, 256),
                pl.BlockSpec((9, 128), lambda n, p: (0, p[0] // 2)),
                pl.BlockSpec((1, 128), lambda n, p: (0, p[0] // 2)),
            ]
            + [full(*shape) for shape in in_shapes],
            out_specs=[full(*shape) for shape, _ in outputs],
            scratch_shapes=[
                pltpu.VMEM(shape, dtype)
                for shape, dtype in [((8 + 8 * BLOCK, 128), F32)] + scratch
            ],
        ),
        out_shape=[jax.ShapeDtypeStruct(shape, dtype) for shape, dtype in outputs],
        cost_estimate=cost,
        name=name,
    )(*inputs)


TABLES = [(512, BLOCK), (512, BLOCK), (BLOCK, 512), (BLOCK, 512)]
BLOCKS = ((8, BLOCK, 128), F32)
BINS = ((8, 512, 128), F32)


def spent(flops):
    return pl.CostEstimate(flops=flops, bytes_accessed=3 * 10**6, transcendentals=0)


def conv(place, got, short, skip):
    inputs = (place, got, short, skip, *(jnp.asarray(t) for t in tables()))
    outputs = [((8, 384, 128), BF)]
    scratch = [BLOCKS, BLOCKS, BINS, BINS, BINS, BLOCKS, ((8 * BLOCK + 8, 128), F32)]
    return on_channels(conv_kernel, "conv", inputs, TABLES, outputs, scratch, None)[0]


def lag_sums(place, got, short, skip):
    inputs = (place, got, short, skip, *(jnp.asarray(t) for t in tables()))
    outputs = [((8, 8, 16, 128), BF)]
    scratch = [BLOCKS, BINS, ((4, 512, 128), F32)]
    cost = spent(2 * 10**9)
    return on_channels(lag_kernel, "lag_sums", inputs, TABLES, outputs, scratch, cost)[0]


def convolved(got, q, low128):
    a, b = got[2 * q, -128:].astype(F32), got[2 * q + 1, -128:].astype(F32)
    return jnp.where(low128, a, turned(b)), jnp.where(low128, turned(a), b)


def mixed_kernel(got, gate_out, grad, edge, short, mixed, head, pad):
    low128 = low_lanes(128)
    pad[0:8] = edge[...].astype(F32)
    pad[8:] = jnp.zeros((8, 512), F32)
    more = sum(short[j : j + 1] * pad[8 - j : 16 - j] for j in (1, 2))
    for q in range(4):
        lanes = slice(128 * q, 128 * q + 128)
        first, second = convolved(got, q, low128)
        gate = gate_out[0:128, lanes]
        gate = jnp.concatenate([gate[0:8] + more[:, lanes], gate[8:]], axis=0)
        mixed[0:128, lanes] = (gate * first).astype(BF)
        mixed[128:256, lanes] = (gate_out[128:256, lanes] * second).astype(BF)
        head[:, lanes] = grad[:, lanes] * first[0:8]


def unpack_mixed(got, gate_out, grad, edge, short):
    return pl.pallas_call(
        mixed_kernel,
        grid=(1,),
        in_specs=[
            pl.BlockSpec((8, 128, 128), lambda n: (0, 2, 0)),
            pl.BlockSpec((BLOCK, 512), lambda n: (0, 0)),
            pl.BlockSpec((8, 512), lambda n: (0, 0)),
            pl.BlockSpec((8, 512), lambda n: (0, 0)),
            pl.BlockSpec((9, 512), lambda n: (0, 0)),
        ],
        out_specs=[
            pl.BlockSpec((BLOCK, 512), lambda n: (0, 0)),
            pl.BlockSpec((8, 512), lambda n: (0, 0)),
        ],
        scratch_shapes=[pltpu.VMEM((16, 512), F32)],
        out_shape=[
            jax.ShapeDtypeStruct((BLOCK, 512), BF),
            jax.ShapeDtypeStruct((8, 512), F32),
        ],
        name="unpack_mixed",
    )(got, gate_out, grad, edge, short)


def grads_kernel(got, grad, tail, short, grads, pad):
    low, low128 = low_lanes(BLOCK), low_lanes(128)
    pad[BLOCK:] = tail[...]
    for q in range(4):
        lanes = slice(128 * q, 128 * q + 128)
        first, second = convolved(got, q, low128)
        pad[0:128, lanes] = grad[0:128, lanes] * first
        pad[128:256, lanes] = grad[128:256, lanes] * second
        a, b = got[2 * q, 0:BLOCK].astype(F32), got[2 * q + 1, 0:BLOCK].astype(F32)
        grads[1, :, lanes] = jnp.where(low, a, turned(b)).astype(BF)
        grads[2, :, lanes] = jnp.where(low, turned(a), b).astype(BF)
        grads[0, :, lanes] = sum(
            short[j : j + 1, lanes] * pad[j : j + BLOCK, lanes] for j in range(3)
        ).astype(BF)


def unpack_grads(got, grad, tail, short):
    return pl.pallas_call(
        grads_kernel,
        out_shape=jax.ShapeDtypeStruct((3, BLOCK, 512), BF),
        scratch_shapes=[pltpu.VMEM((BLOCK + 8, 512), F32)],
        cost_estimate=pl.CostEstimate(flops=10**6, bytes_accessed=2 * 10**6, transcendentals=0),
        name="unpack_grads",
    )(got, grad, tail, short)


def partial_kernel(place, m00, m01, m10, m11, g00, g01, g10, g11, lags, lags_z, packed):
    def term(mixed, grad):
        return lax.dot_general(
            mixed[...], grad[...], (((0,), (0,)), ((), ())), preferred_element_type=F32
        )

    part = term(m00, g00) + term(m01, g01) + term(m10, g10) + term(m11, g11)
    part = part.astype(BF)
    for n in range(32):
        packed[n, :, 0:1024] = part[16 * n : 16 * n + 16]
        s, k = n % 8, n // 8
        lag = lags[s, k].astype(F32) + lags_z[s, k].astype(F32)
        packed[n, :, 1024:1152] = lag.astype(BF)


def partial(place, mixed, grad, grads, lags, lags_z):
    full = lambda *shape: pl.BlockSpec(shape, lambda n, p: (0,) * len(shape))
    return pl.pallas_call(
        partial_kernel,
        grid_spec=pltpu.PrefetchScalarGridSpec(
            num_scalar_prefetch=1,
            grid=(1,),
            in_specs=[full(BLOCK, 512)] * 4
            + [pl.BlockSpec((BLOCK, 1024), lambda n, p: (0, p[0]))]
            + [full(BLOCK, 1024)] * 3
            + [full(8, 4, 16, 128)] * 2,
            out_specs=full(32, 16, 1152),
        ),
        out_shape=jax.ShapeDtypeStruct((32, 16, 1152), BF),
        name="partial",
    )(place, *mixed, grad, *grads, lags, lags_z)


def reduce_kernel(scale, got, shared, lags):
    total = jnp.zeros((16, 1024), F32)
    for n in range(32):
        total = total + got[n, :, 0:1024].astype(F32)
    total = (total * scale).astype(BF)
    for n in range(64):
        shared[n] = total
    for s in range(8):
        lag = jnp.zeros((16, 128), F32)
        for k in range(4):
            lag = lag + got[8 * k + s, :, 1024:1152].astype(F32)
        lags[:, 128 * s : 128 * s + 128] = lag * scale


def reduce(got, scale):
    return pl.pallas_call(
        functools.partial(reduce_kernel, scale),
        out_shape=[
            jax.ShapeDtypeStruct((64, 16, 1024), BF),
            jax.ShapeDtypeStruct((16, 1024), F32),
        ],
        name="reduce",
    )(got)


def half_kernel(place, mine, *refs):
    grad_weight, wide, sems = refs[-3:]

    def copy(n):
        zh, zl, yh = n // 4, n // 2 % 2, n % 2
        rows = slice(128 * (2 * zh + yh), 128 * (2 * zh + yh) + 128)
        lanes = pl.ds(pl.multiple_of(2048 * place[0] + 1024 * zl, 1024), 1024)
        return pltpu.make_async_copy(wide.at[n], grad_weight.at[rows, lanes], sems.at[n])

    for n in range(8):
        for k in range(8):
            wide[n, 16 * k : 16 * k + 16] = mine[8 * n + k].astype(F32)
        copy(n).start()
    for n in range(8):
        copy(n).wait()


def write_half(half, rows, whole=None):
    more = [] if whole is None else [whole]
    return pl.pallas_call(
        half_kernel,
        grid_spec=pltpu.PrefetchScalarGridSpec(
            num_scalar_prefetch=1,
            grid=(1,),
            in_specs=[pl.BlockSpec((64, 16, 1024), lambda n, p: (0, 0, 0))]
            + [pl.BlockSpec(memory_space=pltpu.HBM)] * len(more),
            out_specs=pl.BlockSpec(memory_space=pltpu.HBM),
            scratch_shapes=[
                pltpu.VMEM((8, 128, 1024), F32),
                pltpu.SemaphoreType.DMA((8,)),
            ],
        ),
        out_shape=jax.ShapeDtypeStruct((512, 4096), F32),
        input_output_aliases={2: 0} if more else {},
        cost_estimate=pl.CostEstimate(flops=10**6, bytes_accessed=6 * 10**6, transcendentals=0),
        name="write_half",
    )(half, rows, *more)


def filter_kernel(place, *refs):
    grad_filter = refs[-1]
    low = low_lanes(16)
    for n in range(8):
        row = pl.multiple_of(32 * (place[0] ^ n), 32)
        for q in range(4):
            a = refs[n][:, 256 * q : 256 * q + 128].astype(F32)
            b = refs[n][:, 256 * q + 128 : 256 * q + 256].astype(F32)
            lanes = slice(128 * q, 128 * q + 128)
            grad_filter[pl.ds(row, 16), lanes] = jnp.where(low, a, turned(b))
            grad_filter[pl.ds(row + 16, 16), lanes] = jnp.where(low, turned(a), b)


def write_filter(place, lags):
    full = lambda *shape: pl.BlockSpec(shape, lambda n, p: (0,) * len(shape))
    return pl.pallas_call(
        filter_kernel,
        grid_spec=pltpu.PrefetchScalarGridSpec(
            num_scalar_prefetch=1,
            grid=(1,),
            in_specs=[full(16, 1024)] * 8,
            out_specs=full(BLOCK, 512),
        ),
        out_shape=jax.ShapeDtypeStruct((BLOCK, 512), F32),
        cost_estimate=pl.CostEstimate(flops=10**6, bytes_accessed=2 * 10**6, transcendentals=0),
        name="write_filter",
    )(place, *lags)


def exchange(x, axes):
    return lax.all_to_all(x, axes, 0, 0, tiled=True)


def across(x):
    return lax.ppermute(x, "c", [(0, 1), (1, 0)])


def along(x, step):
    return lax.ppermute(x, SEQ, [(n, n + step) for n in range(8) if 0 <= n + step < 8])


def above(x):
    return lax.ppermute(x, "zl", [(0, 1), (1, 0)])


def opposite(x):
    return lax.ppermute(x, ("zl", "c"), [(n, 3 - n) for n in range(4)])


def gathered(lags):
    return [lags] + [
        lax.ppermute(lags, DEPTH, [(i, i ^ n) for i in range(8)]) for n in range(1, 8)
    ]


def on_device(streams, short_filter, long_filter, skip_gain, out_weight, out_grad):
    scale = 1.0 / math.sqrt(16 * 2048)
    core = lax.axis_index("c").astype(jnp.int32)
    side = lax.axis_index("zl").astype(jnp.int32)
    seq = lax.axis_index(SEQ).astype(jnp.int32)
    grad = out_grad[0]

    def quarter(c, z):
        return lax.dynamic_slice(grad, (0, 1024 * (2 * c + z)), (BLOCK, 1024))

    grads = (
        above(quarter(core, 1 - side)),
        across(quarter(1 - core, side)),
        opposite(quarter(1 - core, 1 - side)),
    )
    short = short_filter.reshape(9, 512)
    packed, grad_mixed, gate_out = pack(streams[:, 0], grad, out_weight, long_filter, short)
    got = exchange(packed, SEQ)
    edge = along(streams[0, 0, BLOCK - 8 :], 1)
    channels = (seq[None], got, short, skip_gain.reshape(1, 512))
    sent = conv(*channels)
    sent, got, grads, edge = lax.optimization_barrier((sent, got, grads, edge))
    channels = (channels[0], got) + channels[2:]
    lags = lag_sums(*channels).reshape(8, 2, 2, 2, 16, 128)

    def of_side(z):
        return lax.dynamic_index_in_dim(lags, z, 2, False).reshape(8, 4, 16, 128)

    lags_own, lags_z = of_side(side), above(of_side(1 - side))
    back = exchange(sent, SEQ)
    back, lags_own = lax.optimization_barrier((back, lags_own))
    m00, head = unpack_mixed(back, gate_out, grad_mixed, edge, short)
    m01, m10 = above(m00), across(m00)
    mixed = (m00, m01, m10, across(m01))
    tail = along(head, -1)
    part = partial((2 * core + side)[None], mixed, grad, grads, lags_own, lags_z)
    part, m00, back, tail = lax.optimization_barrier((part, m00, back, tail))
    part = exchange(part, MOST)
    layer_out = jnp.dot(m00, out_weight, preferred_element_type=F32).astype(BF)
    grad_streams = unpack_grads(back, grad_mixed, tail, short)
    part, layer_out, grad_streams = lax.optimization_barrier((part, layer_out, grad_streams))
    rows, lags = reduce(part, scale)
    rows, lags = lax.optimization_barrier((rows, lags))
    mine = exchange(rows, CHIPS)
    lags = (lags + across(lags)).astype(BF)
    depth = lax.axis_index(DEPTH).astype(jnp.int32)
    grad_filter = write_filter(depth[None], gathered(lags))
    mine, grad_filter = lax.optimization_barrier((mine, grad_filter))
    theirs = across(mine)
    grad_weight = write_half(core[None], mine)
    grad_weight = write_half(1 - core[None], theirs, grad_weight)
    return layer_out[None], grad_streams[:, None], grad_filter, grad_weight


def solution(mesh):
    fine = Mesh(
        mesh.devices.reshape(2, 2, 2, 2, 4, 2), ("zh", "zl", "yh", "c", "x", "yl")
    )
    dp = ("zh", "zl", "yh", "c")
    placed = (P(None, dp, SEQ, None), P(), P(SEQ, None), P(), P(), P(dp, SEQ, None))
    return jax.shard_map(
        on_device,
        mesh=fine,
        in_specs=placed,
        out_specs=(P(dp, SEQ, None), P(None, dp, SEQ, None), P(SEQ, None), P()),
        check_vma=False,
    )
```

```python
import functools
import math

import jax
import jax.numpy as jnp
import numpy as np
from jax import lax
from jax.experimental import pallas as pl
from jax.experimental.pallas import tpu as pltpu
from jax.sharding import Mesh, PartitionSpec as P

BF = jnp.bfloat16
F32 = jnp.float32
BLOCK = 256
HALF = 64
SENT_ROWS = BLOCK + 16
SEQ = ("x", "yl")
MOST = ("zh", "yh") + SEQ
DEPTH = ("zh", "zl", "yh")
CHIPS = DEPTH + SEQ


@functools.lru_cache(maxsize=None)
def tables():
    order = np.concatenate([np.arange(0, BLOCK, 2), np.arange(1, BLOCK, 2)])
    angle = np.pi * ((2 * order[:, None] + 1) * np.arange(BLOCK)[None, :] % 1024) / 512.0
    ahead = np.concatenate([np.cos(angle), -np.sin(angle)], axis=0)
    back = ahead.T / BLOCK

    def two(table):
        table = table.astype(np.float32)
        high = table.astype(jnp.bfloat16)
        return high, (table - high.astype(np.float32)).astype(jnp.bfloat16)

    return two(ahead) + two(back)


def mm(a, b):
    return jnp.dot(a, b, preferred_element_type=F32)


def low_lanes(rows):
    return lax.broadcasted_iota(jnp.int32, (rows, 128), 1) < HALF


def turned(x):
    return pltpu.roll(x, HALF, 1)


def pack_kernel(streams, out_grad, weight, filt, short, packed, grad, gate_out, pad):
    step = pl.program_id(0)
    low, low16 = low_lanes(BLOCK), low_lanes(16)

    @pl.when(step == 0)
    def _():
        grad[...] = jnp.zeros_like(grad)

    grad[...] += lax.dot_general(
        out_grad[...], weight[...], (((1,), (1,)), ((), ())), preferred_element_type=F32
    )

    for q in range(4):

        @pl.when(step == q)
        def _(q=q):
            lanes = slice(128 * q, 128 * q + 128)
            a, b = streams[1, :, lanes].astype(F32), streams[2, :, lanes].astype(F32)
            packed[2 * q, 0:BLOCK, 0:128] = jnp.where(low, a, turned(b)).astype(BF)
            packed[2 * q + 1, 0:BLOCK, 0:128] = jnp.where(low, turned(a), b).astype(BF)
            pad[0:8] = jnp.zeros((8, 128), F32)
            pad[8:] = streams[0, :, lanes].astype(F32)
            gate_out[:, lanes] = sum(
                short[j : j + 1, lanes] * pad[8 - j : 8 - j + BLOCK] for j in range(3)
            )

    @pl.when(step == pl.num_programs(0) - 1)
    def _():
        for q in range(4):
            lanes = slice(128 * q, 128 * q + 128)
            a, b = grad[:, lanes] * gate_out[:, lanes], filt[:, lanes]
            packed[2 * q, 0:BLOCK, 128:256] = jnp.where(low, a, turned(b)).astype(BF)
            packed[2 * q + 1, 0:BLOCK, 128:256] = jnp.where(low, turned(a), b).astype(BF)
            ends = streams[0, :, lanes].astype(F32)
            a = jnp.concatenate([ends[0:8], ends[BLOCK - 8 :]], axis=0)
            b = grad[0:16, lanes]
            packed[2 * q, BLOCK:, 0:128] = jnp.where(low16, a, turned(b)).astype(BF)
            packed[2 * q + 1, BLOCK:, 0:128] = jnp.where(low16, turned(a), b).astype(BF)
            packed[2 * q, BLOCK:, 128:256] = jnp.zeros((16, 128), BF)
            packed[2 * q + 1, BLOCK:, 128:256] = jnp.zeros((16, 128), BF)


def pack(streams, out_grad, weight, filt, short):
    steps = 4
    wide = out_grad.shape[1] // steps
    full = lambda *shape: pl.BlockSpec(shape, lambda k: (0,) * len(shape))
    return pl.pallas_call(
        pack_kernel,
        grid=(steps,),
        in_specs=[
            full(3, BLOCK, 512),
            pl.BlockSpec((BLOCK, wide), lambda k: (0, k)),
            pl.BlockSpec((512, wide), lambda k: (0, k)),
            full(BLOCK, 512),
            full(9, 512),
        ],
        out_specs=[full(8, SENT_ROWS, 256), full(BLOCK, 512), full(BLOCK, 512)],
        out_shape=[
            jax.ShapeDtypeStruct((8, SENT_ROWS, 256), BF),
            jax.ShapeDtypeStruct((BLOCK, 512), F32),
            jax.ShapeDtypeStruct((BLOCK, 512), F32),
        ],
        scratch_shapes=[pltpu.VMEM((8 + BLOCK, 128), F32)],
        name="pack",
    )(streams, out_grad, weight, filt, short)


def split(x):
    high = x.astype(BF)
    return high, (x - high.astype(F32)).astype(BF)


def apply(table_h, table_l, high, rest):
    return mm(table_h[...], high) + mm(table_h[...], rest) + mm(table_l[...], high)


def weights(place, short, skip):
    low1 = low_lanes(1)
    odd = place[0] % 2 == 1
    taps = short[...]
    taps = jnp.where(odd, turned(taps), taps)
    taps_up = turned(taps)
    gain = skip[...]
    gain = jnp.where(odd, turned(gain), gain)
    gain = jnp.where(low1, gain, turned(gain))

    def pair(first, second):
        def row(table, i, j):
            if i is None:
                return jnp.full((1, 128), 1.0 if j == 0 else 0.0, F32)
            return table[3 * i + j : 3 * i + j + 1]

        return [
            jnp.where(low1, row(taps, first, j), row(taps_up, second, j)) for j in range(3)
        ]

    return pair, gain


def prepare(got, pair, pad, prod, gates=None):
    taps = pair(1, 2)
    low = low_lanes(BLOCK)
    pad[0:8] = jnp.zeros((8, 128), F32)

    def load(b, carry):
        rows = pl.ds(pl.multiple_of(8 + BLOCK * b, 8), BLOCK)
        pad[rows] = got[b, 0:BLOCK, 0:128].astype(F32)
        return carry

    lax.fori_loop(0, 8, load, 0)
    for b in range(8):
        start = 8 + BLOCK * b
        s = sum(taps[j] * pad[start - j : start - j + BLOCK] for j in range(3))
        if gates is not None:
            gates[b] = s
        prod[b] = jnp.where(low, s * turned(s), turned(got[b, 0:BLOCK, 128:256].astype(F32)))
    low8 = low_lanes(8)
    gate = pair(0, None)
    for b in range(8):
        ends = got[b, BLOCK:, 0:128].astype(F32)
        first = got[b - 1, BLOCK:, 0:128].astype(F32)[8:] if b else jnp.zeros((8, 128), F32)
        pad[0:8] = first
        pad[8:16] = ends[0:8]
        out = sum(gate[j] * pad[8 - j : 16 - j] for j in range(3))
        prod[b, 0:8] = jnp.where(low8, prod[b, 0:8], turned(out) * ends[0:8])


def spectra(prod, ahead_h, ahead_l, spec):
    low = low_lanes(BLOCK)
    sigma = jnp.where(low, 1.0, -1.0)

    def transform(n, carry):
        x = jnp.concatenate(
            [jnp.where(low, prod[b], prod[7 - b]) for b in (2 * n, 2 * n + 1)], axis=1
        )
        out = apply(ahead_h, ahead_l, *split(x))
        for t in range(2):
            spec[2 * n + t, 0:BLOCK] = out[:BLOCK, 128 * t : 128 * t + 128]
            spec[2 * n + t, BLOCK:] = out[BLOCK:, 128 * t : 128 * t + 128] * sigma
        return carry

    lax.fori_loop(0, 4, transform, 0)


def over_bins(spec, use):
    for sign, base in ((1.0, 0), (-1.0, 128)):

        def step(n, carry, sign=sign, base=base):
            re = pl.ds(pl.multiple_of(base + 8 * n, 8), 8)
            im = pl.ds(pl.multiple_of(BLOCK + base + 8 * n, 8), 8)
            own = [(spec[j, re], spec[j, im]) for j in range(8)]
            both = [own[0]]
            for j in range(1, 8):
                both.append(
                    (own[j][0] - sign * own[j - 1][1], own[j][1] + sign * own[j - 1][0])
                )
            use(re, im, own, both)
            return carry

        lax.fori_loop(0, 16, step, 0)


def summed(pairs):
    first = True
    for (ar, ai), (br, bi) in pairs:
        pr = ar * br - ai * bi
        pi = ar * bi + ai * br
        tr, ti = (pr, pi) if first else (tr + pr, ti + pi)
        first = False
    return tr, ti


def flipped(x, sign):
    return jnp.concatenate([x[0:BLOCK], x[BLOCK:] * sign], axis=0)


def conv_kernel(
    place, got, short, skip, ahead_h, ahead_l, back_h, back_l,
    sent,
    pad, prod, gates, spec, fspec, res, time, after,
):
    low = low_lanes(BLOCK)
    sigma = jnp.where(low, 1.0, -1.0)
    pair, gain = weights(place, short, skip)

    def filters(n, carry):
        def blocks(b):
            x, y = (got[n, 0:BLOCK, 128:256].astype(F32) for n in (b, b + 1))
            return jnp.where(low, turned(x), y).astype(BF)

        f = jnp.concatenate([blocks(4 * n), blocks(4 * n + 2)], axis=1)
        out = mm(ahead_h[...], f) + mm(ahead_l[...], f)
        low512 = low_lanes(512)
        for t in range(2):
            x = out[:, 128 * t : 128 * t + 128]
            y = turned(x)
            fspec[4 * n + 2 * t] = jnp.where(low512, x, y)
            fspec[4 * n + 2 * t + 1] = jnp.where(low512, y, x)
        return carry

    lax.fori_loop(0, 2, filters, 0)
    prepare(got, pair, pad, prod, gates)
    spectra(prod, ahead_h, ahead_l, spec)

    def multiply(re, im, own, both):
        filt = [(fspec[m, re], fspec[m, im]) for m in range(8)]
        for i in range(8):
            tr, ti = summed([(filt[m], both[i - m]) for m in range(i + 1)])
            res[i, re] = tr
            res[i, im] = ti

    over_bins(spec, multiply)

    def invert(n, carry):
        x = jnp.concatenate([flipped(res[b], sigma) for b in (2 * n, 2 * n + 1)], axis=1)
        out = apply(back_h, back_l, *split(x))
        time[2 * n] = out[:, :128]
        time[2 * n + 1] = out[:, 128:]
        return carry

    lax.fori_loop(0, 4, invert, 0)

    low128 = low_lanes(128)

    def gate(b, carry):
        t = jnp.where(low, time[b], time[7 - b]) + gain * prod[b]
        rows = pl.ds(pl.multiple_of(BLOCK * b, 8), BLOCK)
        after[rows] = jnp.where(low, turned(t), t) * turned(gates[b])
        sent[b, BLOCK:384] = jnp.where(low128, t[0:128], turned(t[128:256])).astype(BF)
        return carry

    lax.fori_loop(0, 8, gate, 0)
    low8 = low_lanes(8)
    for b in range(8):
        if b < 7:
            t = jnp.where(low8, time[b + 1, 0:8], time[6 - b, 0:8]) + gain * prod[b + 1, 0:8]
        else:
            t = jnp.zeros((8, 128), F32)
        sent[b, 384:400] = jnp.concatenate([t, t], axis=0).astype(BF)
    after[8 * BLOCK :] = jnp.zeros((8, 128), F32)
    taps = pair(1, 2)
    for b in range(8):
        start = BLOCK * b
        y = sum(taps[j] * after[start + j : start + j + BLOCK] for j in range(3))
        sent[b, 0:BLOCK] = y.astype(BF)


def lag_kernel(
    place, got, short, skip, ahead_h, ahead_l, back_h, back_l,
    lags, lags_z,
    pad, prod, spec, lres, rows,
):
    pair, _ = weights(place, short, skip)
    prepare(got, pair, pad, prod)
    spectra(prod, ahead_h, ahead_l, spec)
    zero = jnp.zeros((8, 128), F32)
    low8 = low_lanes(8)

    def multiply(re, im, own, both):
        grads, shifted = [], []
        for i in range(8):
            grads.append(
                tuple(jnp.where(low8, turned(own[7 - i][k]), own[7 - i][k]) for k in range(2))
            )
            before = both[i - 1] if i else (zero, zero)
            shifted.append(
                tuple(jnp.where(low8, before[k], turned(both[i][k])) for k in range(2))
            )
        for a in range(4):
            tr, ti = summed([(grads[i], shifted[i - 2 * a]) for i in range(2 * a, 8)])
            lres[a, re] = tr
            lres[a, im] = ti

    over_bins(spec, multiply)

    def invert(n, carry):
        x = jnp.concatenate([flipped(lres[a], -1.0) for a in (2 * n, 2 * n + 1)], axis=1)
        out = apply(back_h, back_l, *split(x))
        for t in range(2):
            for k in range(4):
                there = pl.ds(8 * n + 4 * t + k, 64, stride=16)
                rows[there, :] = out[64 * k : 64 * k + 64, 128 * t : 128 * t + 128]
        return carry

    for n in range(2):
        invert(n, 0)
    for z in range(2):
        for ref, side in ((lags, place[1]), (lags_z, 1 - place[1])):
            part = rows[pl.ds(pl.multiple_of(512 * z + 256 * side, 256), 256), :]
            ref[16 * z : 16 * z + 16] = part.reshape(16, 16, 128).astype(BF)


def on_channels(kernel, name, inputs, in_shapes, outputs, scratch, cost):
    full = lambda *shape: pl.BlockSpec(shape, lambda n, p: (0,) * len(shape))
    return pl.pallas_call(
        kernel,
        grid_spec=pltpu.PrefetchScalarGridSpec(
            num_scalar_prefetch=1,
            grid=(1,),
            in_specs=[
                full(8, SENT_ROWS, 256),
                pl.BlockSpec((9, 128), lambda n, p: (0, p[0] // 2)),
                pl.BlockSpec((1, 128), lambda n, p: (0, p[0] // 2)),
            ]
            + [full(*shape) for shape in in_shapes],
            out_specs=[full(*shape) for shape, _ in outputs],
            scratch_shapes=[
                pltpu.VMEM(shape, dtype)
                for shape, dtype in [((8 + 8 * BLOCK, 128), F32)] + scratch
            ],
        ),
        out_shape=[jax.ShapeDtypeStruct(shape, dtype) for shape, dtype in outputs],
        cost_estimate=cost,
        name=name,
    )(*inputs)


TABLES = [(512, BLOCK), (512, BLOCK), (BLOCK, 512), (BLOCK, 512)]
BLOCKS = ((8, BLOCK, 128), F32)
BINS = ((8, 512, 128), F32)


def spent(flops):
    return pl.CostEstimate(flops=flops, bytes_accessed=3 * 10**6, transcendentals=0)


def conv(place, got, short, skip):
    inputs = (place, got, short, skip, *(jnp.asarray(t) for t in tables()))
    outputs = [((8, 400, 128), BF)]
    scratch = [BLOCKS, BLOCKS, BINS, BINS, BINS, BLOCKS, ((8 * BLOCK + 8, 128), F32)]
    return on_channels(conv_kernel, "conv", inputs, TABLES, outputs, scratch, None)[0]


def lag_sums(place, got, short, skip):
    inputs = (place, got, short, skip, *(jnp.asarray(t) for t in tables()))
    outputs = [((32, 16, 128), BF)] * 2
    scratch = [BLOCKS, BINS, ((4, 512, 128), F32), ((1024, 128), F32)]
    cost = spent(2 * 10**9)
    return on_channels(lag_kernel, "lag_sums", inputs, TABLES, outputs, scratch, cost)


def convolved(got, q, start, low128):
    there = slice(start, start + 128)
    a, b = got[2 * q, there].astype(F32), got[2 * q + 1, there].astype(F32)
    return jnp.where(low128, a, turned(b)), jnp.where(low128, turned(a), b)


def mixed_kernel(got, gate_out, edge, short, mixed, pad):
    low128 = low_lanes(128)
    pad[0:8] = edge[...].astype(F32)
    pad[8:] = jnp.zeros((8, 512), F32)
    more = sum(short[j : j + 1] * pad[8 - j : 16 - j] for j in (1, 2))
    for q in range(4):
        lanes = slice(128 * q, 128 * q + 128)
        first, second = convolved(got, q, 0, low128)
        gate = gate_out[0:128, lanes]
        gate = jnp.concatenate([gate[0:8] + more[:, lanes], gate[8:]], axis=0)
        mixed[0:128, lanes] = (gate * first).astype(BF)
        mixed[128:256, lanes] = (gate_out[128:256, lanes] * second).astype(BF)


def unpack_mixed(got, gate_out, edge, short):
    full = lambda *shape: pl.BlockSpec(shape, lambda n: (0,) * len(shape))
    return pl.pallas_call(
        mixed_kernel,
        grid=(1,),
        in_specs=[
            pl.BlockSpec((8, 128, 128), lambda n: (0, 2, 0)),
            full(BLOCK, 512),
            full(8, 512),
            full(9, 512),
        ],
        out_specs=full(BLOCK, 512),
        out_shape=jax.ShapeDtypeStruct((BLOCK, 512), BF),
        scratch_shapes=[pltpu.VMEM((16, 512), F32)],
        name="unpack_mixed",
    )(got, gate_out, edge, short)


def grads_kernel(got, grad, later, short, grads, pad):
    low, low128, low8 = low_lanes(BLOCK), low_lanes(128), low_lanes(8)
    for q in range(4):
        lanes = slice(128 * q, 128 * q + 128)
        first, second = convolved(got, q, BLOCK, low128)
        pad[0:128, lanes] = grad[0:128, lanes] * first
        pad[128:256, lanes] = grad[128:256, lanes] * second
        a, b = (got[2 * q + n, 384:400].astype(F32)[0:8] for n in range(2))
        pad[256:264, lanes] = later[:, lanes] * jnp.where(low8, a, turned(b))
        a, b = got[2 * q, 0:BLOCK].astype(F32), got[2 * q + 1, 0:BLOCK].astype(F32)
        grads[1, :, lanes] = jnp.where(low, a, turned(b)).astype(BF)
        grads[2, :, lanes] = jnp.where(low, turned(a), b).astype(BF)
        grads[0, :, lanes] = sum(
            short[j : j + 1, lanes] * pad[j : j + BLOCK, lanes] for j in range(3)
        ).astype(BF)


def unpack_grads(got, grad, later, short):
    return pl.pallas_call(
        grads_kernel,
        out_shape=jax.ShapeDtypeStruct((3, BLOCK, 512), BF),
        scratch_shapes=[pltpu.VMEM((BLOCK + 8, 512), F32)],
        cost_estimate=pl.CostEstimate(flops=10**6, bytes_accessed=2 * 10**6, transcendentals=0),
        name="unpack_grads",
    )(got, grad, later, short)


def partial_kernel(place, m00, m01, m10, m11, g00, g01, g10, g11, lags, lags_z, packed):
    def term(mixed, grad):
        return lax.dot_general(
            mixed[...], grad[...], (((0,), (0,)), ((), ())), preferred_element_type=F32
        )

    part = term(m00, g00) + term(m01, g01) + term(m10, g10) + term(m11, g11)
    part = part.astype(BF)
    for n in range(32):
        packed[n, :, 0:1024] = part[16 * n : 16 * n + 16]
        lag = lags[n].astype(F32) + lags_z[n].astype(F32)
        packed[n, :, 1024:1152] = lag.astype(BF)


def partial(place, mixed, grad, grads, lags, lags_z):
    full = lambda *shape: pl.BlockSpec(shape, lambda n, p: (0,) * len(shape))
    return pl.pallas_call(
        partial_kernel,
        grid_spec=pltpu.PrefetchScalarGridSpec(
            num_scalar_prefetch=1,
            grid=(1,),
            in_specs=[full(BLOCK, 512)] * 4
            + [pl.BlockSpec((BLOCK, 1024), lambda n, p: (0, p[0]))]
            + [full(BLOCK, 1024)] * 3
            + [full(32, 16, 128)] * 2,
            out_specs=full(32, 16, 1152),
        ),
        out_shape=jax.ShapeDtypeStruct((32, 16, 1152), BF),
        name="partial",
    )(place, *mixed, grad, *grads, lags, lags_z)


def reduce_kernel(scale, got, shared, lags):
    total = jnp.zeros((16, 1024), F32)
    for n in range(32):
        total = total + got[n, :, 0:1024].astype(F32)
    total = (total * scale).astype(BF)
    low = low_lanes(16)
    for q in range(4):
        a, b = (
            sum(got[8 * k + s, :, 1024:1152].astype(F32) for k in range(4))
            for s in (2 * q, 2 * q + 1)
        )
        sides = (jnp.where(low, turned(a), b), jnp.where(low, a, turned(b)))
        for s in range(8):
            start = 4 * (s // 2)
            lags[s, 4 * q : 4 * q + 4] = sides[s % 2][start : start + 4] * scale
    for n in range(64):
        shared[n, :, 0:1024] = total
        shared[n, :, 1024:1152] = lags[n % 8].astype(BF)


def reduce(got, scale):
    return pl.pallas_call(
        functools.partial(reduce_kernel, scale),
        out_shape=jax.ShapeDtypeStruct((64, 16, 1152), BF),
        scratch_shapes=[pltpu.VMEM((8, 16, 128), F32)],
        name="reduce",
    )(got)


def start_writes(place, rows, grad_weight, wide, sems):
    copies = []
    for n in range(8):
        zh, zl, yh = n // 4, n // 2 % 2, n % 2
        for k in range(8):
            wide[n, 16 * k : 16 * k + 16] = rows[8 * n + k].astype(F32)
        there = slice(128 * (2 * zh + yh), 128 * (2 * zh + yh) + 128)
        lanes = pl.ds(pl.multiple_of(2048 * place[0] + 1024 * zl, 1024), 1024)
        copies.append(
            pltpu.make_async_copy(wide.at[n], grad_weight.at[there, lanes], sems.at[n])
        )
        copies[-1].start()
    return copies


def first_kernel(place, rows, grad_weight, wide, sems):
    for copy in start_writes(place, rows, grad_weight, wide, sems):
        copy.wait()


def last_kernel(place, rows, lags, lags_c, whole, grad_weight, grad_filter, wide, sems, sums):
    copies = start_writes(place, rows, grad_weight, wide, sems)
    total = lags[...].astype(F32) + lags_c[...].astype(F32)
    sums[...] = total.reshape(1024, 128)
    for q in range(4):
        for k in range(4):
            part = sums[pl.ds(4 * q + k, 64, stride=16), :]
            grad_filter[64 * k : 64 * k + 64, 128 * q : 128 * q + 128] = part
    for copy in copies:
        copy.wait()


def write_half(half, rows, mine=None, whole=None):
    last = whole is not None
    rows_spec = pl.BlockSpec((64, 16, 1024), lambda n, p: (0, 0, 0))
    lags_spec = pl.BlockSpec((64, 16, 128), lambda n, p: (0, 0, 8))
    hbm = pl.BlockSpec(memory_space=pltpu.HBM)
    shapes = [jax.ShapeDtypeStruct((512, 4096), F32)]
    scratch = [pltpu.VMEM((8, 128, 1024), F32), pltpu.SemaphoreType.DMA((8,))]
    if last:
        shapes.append(jax.ShapeDtypeStruct((BLOCK, 512), F32))
        scratch.append(pltpu.VMEM((1024, 128), F32))
    return pl.pallas_call(
        last_kernel if last else first_kernel,
        grid_spec=pltpu.PrefetchScalarGridSpec(
            num_scalar_prefetch=1,
            grid=(1,),
            in_specs=[rows_spec] + [lags_spec, lags_spec, hbm] * last,
            out_specs=[hbm] + [pl.BlockSpec((BLOCK, 512), lambda n, p: (0, 0))] * last,
            scratch_shapes=scratch,
        ),
        out_shape=shapes,
        input_output_aliases={4: 0} if last else {},
        cost_estimate=pl.CostEstimate(flops=10**6, bytes_accessed=6 * 10**6, transcendentals=0),
        name="write_last" if last else "write_first",
    )(half, rows, *([rows, mine, whole] if last else []))


def exchange(x, axes):
    return lax.all_to_all(x, axes, 0, 0, tiled=True)


def across(x):
    return lax.ppermute(x, "c", [(0, 1), (1, 0)])


def along(x, step):
    return lax.ppermute(x, SEQ, [(n, n + step) for n in range(8) if 0 <= n + step < 8])


def above(x):
    return lax.ppermute(x, "zl", [(0, 1), (1, 0)])


def opposite(x):
    return lax.ppermute(x, ("zl", "c"), [(n, 3 - n) for n in range(4)])


def on_device(streams, short_filter, long_filter, skip_gain, out_weight, out_grad):
    scale = 1.0 / math.sqrt(16 * 2048)
    core = lax.axis_index("c").astype(jnp.int32)
    side = lax.axis_index("zl").astype(jnp.int32)
    seq = lax.axis_index(SEQ).astype(jnp.int32)
    grad = out_grad[0]

    def quarter(c, z):
        return lax.dynamic_slice(grad, (0, 1024 * (2 * c + z)), (BLOCK, 1024))

    grads = (
        above(quarter(core, 1 - side)),
        across(quarter(1 - core, side)),
        opposite(quarter(1 - core, 1 - side)),
    )
    short = short_filter.reshape(9, 512)
    packed, grad_mixed, gate_out = pack(streams[:, 0], grad, out_weight, long_filter, short)
    got = exchange(packed, SEQ)
    edge = along(streams[0, 0, BLOCK - 8 :], 1)
    later = along(grad_mixed[:8], -1)
    place = jnp.stack([seq, side])
    gain = skip_gain.reshape(1, 512)
    sent = conv(place, got, short, gain)
    sent, got, grads, edge, later = lax.optimization_barrier((sent, got, grads, edge, later))
    lags_own, lags = lag_sums(place, got, short, gain)
    lags_z = above(lags)
    back = exchange(sent, SEQ)
    back, lags_own, lags_z = lax.optimization_barrier((back, lags_own, lags_z))
    m00 = unpack_mixed(back, gate_out, edge, short)
    m01, m10 = above(m00), across(m00)
    mixed = (m00, m01, m10, across(m01))
    part = partial((2 * core + side)[None], mixed, grad, grads, lags_own, lags_z)
    part, m00, back = lax.optimization_barrier((part, m00, back))
    part = exchange(part, MOST)
    layer_out = jnp.dot(m00, out_weight, preferred_element_type=F32).astype(BF)
    part, m00, layer_out = lax.optimization_barrier((part, m00, layer_out))
    rows, back = lax.optimization_barrier((reduce(part, scale), back))
    mine = exchange(rows, CHIPS)
    grad_streams = unpack_grads(back, grad_mixed, later, short)
    mine, grad_streams = lax.optimization_barrier((mine, grad_streams))
    theirs = across(mine)
    grad_weight = write_half(core[None], mine)[0]
    grad_weight, grad_filter = write_half(1 - core[None], theirs, mine, grad_weight)
    return layer_out[None], grad_streams[:, None], grad_filter, grad_weight


def solution(mesh):
    fine = Mesh(
        mesh.devices.reshape(2, 2, 2, 2, 4, 2), ("zh", "zl", "yh", "c", "x", "yl")
    )
    dp = ("zh", "zl", "yh", "c")
    placed = (P(None, dp, SEQ, None), P(), P(SEQ, None), P(), P(), P(dp, SEQ, None))
    return jax.shard_map(
        on_device,
        mesh=fine,
        in_specs=placed,
        out_specs=(P(dp, SEQ, None), P(None, dp, SEQ, None), P(SEQ, None), P()),
        check_vma=False,
    )
```

```python
import functools
import math

import jax
import jax.numpy as jnp
import numpy as np
from jax import lax
from jax.experimental import pallas as pl
from jax.experimental.pallas import tpu as pltpu
from jax.sharding import Mesh, PartitionSpec as P

BF = jnp.bfloat16
F32 = jnp.float32
BLOCK = 256
HALF = 64
SENT_ROWS = BLOCK + 16
SEQ = ("x", "yl")
MOST = ("zh", "yh") + SEQ
DEPTH = ("zh", "zl", "yh")
CHIPS = DEPTH + SEQ


@functools.lru_cache(maxsize=None)
def tables():
    order = np.concatenate([np.arange(0, BLOCK, 2), np.arange(1, BLOCK, 2)])
    angle = np.pi * ((2 * order[:, None] + 1) * np.arange(BLOCK)[None, :] % 1024) / 512.0
    ahead = np.concatenate([np.cos(angle), -np.sin(angle)], axis=0)
    back = ahead.T / BLOCK

    def two(table):
        table = table.astype(np.float32)
        high = table.astype(jnp.bfloat16)
        return high, (table - high.astype(np.float32)).astype(jnp.bfloat16)

    return two(ahead) + two(back)


def mm(a, b):
    return jnp.dot(a, b, preferred_element_type=F32)


def low_lanes(rows):
    return lax.broadcasted_iota(jnp.int32, (rows, 128), 1) < HALF


def turned(x):
    return pltpu.roll(x, HALF, 1)


def pack_kernel(streams, out_grad, weight, filt, short, packed, grad, gate_out, pad):
    step = pl.program_id(0)
    low, low16 = low_lanes(BLOCK), low_lanes(16)

    @pl.when(step == 0)
    def _():
        grad[...] = jnp.zeros_like(grad)

    grad[...] += lax.dot_general(
        out_grad[...], weight[...], (((1,), (1,)), ((), ())), preferred_element_type=F32
    )

    for q in range(4):

        @pl.when(step == q)
        def _(q=q):
            lanes = slice(128 * q, 128 * q + 128)
            a, b = streams[1, :, lanes].astype(F32), streams[2, :, lanes].astype(F32)
            packed[2 * q, 0:BLOCK, 0:128] = jnp.where(low, a, turned(b)).astype(BF)
            packed[2 * q + 1, 0:BLOCK, 0:128] = jnp.where(low, turned(a), b).astype(BF)
            pad[0:8] = jnp.zeros((8, 128), F32)
            pad[8:] = streams[0, :, lanes].astype(F32)
            gate_out[:, lanes] = sum(
                short[0, j : j + 1, lanes] * pad[8 - j : 8 - j + BLOCK] for j in range(3)
            )

    @pl.when(step == pl.num_programs(0) - 1)
    def _():
        for q in range(4):
            lanes = slice(128 * q, 128 * q + 128)
            a, b = grad[:, lanes] * gate_out[:, lanes], filt[:, lanes]
            packed[2 * q, 0:BLOCK, 128:256] = jnp.where(low, a, turned(b)).astype(BF)
            packed[2 * q + 1, 0:BLOCK, 128:256] = jnp.where(low, turned(a), b).astype(BF)
            ends = streams[0, :, lanes].astype(F32)
            a = jnp.concatenate([ends[0:8], ends[BLOCK - 8 :]], axis=0)
            b = grad[0:16, lanes]
            packed[2 * q, BLOCK:, 0:128] = jnp.where(low16, a, turned(b)).astype(BF)
            packed[2 * q + 1, BLOCK:, 0:128] = jnp.where(low16, turned(a), b).astype(BF)
            packed[2 * q, BLOCK:, 128:256] = jnp.zeros((16, 128), BF)
            packed[2 * q + 1, BLOCK:, 128:256] = jnp.zeros((16, 128), BF)


def pack(streams, out_grad, weight, filt, short):
    steps = 4
    wide = out_grad.shape[1] // steps
    full = lambda *shape: pl.BlockSpec(shape, lambda k: (0,) * len(shape))
    return pl.pallas_call(
        pack_kernel,
        grid=(steps,),
        in_specs=[
            full(3, BLOCK, 512),
            pl.BlockSpec((BLOCK, wide), lambda k: (0, k)),
            pl.BlockSpec((512, wide), lambda k: (0, k)),
            full(BLOCK, 512),
            full(3, 3, 512),
        ],
        out_specs=[full(8, SENT_ROWS, 256), full(BLOCK, 512), full(BLOCK, 512)],
        out_shape=[
            jax.ShapeDtypeStruct((8, SENT_ROWS, 256), BF),
            jax.ShapeDtypeStruct((BLOCK, 512), F32),
            jax.ShapeDtypeStruct((BLOCK, 512), F32),
        ],
        scratch_shapes=[pltpu.VMEM((8 + BLOCK, 128), F32)],
        name="pack",
    )(streams, out_grad, weight, filt, short)


def split(x):
    high = x.astype(BF)
    return high, (x - high.astype(F32)).astype(BF)


def apply(table_h, table_l, high, rest):
    return mm(table_h[...], high) + mm(table_h[...], rest) + mm(table_l[...], high)


def weights(place, short, skip):
    low1 = low_lanes(1)
    odd = place[0] % 2 == 1
    taps = jnp.concatenate([short[n] for n in range(3)], axis=0)
    taps = jnp.where(odd, turned(taps), taps)
    taps_up = turned(taps)
    gain = skip[...]
    gain = jnp.where(odd, turned(gain), gain)
    gain = jnp.where(low1, gain, turned(gain))

    def pair(first, second):
        def row(table, i, j):
            if i is None:
                return jnp.full((1, 128), 1.0 if j == 0 else 0.0, F32)
            return table[3 * i + j : 3 * i + j + 1]

        return [
            jnp.where(low1, row(taps, first, j), row(taps_up, second, j)) for j in range(3)
        ]

    return pair, gain


def prepare(got, pair, pad, prod, gates=None):
    taps = pair(1, 2)
    low = low_lanes(BLOCK)
    pad[0:8] = jnp.zeros((8, 128), F32)

    def load(b, carry):
        rows = pl.ds(pl.multiple_of(8 + BLOCK * b, 8), BLOCK)
        pad[rows] = got[b, 0:BLOCK, 0:128].astype(F32)
        return carry

    lax.fori_loop(0, 8, load, 0)
    for b in range(8):
        start = 8 + BLOCK * b
        s = sum(taps[j] * pad[start - j : start - j + BLOCK] for j in range(3))
        if gates is not None:
            gates[b] = s
        prod[b] = jnp.where(low, s * turned(s), turned(got[b, 0:BLOCK, 128:256].astype(F32)))
    low8 = low_lanes(8)
    gate = pair(0, None)
    for b in range(8):
        ends = got[b, BLOCK:, 0:128].astype(F32)
        first = got[b - 1, BLOCK:, 0:128].astype(F32)[8:] if b else jnp.zeros((8, 128), F32)
        pad[0:8] = first
        pad[8:16] = ends[0:8]
        out = sum(gate[j] * pad[8 - j : 16 - j] for j in range(3))
        prod[b, 0:8] = jnp.where(low8, prod[b, 0:8], turned(out) * ends[0:8])


def spectra(prod, ahead_h, ahead_l, spec):
    low = low_lanes(BLOCK)
    sigma = jnp.where(low, 1.0, -1.0)

    def transform(n, carry):
        x = jnp.concatenate(
            [jnp.where(low, prod[b], prod[7 - b]) for b in (2 * n, 2 * n + 1)], axis=1
        )
        out = apply(ahead_h, ahead_l, *split(x))
        for t in range(2):
            spec[2 * n + t, 0:BLOCK] = out[:BLOCK, 128 * t : 128 * t + 128]
            spec[2 * n + t, BLOCK:] = out[BLOCK:, 128 * t : 128 * t + 128] * sigma
        return carry

    lax.fori_loop(0, 4, transform, 0)


def over_bins(spec, use):
    for sign, base in ((1.0, 0), (-1.0, 128)):

        def step(n, carry, sign=sign, base=base):
            re = pl.ds(pl.multiple_of(base + 8 * n, 8), 8)
            im = pl.ds(pl.multiple_of(BLOCK + base + 8 * n, 8), 8)
            own = [(spec[j, re], spec[j, im]) for j in range(8)]
            both = [own[0]]
            for j in range(1, 8):
                both.append(
                    (own[j][0] - sign * own[j - 1][1], own[j][1] + sign * own[j - 1][0])
                )
            use(re, im, own, both)
            return carry

        lax.fori_loop(0, 16, step, 0)


def summed(pairs):
    first = True
    for (ar, ai), (br, bi) in pairs:
        pr = ar * br - ai * bi
        pi = ar * bi + ai * br
        tr, ti = (pr, pi) if first else (tr + pr, ti + pi)
        first = False
    return tr, ti


def flipped(x, sign):
    return jnp.concatenate([x[0:BLOCK], x[BLOCK:] * sign], axis=0)


def conv_kernel(
    place, got, short, skip, ahead_h, ahead_l, back_h, back_l,
    sent,
    pad, prod, gates, spec, fspec, res, time, after,
):
    low = low_lanes(BLOCK)
    sigma = jnp.where(low, 1.0, -1.0)
    pair, gain = weights(place, short, skip)

    def filters(n, carry):
        def blocks(b):
            x, y = (got[n, 0:BLOCK, 128:256].astype(F32) for n in (b, b + 1))
            return jnp.where(low, turned(x), y).astype(BF)

        f = jnp.concatenate([blocks(4 * n), blocks(4 * n + 2)], axis=1)
        out = mm(ahead_h[...], f) + mm(ahead_l[...], f)
        low512 = low_lanes(512)
        for t in range(2):
            x = out[:, 128 * t : 128 * t + 128]
            y = turned(x)
            fspec[4 * n + 2 * t] = jnp.where(low512, x, y)
            fspec[4 * n + 2 * t + 1] = jnp.where(low512, y, x)
        return carry

    lax.fori_loop(0, 2, filters, 0)
    prepare(got, pair, pad, prod, gates)
    spectra(prod, ahead_h, ahead_l, spec)

    def multiply(re, im, own, both):
        filt = [(fspec[m, re], fspec[m, im]) for m in range(8)]
        for i in range(8):
            tr, ti = summed([(filt[m], both[i - m]) for m in range(i + 1)])
            res[i, re] = tr
            res[i, im] = ti

    over_bins(spec, multiply)

    def invert(n, carry):
        x = jnp.concatenate([flipped(res[b], sigma) for b in (2 * n, 2 * n + 1)], axis=1)
        out = apply(back_h, back_l, *split(x))
        time[2 * n] = out[:, :128]
        time[2 * n + 1] = out[:, 128:]
        return carry

    lax.fori_loop(0, 4, invert, 0)

    low128 = low_lanes(128)

    def gate(b, carry):
        t = jnp.where(low, time[b], time[7 - b]) + gain * prod[b]
        rows = pl.ds(pl.multiple_of(BLOCK * b, 8), BLOCK)
        after[rows] = jnp.where(low, turned(t), t) * turned(gates[b])
        sent[b, BLOCK:384] = jnp.where(low128, t[0:128], turned(t[128:256])).astype(BF)
        return carry

    lax.fori_loop(0, 8, gate, 0)
    low8 = low_lanes(8)
    for b in range(8):
        if b < 7:
            t = jnp.where(low8, time[b + 1, 0:8], time[6 - b, 0:8]) + gain * prod[b + 1, 0:8]
        else:
            t = jnp.zeros((8, 128), F32)
        sent[b, 384:400] = jnp.concatenate([t, t], axis=0).astype(BF)
    after[8 * BLOCK :] = jnp.zeros((8, 128), F32)
    taps = pair(1, 2)
    for b in range(8):
        start = BLOCK * b
        y = sum(taps[j] * after[start + j : start + j + BLOCK] for j in range(3))
        sent[b, 0:BLOCK] = y.astype(BF)


def lag_kernel(
    place, got, short, skip, ahead_h, ahead_l, back_h, back_l,
    lags, lags_z,
    pad, prod, spec, lres, rows,
):
    pair, _ = weights(place, short, skip)
    prepare(got, pair, pad, prod)
    spectra(prod, ahead_h, ahead_l, spec)
    zero = jnp.zeros((8, 128), F32)
    low8 = low_lanes(8)

    def multiply(re, im, own, both):
        grads, shifted = [], []
        for i in range(8):
            grads.append(
                tuple(jnp.where(low8, turned(own[7 - i][k]), own[7 - i][k]) for k in range(2))
            )
            before = both[i - 1] if i else (zero, zero)
            shifted.append(
                tuple(jnp.where(low8, before[k], turned(both[i][k])) for k in range(2))
            )
        for a in range(4):
            tr, ti = summed([(grads[i], shifted[i - 2 * a]) for i in range(2 * a, 8)])
            lres[a, re] = tr
            lres[a, im] = ti

    over_bins(spec, multiply)

    def invert(n, carry):
        x = jnp.concatenate([flipped(lres[a], -1.0) for a in (2 * n, 2 * n + 1)], axis=1)
        out = apply(back_h, back_l, *split(x))
        for t in range(2):
            for k in range(4):
                there = pl.ds(8 * n + 4 * t + k, 64, stride=16)
                rows[there, :] = out[64 * k : 64 * k + 64, 128 * t : 128 * t + 128]
        return carry

    for n in range(2):
        invert(n, 0)
    for z in range(2):
        for ref, side in ((lags, place[1]), (lags_z, 1 - place[1])):
            part = rows[pl.ds(pl.multiple_of(512 * z + 256 * side, 256), 256), :]
            ref[16 * z : 16 * z + 16] = part.reshape(16, 16, 128).astype(BF)


def on_channels(kernel, name, inputs, in_shapes, outputs, scratch, cost):
    full = lambda *shape: pl.BlockSpec(shape, lambda n, p: (0,) * len(shape))
    return pl.pallas_call(
        kernel,
        grid_spec=pltpu.PrefetchScalarGridSpec(
            num_scalar_prefetch=1,
            grid=(1,),
            in_specs=[
                full(8, SENT_ROWS, 256),
                pl.BlockSpec((3, 3, 128), lambda n, p: (0, 0, p[0] // 2)),
                pl.BlockSpec((1, 128), lambda n, p: (0, p[0] // 2)),
            ]
            + [full(*shape) for shape in in_shapes],
            out_specs=[full(*shape) for shape, _ in outputs],
            scratch_shapes=[
                pltpu.VMEM(shape, dtype)
                for shape, dtype in [((8 + 8 * BLOCK, 128), F32)] + scratch
            ],
        ),
        out_shape=[jax.ShapeDtypeStruct(shape, dtype) for shape, dtype in outputs],
        cost_estimate=cost,
        name=name,
    )(*inputs)


TABLES = [(512, BLOCK), (512, BLOCK), (BLOCK, 512), (BLOCK, 512)]
BLOCKS = ((8, BLOCK, 128), F32)
BINS = ((8, 512, 128), F32)


def spent(flops):
    return pl.CostEstimate(flops=flops, bytes_accessed=3 * 10**6, transcendentals=0)


def conv(place, got, short, skip):
    inputs = (place, got, short, skip, *(jnp.asarray(t) for t in tables()))
    outputs = [((8, 400, 128), BF)]
    scratch = [BLOCKS, BLOCKS, BINS, BINS, BINS, BLOCKS, ((8 * BLOCK + 8, 128), F32)]
    return on_channels(conv_kernel, "conv", inputs, TABLES, outputs, scratch, None)[0]


def lag_sums(place, got, short, skip):
    inputs = (place, got, short, skip, *(jnp.asarray(t) for t in tables()))
    outputs = [((32, 16, 128), BF)] * 2
    scratch = [BLOCKS, BINS, ((4, 512, 128), F32), ((1024, 128), F32)]
    cost = spent(2 * 10**9)
    return on_channels(lag_kernel, "lag_sums", inputs, TABLES, outputs, scratch, cost)


def convolved(got, q, start, low128):
    there = slice(start, start + 128)
    a, b = got[2 * q, there].astype(F32), got[2 * q + 1, there].astype(F32)
    return jnp.where(low128, a, turned(b)), jnp.where(low128, turned(a), b)


def mixed_kernel(got, gate_out, edge, short, lags, mixed, joined, pad):
    low128 = low_lanes(128)
    pad[0:8] = edge[...].astype(F32)
    pad[8:] = jnp.zeros((8, 512), F32)
    more = sum(short[0, j : j + 1] * pad[8 - j : 16 - j] for j in (1, 2))
    for q in range(4):
        lanes = slice(128 * q, 128 * q + 128)
        first, second = convolved(got, q, 0, low128)
        gate = gate_out[0:128, lanes]
        gate = jnp.concatenate([gate[0:8] + more[:, lanes], gate[8:]], axis=0)
        for ref in (mixed, joined):
            ref[0:128, lanes] = (gate * first).astype(BF)
            ref[128:256, lanes] = (gate_out[128:256, lanes] * second).astype(BF)
    for n in range(32):
        start, lane = 16 * (n % 16), 512 + 128 * (n // 16)
        joined[start : start + 16, lane : lane + 128] = lags[n]


def unpack_mixed(got, gate_out, edge, short, lags):
    full = lambda *shape: pl.BlockSpec(shape, lambda n: (0,) * len(shape))
    return pl.pallas_call(
        mixed_kernel,
        grid=(1,),
        in_specs=[
            pl.BlockSpec((8, 128, 128), lambda n: (0, 2, 0)),
            full(BLOCK, 512),
            full(8, 512),
            full(3, 3, 512),
            full(32, 16, 128),
        ],
        out_specs=[full(BLOCK, 512), full(BLOCK, 768)],
        out_shape=[
            jax.ShapeDtypeStruct((BLOCK, 512), BF),
            jax.ShapeDtypeStruct((BLOCK, 768), BF),
        ],
        scratch_shapes=[pltpu.VMEM((16, 512), F32)],
        name="unpack_mixed",
    )(got, gate_out, edge, short, lags)


def grads_kernel(got, grad, later, short, grads, pad):
    low, low128, low8 = low_lanes(BLOCK), low_lanes(128), low_lanes(8)
    for q in range(4):
        lanes = slice(128 * q, 128 * q + 128)
        first, second = convolved(got, q, BLOCK, low128)
        pad[0:128, lanes] = grad[0:128, lanes] * first
        pad[128:256, lanes] = grad[128:256, lanes] * second
        a, b = (got[2 * q + n, 384:400].astype(F32)[0:8] for n in range(2))
        pad[256:264, lanes] = later[:, lanes] * jnp.where(low8, a, turned(b))
        a, b = got[2 * q, 0:BLOCK].astype(F32), got[2 * q + 1, 0:BLOCK].astype(F32)
        grads[1, :, lanes] = jnp.where(low, a, turned(b)).astype(BF)
        grads[2, :, lanes] = jnp.where(low, turned(a), b).astype(BF)
        grads[0, :, lanes] = sum(
            short[0, j : j + 1, lanes] * pad[j : j + BLOCK, lanes] for j in range(3)
        ).astype(BF)


def unpack_grads(got, grad, later, short):
    return pl.pallas_call(
        grads_kernel,
        out_shape=jax.ShapeDtypeStruct((3, BLOCK, 512), BF),
        scratch_shapes=[pltpu.VMEM((BLOCK + 8, 512), F32)],
        cost_estimate=pl.CostEstimate(flops=10**6, bytes_accessed=2 * 10**6, transcendentals=0),
        name="unpack_grads",
    )(got, grad, later, short)


def partial_kernel(place, m00, m01, m10, m11, g00, g01, g10, g11, lags, packed):
    def term(mixed, grad):
        return lax.dot_general(
            mixed[:, 0:512], grad[...], (((0,), (0,)), ((), ())), preferred_element_type=F32
        )

    part = term(m00, g00) + term(m01, g01) + term(m10, g10) + term(m11, g11)
    part = part.astype(BF)
    for n in range(32):
        packed[n, :, 0:1024] = part[16 * n : 16 * n + 16]
        start, lane = 16 * (n % 16), 512 + 128 * (n // 16)
        lag_z = m01[start : start + 16, lane : lane + 128]
        lag = lags[n].astype(F32) + lag_z.astype(F32)
        packed[n, :, 1024:1152] = lag.astype(BF)


def partial(place, mixed, grad, grads, lags):
    full = lambda *shape: pl.BlockSpec(shape, lambda n, p: (0,) * len(shape))
    return pl.pallas_call(
        partial_kernel,
        grid_spec=pltpu.PrefetchScalarGridSpec(
            num_scalar_prefetch=1,
            grid=(1,),
            in_specs=[full(BLOCK, 512), full(BLOCK, 768), full(BLOCK, 512), full(BLOCK, 512)]
            + [pl.BlockSpec((BLOCK, 1024), lambda n, p: (0, p[0]))]
            + [full(BLOCK, 1024)] * 3
            + [full(32, 16, 128)],
            out_specs=full(32, 16, 1152),
        ),
        out_shape=jax.ShapeDtypeStruct((32, 16, 1152), BF),
        name="partial",
    )(place, *mixed, grad, *grads, lags)


def reduce_kernel(scale, got, shared, held, lags, wide, in_sems, out_sems):
    copies = [
        pltpu.make_async_copy(
            got.at[8 * k : 8 * k + 8], held.at[8 * k : 8 * k + 8], in_sems.at[k]
        )
        for k in range(4)
    ]
    for copy in copies:
        copy.start()
    total = jnp.zeros((16, 1024), F32)
    sums = [jnp.zeros((16, 128), F32) for _ in range(8)]
    for k in range(4):
        copies[k].wait()
        for s in range(8):
            total = total + held[8 * k + s, :, 0:1024].astype(F32)
            sums[s] = sums[s] + held[8 * k + s, :, 1024:1152].astype(F32)
    total = (total * scale).astype(BF)
    low = low_lanes(16)
    for q in range(4):
        a, b = sums[2 * q] * scale, sums[2 * q + 1] * scale
        sides = (jnp.where(low, turned(a), b), jnp.where(low, a, turned(b)))
        for s in range(8):
            start = 4 * (s // 2)
            lags[s, 4 * q : 4 * q + 4] = sides[s % 2][start : start + 4]
    for s in range(8):
        wide[s, :, 0:1024] = total
        wide[s, :, 1024:1152] = lags[s].astype(BF)
    copies = [
        pltpu.make_async_copy(wide, shared.at[8 * k : 8 * k + 8], out_sems.at[k])
        for k in range(8)
    ]
    for copy in copies:
        copy.start()
    for copy in copies:
        copy.wait()


def reduce(got, scale):
    return pl.pallas_call(
        functools.partial(reduce_kernel, scale),
        in_specs=[pl.BlockSpec(memory_space=pltpu.HBM)],
        out_specs=pl.BlockSpec(memory_space=pltpu.HBM),
        out_shape=jax.ShapeDtypeStruct((64, 16, 1152), BF),
        scratch_shapes=[
            pltpu.VMEM((32, 16, 1152), BF),
            pltpu.VMEM((8, 16, 128), F32),
            pltpu.VMEM((8, 16, 1152), BF),
            pltpu.SemaphoreType.DMA((4,)),
            pltpu.SemaphoreType.DMA((8,)),
        ],
        name="reduce",
    )(got)


def start_writes(place, rows, grad_weight, held, wide, in_sems, out_sems):
    reads = [
        pltpu.make_async_copy(
            rows.at[8 * n : 8 * n + 8, :, 0:1024], held.at[n], in_sems.at[n]
        )
        for n in range(8)
    ]
    for copy in reads:
        copy.start()
    copies = []
    for n in range(8):
        reads[n].wait()
        zh, zl, yh = n // 4, n // 2 % 2, n % 2
        for k in range(8):
            wide[n, 16 * k : 16 * k + 16] = held[n, k].astype(F32)
        there = slice(128 * (2 * zh + yh), 128 * (2 * zh + yh) + 128)
        lanes = pl.ds(pl.multiple_of(2048 * place[0] + 1024 * zl, 1024), 1024)
        copies.append(
            pltpu.make_async_copy(wide.at[n], grad_weight.at[there, lanes], out_sems.at[n])
        )
        copies[-1].start()
    return copies


def first_kernel(place, rows, grad_weight, *scratch):
    for copy in start_writes(place, rows, grad_weight, *scratch):
        copy.wait()


def last_kernel(place, rows, lags, lags_c, whole, grad_weight, grad_filter, sums, *scratch):
    copies = start_writes(place, rows, grad_weight, *scratch)
    total = lags[...].astype(F32) + lags_c[...].astype(F32)
    sums[...] = total.reshape(1024, 128)
    for q in range(4):
        for k in range(4):
            part = sums[pl.ds(4 * q + k, 64, stride=16), :]
            grad_filter[64 * k : 64 * k + 64, 128 * q : 128 * q + 128] = part
    for copy in copies:
        copy.wait()


def write_half(half, rows, mine=None, whole=None):
    last = whole is not None
    lags_spec = pl.BlockSpec((64, 16, 128), lambda n, p: (0, 0, 8))
    hbm = pl.BlockSpec(memory_space=pltpu.HBM)
    shapes = [jax.ShapeDtypeStruct((512, 4096), F32)]
    if last:
        shapes.append(jax.ShapeDtypeStruct((BLOCK, 512), F32))
    return pl.pallas_call(
        last_kernel if last else first_kernel,
        grid_spec=pltpu.PrefetchScalarGridSpec(
            num_scalar_prefetch=1,
            grid=(1,),
            in_specs=[hbm] + [lags_spec, lags_spec, hbm] * last,
            out_specs=[hbm] + [pl.BlockSpec((BLOCK, 512), lambda n, p: (0, 0))] * last,
            scratch_shapes=[pltpu.VMEM((1024, 128), F32)] * last
            + [
                pltpu.VMEM((8, 8, 16, 1024), BF),
                pltpu.VMEM((8, 128, 1024), F32),
                pltpu.SemaphoreType.DMA((8,)),
                pltpu.SemaphoreType.DMA((8,)),
            ],
        ),
        out_shape=shapes,
        input_output_aliases={4: 0} if last else {},
        cost_estimate=pl.CostEstimate(flops=10**6, bytes_accessed=6 * 10**6, transcendentals=0),
        name="write_last" if last else "write_first",
    )(half, rows, *([rows, mine, whole] if last else []))


def exchange(x, axes):
    return lax.all_to_all(x, axes, 0, 0, tiled=True)


def across(x):
    return lax.ppermute(x, "c", [(0, 1), (1, 0)])


def along(x, step):
    return lax.ppermute(x, SEQ, [(n, n + step) for n in range(8) if 0 <= n + step < 8])


def above(x):
    return lax.ppermute(x, "zl", [(0, 1), (1, 0)])


def opposite(x):
    return lax.ppermute(x, ("zl", "c"), [(n, 3 - n) for n in range(4)])


def on_device(streams, short_filter, long_filter, skip_gain, out_weight, out_grad):
    scale = 1.0 / math.sqrt(16 * 2048)
    core = lax.axis_index("c").astype(jnp.int32)
    side = lax.axis_index("zl").astype(jnp.int32)
    seq = lax.axis_index(SEQ).astype(jnp.int32)
    grad = out_grad[0]

    def quarter(c, z):
        return lax.dynamic_slice(grad, (0, 1024 * (2 * c + z)), (BLOCK, 1024))

    grads = (
        above(quarter(core, 1 - side)),
        across(quarter(1 - core, side)),
        opposite(quarter(1 - core, 1 - side)),
    )
    short = short_filter
    packed, grad_mixed, gate_out = pack(streams[:, 0], grad, out_weight, long_filter, short)
    got = exchange(packed, SEQ)
    edge = along(streams[0, 0, BLOCK - 8 :], 1)
    later = along(grad_mixed[:8], -1)
    place = jnp.stack([seq, side])
    gain = skip_gain.reshape(1, 512)
    sent = conv(place, got, short, gain)
    sent, got, grads, edge, later = lax.optimization_barrier((sent, got, grads, edge, later))
    lags_own, lags = lag_sums(place, got, short, gain)
    back = exchange(sent, SEQ)
    back, lags_own, lags = lax.optimization_barrier((back, lags_own, lags))
    m00, joined = unpack_mixed(back, gate_out, edge, short, lags)
    m01, m10 = above(joined), across(m00)
    mixed = (m00, m01, m10, across(m01[:, :512]))
    part = partial((2 * core + side)[None], mixed, grad, grads, lags_own)
    part, m00, back = lax.optimization_barrier((part, m00, back))
    part = exchange(part, MOST)
    layer_out = jnp.dot(m00, out_weight, preferred_element_type=F32).astype(BF)
    part, m00, layer_out = lax.optimization_barrier((part, m00, layer_out))
    rows, back = lax.optimization_barrier((reduce(part, scale), back))
    mine = exchange(rows, CHIPS)
    grad_streams = unpack_grads(back, grad_mixed, later, short)
    mine, grad_streams = lax.optimization_barrier((mine, grad_streams))
    theirs = across(mine)
    grad_weight = write_half(core[None], mine)[0]
    grad_weight, grad_filter = write_half(1 - core[None], theirs, mine, grad_weight)
    return layer_out[None], grad_streams[:, None], grad_filter, grad_weight


def solution(mesh):
    fine = Mesh(
        mesh.devices.reshape(2, 2, 2, 2, 4, 2), ("zh", "zl", "yh", "c", "x", "yl")
    )
    dp = ("zh", "zl", "yh", "c")
    placed = (P(None, dp, SEQ, None), P(), P(SEQ, None), P(), P(), P(dp, SEQ, None))
    return jax.shard_map(
        on_device,
        mesh=fine,
        in_specs=placed,
        out_specs=(P(dp, SEQ, None), P(None, dp, SEQ, None), P(SEQ, None), P()),
        check_vma=False,
    )
```

```python
import functools
import math

import jax
import jax.numpy as jnp
import numpy as np
from jax import lax
from jax.experimental import pallas as pl
from jax.experimental.pallas import tpu as pltpu
from jax.sharding import Mesh, PartitionSpec as P

BF = jnp.bfloat16
F32 = jnp.float32
BLOCK = 256
HALF = 64
SENT_ROWS = BLOCK + 16
SEQ = ("x", "yl")
MOST = ("zh", "yh") + SEQ
DEPTH = ("zh", "zl", "yh")
CHIPS = DEPTH + SEQ


@functools.lru_cache(maxsize=None)
def tables():
    order = np.concatenate([np.arange(0, BLOCK, 2), np.arange(1, BLOCK, 2)])
    angle = np.pi * ((2 * order[:, None] + 1) * np.arange(BLOCK)[None, :] % 1024) / 512.0
    ahead = np.concatenate([np.cos(angle), -np.sin(angle)], axis=0)
    back = ahead.T / BLOCK

    def two(table):
        table = table.astype(np.float32)
        high = table.astype(jnp.bfloat16)
        return high, (table - high.astype(np.float32)).astype(jnp.bfloat16)

    return two(ahead) + two(back)


def mm(a, b):
    return jnp.dot(a, b, preferred_element_type=F32)


def low_lanes(rows):
    return lax.broadcasted_iota(jnp.int32, (rows, 128), 1) < HALF


def turned(x):
    return pltpu.roll(x, HALF, 1)


def pack_kernel(streams, out_grad, weight, filt, short, packed, grad, gate_out, pad):
    step = pl.program_id(0)
    low, low16 = low_lanes(BLOCK), low_lanes(16)

    @pl.when(step == 0)
    def _():
        grad[...] = jnp.zeros_like(grad)

    grad[...] += lax.dot_general(
        out_grad[...], weight[...], (((1,), (1,)), ((), ())), preferred_element_type=F32
    )

    for q in range(4):

        @pl.when(step == q)
        def _(q=q):
            lanes = slice(128 * q, 128 * q + 128)
            a, b = streams[1, :, lanes].astype(F32), streams[2, :, lanes].astype(F32)
            packed[2 * q, 0:BLOCK, 0:128] = jnp.where(low, a, turned(b)).astype(BF)
            packed[2 * q + 1, 0:BLOCK, 0:128] = jnp.where(low, turned(a), b).astype(BF)
            pad[0:8] = jnp.zeros((8, 128), F32)
            pad[8:] = streams[0, :, lanes].astype(F32)
            gate_out[:, lanes] = sum(
                short[0, j : j + 1, lanes] * pad[8 - j : 8 - j + BLOCK] for j in range(3)
            )

    @pl.when(step == pl.num_programs(0) - 1)
    def _():
        for q in range(4):
            lanes = slice(128 * q, 128 * q + 128)
            a, b = grad[:, lanes] * gate_out[:, lanes], filt[:, lanes]
            packed[2 * q, 0:BLOCK, 128:256] = jnp.where(low, a, turned(b)).astype(BF)
            packed[2 * q + 1, 0:BLOCK, 128:256] = jnp.where(low, turned(a), b).astype(BF)
            ends = streams[0, :, lanes].astype(F32)
            a = jnp.concatenate([ends[0:8], ends[BLOCK - 8 :]], axis=0)
            b = grad[0:16, lanes]
            packed[2 * q, BLOCK:, 0:128] = jnp.where(low16, a, turned(b)).astype(BF)
            packed[2 * q + 1, BLOCK:, 0:128] = jnp.where(low16, turned(a), b).astype(BF)
            packed[2 * q, BLOCK:, 128:256] = jnp.zeros((16, 128), BF)
            packed[2 * q + 1, BLOCK:, 128:256] = jnp.zeros((16, 128), BF)


def pack(streams, out_grad, weight, filt, short):
    steps = 4
    wide = out_grad.shape[1] // steps
    full = lambda *shape: pl.BlockSpec(shape, lambda k: (0,) * len(shape))
    return pl.pallas_call(
        pack_kernel,
        grid=(steps,),
        in_specs=[
            full(3, BLOCK, 512),
            pl.BlockSpec((BLOCK, wide), lambda k: (0, k)),
            pl.BlockSpec((512, wide), lambda k: (0, k)),
            full(BLOCK, 512),
            full(3, 3, 512),
        ],
        out_specs=[full(8, SENT_ROWS, 256), full(BLOCK, 512), full(BLOCK, 512)],
        out_shape=[
            jax.ShapeDtypeStruct((8, SENT_ROWS, 256), BF),
            jax.ShapeDtypeStruct((BLOCK, 512), F32),
            jax.ShapeDtypeStruct((BLOCK, 512), F32),
        ],
        scratch_shapes=[pltpu.VMEM((8 + BLOCK, 128), F32)],
        name="pack",
    )(streams, out_grad, weight, filt, short)


def split(x):
    high = x.astype(BF)
    return high, (x - high.astype(F32)).astype(BF)


def apply(table_h, table_l, high, rest):
    return mm(table_h[...], high) + mm(table_h[...], rest) + mm(table_l[...], high)


def weights(place, short, skip):
    low1 = low_lanes(1)
    odd = place[0] % 2 == 1
    taps = jnp.concatenate([short[n] for n in range(3)], axis=0)
    taps = jnp.where(odd, turned(taps), taps)
    taps_up = turned(taps)
    gain = skip[...]
    gain = jnp.where(odd, turned(gain), gain)
    gain = jnp.where(low1, gain, turned(gain))

    def pair(first, second):
        def row(table, i, j):
            if i is None:
                return jnp.full((1, 128), 1.0 if j == 0 else 0.0, F32)
            return table[3 * i + j : 3 * i + j + 1]

        return [
            jnp.where(low1, row(taps, first, j), row(taps_up, second, j)) for j in range(3)
        ]

    return pair, gain


def prepare(got, pair, pad, prod, gates=None):
    taps = pair(1, 2)
    low = low_lanes(BLOCK)
    pad[0:8] = jnp.zeros((8, 128), F32)

    def load(b, carry):
        rows = pl.ds(pl.multiple_of(8 + BLOCK * b, 8), BLOCK)
        pad[rows] = got[b, 0:BLOCK, 0:128].astype(F32)
        return carry

    lax.fori_loop(0, 8, load, 0)
    for b in range(8):
        start = 8 + BLOCK * b
        s = sum(taps[j] * pad[start - j : start - j + BLOCK] for j in range(3))
        if gates is not None:
            gates[b] = s
        prod[b] = jnp.where(low, s * turned(s), turned(got[b, 0:BLOCK, 128:256].astype(F32)))
    low8 = low_lanes(8)
    gate = pair(0, None)
    for b in range(8):
        ends = got[b, BLOCK:, 0:128].astype(F32)
        first = got[b - 1, BLOCK:, 0:128].astype(F32)[8:] if b else jnp.zeros((8, 128), F32)
        pad[0:8] = first
        pad[8:16] = ends[0:8]
        out = sum(gate[j] * pad[8 - j : 16 - j] for j in range(3))
        prod[b, 0:8] = jnp.where(low8, prod[b, 0:8], turned(out) * ends[0:8])


def spectra(prod, ahead_h, ahead_l, spec):
    low = low_lanes(BLOCK)
    sigma = jnp.where(low, 1.0, -1.0)

    def transform(n, carry):
        x = jnp.concatenate(
            [jnp.where(low, prod[b], prod[7 - b]) for b in (2 * n, 2 * n + 1)], axis=1
        )
        out = apply(ahead_h, ahead_l, *split(x))
        for t in range(2):
            spec[2 * n + t, 0:BLOCK] = out[:BLOCK, 128 * t : 128 * t + 128]
            spec[2 * n + t, BLOCK:] = out[BLOCK:, 128 * t : 128 * t + 128] * sigma
        return carry

    lax.fori_loop(0, 4, transform, 0)


def over_bins(spec, use):
    for sign, base in ((1.0, 0), (-1.0, 128)):

        def step(n, carry, sign=sign, base=base):
            re = pl.ds(pl.multiple_of(base + 8 * n, 8), 8)
            im = pl.ds(pl.multiple_of(BLOCK + base + 8 * n, 8), 8)
            own = [(spec[j, re], spec[j, im]) for j in range(8)]
            both = [own[0]]
            for j in range(1, 8):
                both.append(
                    (own[j][0] - sign * own[j - 1][1], own[j][1] + sign * own[j - 1][0])
                )
            use(re, im, own, both)
            return carry

        lax.fori_loop(0, 16, step, 0)


def summed(pairs):
    first = True
    for (ar, ai), (br, bi) in pairs:
        pr = ar * br - ai * bi
        pi = ar * bi + ai * br
        tr, ti = (pr, pi) if first else (tr + pr, ti + pi)
        first = False
    return tr, ti


def flipped(x, sign):
    return jnp.concatenate([x[0:BLOCK], x[BLOCK:] * sign], axis=0)


def conv_kernel(
    place, got, short, skip, ahead_h, ahead_l, back_h, back_l,
    sent,
    pad, prod, gates, spec, fspec, res, time, after,
):
    low = low_lanes(BLOCK)
    sigma = jnp.where(low, 1.0, -1.0)
    pair, gain = weights(place, short, skip)

    def filters(n, carry):
        def blocks(b):
            x, y = (got[n, 0:BLOCK, 128:256].astype(F32) for n in (b, b + 1))
            return jnp.where(low, turned(x), y).astype(BF)

        f = jnp.concatenate([blocks(4 * n), blocks(4 * n + 2)], axis=1)
        out = mm(ahead_h[...], f) + mm(ahead_l[...], f)
        low512 = low_lanes(512)
        for t in range(2):
            x = out[:, 128 * t : 128 * t + 128]
            y = turned(x)
            fspec[4 * n + 2 * t] = jnp.where(low512, x, y)
            fspec[4 * n + 2 * t + 1] = jnp.where(low512, y, x)
        return carry

    lax.fori_loop(0, 2, filters, 0)
    prepare(got, pair, pad, prod, gates)
    spectra(prod, ahead_h, ahead_l, spec)

    def multiply(re, im, own, both):
        filt = [(fspec[m, re], fspec[m, im]) for m in range(8)]
        for i in range(8):
            tr, ti = summed([(filt[m], both[i - m]) for m in range(i + 1)])
            res[i, re] = tr
            res[i, im] = ti

    over_bins(spec, multiply)

    def invert(n, carry):
        x = jnp.concatenate([flipped(res[b], sigma) for b in (2 * n, 2 * n + 1)], axis=1)
        out = apply(back_h, back_l, *split(x))
        time[2 * n] = out[:, :128]
        time[2 * n + 1] = out[:, 128:]
        return carry

    lax.fori_loop(0, 4, invert, 0)

    low128 = low_lanes(128)

    def gate(b, carry):
        t = jnp.where(low, time[b], time[7 - b]) + gain * prod[b]
        rows = pl.ds(pl.multiple_of(BLOCK * b, 8), BLOCK)
        after[rows] = jnp.where(low, turned(t), t) * turned(gates[b])
        sent[b, BLOCK:384] = jnp.where(low128, t[0:128], turned(t[128:256])).astype(BF)
        return carry

    lax.fori_loop(0, 8, gate, 0)
    low8 = low_lanes(8)
    for b in range(8):
        if b < 7:
            t = jnp.where(low8, time[b + 1, 0:8], time[6 - b, 0:8]) + gain * prod[b + 1, 0:8]
        else:
            t = jnp.zeros((8, 128), F32)
        sent[b, 384:400] = jnp.concatenate([t, t], axis=0).astype(BF)
    after[8 * BLOCK :] = jnp.zeros((8, 128), F32)
    taps = pair(1, 2)
    for b in range(8):
        start = BLOCK * b
        y = sum(taps[j] * after[start + j : start + j + BLOCK] for j in range(3))
        sent[b, 0:BLOCK] = y.astype(BF)


def lag_kernel(
    place, got, short, skip, ahead_h, ahead_l, back_h, back_l,
    lags, lags_z,
    pad, prod, spec, lres, rows,
):
    pair, _ = weights(place, short, skip)
    prepare(got, pair, pad, prod)
    spectra(prod, ahead_h, ahead_l, spec)
    zero = jnp.zeros((8, 128), F32)
    low8 = low_lanes(8)

    def multiply(re, im, own, both):
        grads, shifted = [], []
        for i in range(8):
            grads.append(
                tuple(jnp.where(low8, turned(own[7 - i][k]), own[7 - i][k]) for k in range(2))
            )
            before = both[i - 1] if i else (zero, zero)
            shifted.append(
                tuple(jnp.where(low8, before[k], turned(both[i][k])) for k in range(2))
            )
        for a in range(4):
            tr, ti = summed([(grads[i], shifted[i - 2 * a]) for i in range(2 * a, 8)])
            lres[a, re] = tr
            lres[a, im] = ti

    over_bins(spec, multiply)

    def invert(n, carry):
        x = jnp.concatenate([flipped(lres[a], -1.0) for a in (2 * n, 2 * n + 1)], axis=1)
        out = apply(back_h, back_l, *split(x))
        for t in range(2):
            for k in range(4):
                there = pl.ds(8 * n + 4 * t + k, 64, stride=16)
                rows[there, :] = out[64 * k : 64 * k + 64, 128 * t : 128 * t + 128]
        return carry

    for n in range(2):
        invert(n, 0)
    for z in range(2):
        for ref, side in ((lags, place[1]), (lags_z, 1 - place[1])):
            part = rows[pl.ds(pl.multiple_of(512 * z + 256 * side, 256), 256), :]
            ref[16 * z : 16 * z + 16] = part.reshape(16, 16, 128).astype(BF)


def on_channels(kernel, name, inputs, in_shapes, outputs, scratch, cost):
    full = lambda *shape: pl.BlockSpec(shape, lambda n, p: (0,) * len(shape))
    return pl.pallas_call(
        kernel,
        grid_spec=pltpu.PrefetchScalarGridSpec(
            num_scalar_prefetch=1,
            grid=(1,),
            in_specs=[
                full(8, SENT_ROWS, 256),
                pl.BlockSpec((3, 3, 128), lambda n, p: (0, 0, p[0] // 2)),
                pl.BlockSpec((1, 128), lambda n, p: (0, p[0] // 2)),
            ]
            + [full(*shape) for shape in in_shapes],
            out_specs=[full(*shape) for shape, _ in outputs],
            scratch_shapes=[
                pltpu.VMEM(shape, dtype)
                for shape, dtype in [((8 + 8 * BLOCK, 128), F32)] + scratch
            ],
        ),
        out_shape=[jax.ShapeDtypeStruct(shape, dtype) for shape, dtype in outputs],
        cost_estimate=cost,
        name=name,
    )(*inputs)


TABLES = [(512, BLOCK), (512, BLOCK), (BLOCK, 512), (BLOCK, 512)]
BLOCKS = ((8, BLOCK, 128), F32)
BINS = ((8, 512, 128), F32)


def spent(flops):
    return pl.CostEstimate(flops=flops, bytes_accessed=3 * 10**6, transcendentals=0)


def conv(place, got, short, skip):
    inputs = (place, got, short, skip, *(jnp.asarray(t) for t in tables()))
    outputs = [((8, 400, 128), BF)]
    scratch = [BLOCKS, BLOCKS, BINS, BINS, BINS, BLOCKS, ((8 * BLOCK + 8, 128), F32)]
    return on_channels(conv_kernel, "conv", inputs, TABLES, outputs, scratch, None)[0]


def lag_sums(place, got, short, skip):
    inputs = (place, got, short, skip, *(jnp.asarray(t) for t in tables()))
    outputs = [((32, 16, 128), BF)] * 2
    scratch = [BLOCKS, BINS, ((4, 512, 128), F32), ((1024, 128), F32)]
    cost = spent(2 * 10**9)
    return on_channels(lag_kernel, "lag_sums", inputs, TABLES, outputs, scratch, cost)


def convolved(got, q, start, low128):
    there = slice(start, start + 128)
    a, b = got[2 * q, there].astype(F32), got[2 * q + 1, there].astype(F32)
    return jnp.where(low128, a, turned(b)), jnp.where(low128, turned(a), b)


def mixed_kernel(got, gate_out, edge, short, lags, mixed, joined, pad):
    low128 = low_lanes(128)
    pad[0:8] = edge[...].astype(F32)
    pad[8:] = jnp.zeros((8, 512), F32)
    more = sum(short[0, j : j + 1] * pad[8 - j : 16 - j] for j in (1, 2))
    for q in range(4):
        lanes = slice(128 * q, 128 * q + 128)
        first, second = convolved(got, q, 0, low128)
        gate = gate_out[0:128, lanes]
        gate = jnp.concatenate([gate[0:8] + more[:, lanes], gate[8:]], axis=0)
        for ref in (mixed, joined):
            ref[0:128, lanes] = (gate * first).astype(BF)
            ref[128:256, lanes] = (gate_out[128:256, lanes] * second).astype(BF)
    for n in range(32):
        start, lane = 16 * (n % 16), 512 + 128 * (n // 16)
        joined[start : start + 16, lane : lane + 128] = lags[n]


def unpack_mixed(got, gate_out, edge, short, lags):
    full = lambda *shape: pl.BlockSpec(shape, lambda n: (0,) * len(shape))
    return pl.pallas_call(
        mixed_kernel,
        grid=(1,),
        in_specs=[
            pl.BlockSpec((8, 128, 128), lambda n: (0, 2, 0)),
            full(BLOCK, 512),
            full(8, 512),
            full(3, 3, 512),
            full(32, 16, 128),
        ],
        out_specs=[full(BLOCK, 512), full(BLOCK, 768)],
        out_shape=[
            jax.ShapeDtypeStruct((BLOCK, 512), BF),
            jax.ShapeDtypeStruct((BLOCK, 768), BF),
        ],
        scratch_shapes=[pltpu.VMEM((16, 512), F32)],
        name="unpack_mixed",
    )(got, gate_out, edge, short, lags)


def grads_kernel(got, grad, later, short, grads, pad):
    low, low128, low8 = low_lanes(BLOCK), low_lanes(128), low_lanes(8)
    for q in range(4):
        lanes = slice(128 * q, 128 * q + 128)
        first, second = convolved(got, q, BLOCK, low128)
        pad[0:128, lanes] = grad[0:128, lanes] * first
        pad[128:256, lanes] = grad[128:256, lanes] * second
        a, b = (got[2 * q + n, 384:400].astype(F32)[0:8] for n in range(2))
        pad[256:264, lanes] = later[:, lanes] * jnp.where(low8, a, turned(b))
        a, b = got[2 * q, 0:BLOCK].astype(F32), got[2 * q + 1, 0:BLOCK].astype(F32)
        grads[1, :, lanes] = jnp.where(low, a, turned(b)).astype(BF)
        grads[2, :, lanes] = jnp.where(low, turned(a), b).astype(BF)
        grads[0, :, lanes] = sum(
            short[0, j : j + 1, lanes] * pad[j : j + BLOCK, lanes] for j in range(3)
        ).astype(BF)


def unpack_grads(got, grad, later, short):
    return pl.pallas_call(
        grads_kernel,
        out_shape=jax.ShapeDtypeStruct((3, BLOCK, 512), BF),
        scratch_shapes=[pltpu.VMEM((BLOCK + 8, 512), F32)],
        cost_estimate=pl.CostEstimate(flops=10**6, bytes_accessed=2 * 10**6, transcendentals=0),
        name="unpack_grads",
    )(got, grad, later, short)


def partial_kernel(place, m00, m01, m10, m11, g00, g01, g10, g11, lags, lags_z, packed):
    def term(mixed, grad):
        return lax.dot_general(
            mixed[...], grad[...], (((0,), (0,)), ((), ())), preferred_element_type=F32
        )

    part = term(m00, g00) + term(m01, g01) + term(m10, g10) + term(m11, g11)
    part = part.astype(BF)
    first = pl.multiple_of(128 * (pl.program_id(0) % 2), 128)
    for n in range(8):
        packed[n, :, 0:1024] = part[16 * n : 16 * n + 16]
        lag = lags[n].astype(F32) + lags_z[pl.ds(first + 16 * n, 16), :].astype(F32)
        packed[n, :, 1024:1152] = lag.astype(BF)


def partial(place, mixed, grad, grads, lags):
    full = lambda *shape: pl.BlockSpec(shape, lambda n, p: (0,) * len(shape))
    tall = pl.BlockSpec((BLOCK, 128), lambda n, p: (0, n))
    return pl.pallas_call(
        partial_kernel,
        grid_spec=pltpu.PrefetchScalarGridSpec(
            num_scalar_prefetch=1,
            grid=(4,),
            in_specs=[tall] * 4
            + [pl.BlockSpec((BLOCK, 1024), lambda n, p: (0, p[0]))]
            + [full(BLOCK, 1024)] * 3
            + [
                pl.BlockSpec((8, 16, 128), lambda n, p: (n, 0, 0)),
                pl.BlockSpec((BLOCK, 128), lambda n, p: (0, 4 + n // 2)),
            ],
            out_specs=pl.BlockSpec((8, 16, 1152), lambda n, p: (n, 0, 0)),
        ),
        out_shape=jax.ShapeDtypeStruct((32, 16, 1152), BF),
        name="partial",
    )(place, *mixed, grad, *grads, lags, mixed[1])


def reduce_kernel(scale, got, shared, held, lags, wide, in_sems, out_sems):
    copies = [
        pltpu.make_async_copy(
            got.at[8 * k : 8 * k + 8], held.at[8 * k : 8 * k + 8], in_sems.at[k]
        )
        for k in range(4)
    ]
    for copy in copies:
        copy.start()
    total = jnp.zeros((16, 1024), F32)
    sums = [jnp.zeros((16, 128), F32) for _ in range(8)]
    for k in range(4):
        copies[k].wait()
        for s in range(8):
            total = total + held[8 * k + s, :, 0:1024].astype(F32)
            sums[s] = sums[s] + held[8 * k + s, :, 1024:1152].astype(F32)
    total = (total * scale).astype(BF)
    low = low_lanes(16)
    for q in range(4):
        a, b = sums[2 * q] * scale, sums[2 * q + 1] * scale
        sides = (jnp.where(low, turned(a), b), jnp.where(low, a, turned(b)))
        for s in range(8):
            start = 4 * (s // 2)
            lags[s, 4 * q : 4 * q + 4] = sides[s % 2][start : start + 4]
    for s in range(8):
        wide[s, :, 0:1024] = total
        wide[s, :, 1024:1152] = lags[s].astype(BF)
    copies = [
        pltpu.make_async_copy(wide, shared.at[8 * k : 8 * k + 8], out_sems.at[k])
        for k in range(8)
    ]
    for copy in copies:
        copy.start()
    for copy in copies:
        copy.wait()


def reduce(got, scale):
    return pl.pallas_call(
        functools.partial(reduce_kernel, scale),
        in_specs=[pl.BlockSpec(memory_space=pltpu.HBM)],
        out_specs=pl.BlockSpec(memory_space=pltpu.HBM),
        out_shape=jax.ShapeDtypeStruct((64, 16, 1152), BF),
        scratch_shapes=[
            pltpu.VMEM((32, 16, 1152), BF),
            pltpu.VMEM((8, 16, 128), F32),
            pltpu.VMEM((8, 16, 1152), BF),
            pltpu.SemaphoreType.DMA((4,)),
            pltpu.SemaphoreType.DMA((8,)),
        ],
        name="reduce",
    )(got)


def start_writes(place, rows, grad_weight, held, wide, in_sems, out_sems, more=()):
    reads = [
        pltpu.make_async_copy(
            rows.at[8 * n : 8 * n + 8, :, 0:1024], held.at[n], in_sems.at[n]
        )
        for n in range(8)
    ]
    for copy in reads + list(more):
        copy.start()
    copies = []
    for n in range(8):
        reads[n].wait()
        zh, zl, yh = n // 4, n // 2 % 2, n % 2
        for k in range(8):
            wide[n, 16 * k : 16 * k + 16] = held[n, k].astype(F32)
        there = slice(128 * (2 * zh + yh), 128 * (2 * zh + yh) + 128)
        lanes = pl.ds(pl.multiple_of(2048 * place[0] + 1024 * zl, 1024), 1024)
        copies.append(
            pltpu.make_async_copy(wide.at[n], grad_weight.at[there, lanes], out_sems.at[n])
        )
        copies[-1].start()
    return copies


def first_kernel(place, rows, grad_weight, *scratch):
    for copy in start_writes(place, rows, grad_weight, *scratch):
        copy.wait()


def last_kernel(
    place, rows, mine, whole, grad_weight, grad_filter, lags, sums, filt, lag_sems, *scratch
):
    reads = [
        pltpu.make_async_copy(src.at[:, :, 1024:1152], lags.at[n], lag_sems.at[n])
        for n, src in enumerate((rows, mine))
    ]
    copies = start_writes(place, rows, grad_weight, *scratch, more=reads)
    for copy in reads:
        copy.wait()
    sums[...] = (lags[0].astype(F32) + lags[1].astype(F32)).reshape(1024, 128)
    for q in range(4):
        for k in range(4):
            part = sums[pl.ds(4 * q + k, 64, stride=16), :]
            filt[64 * k : 64 * k + 64, 128 * q : 128 * q + 128] = part
    copies.append(pltpu.make_async_copy(filt, grad_filter, lag_sems.at[2]))
    copies[-1].start()
    for copy in copies:
        copy.wait()


def write_half(half, rows, mine=None, whole=None):
    last = whole is not None
    hbm = pl.BlockSpec(memory_space=pltpu.HBM)
    shapes = [jax.ShapeDtypeStruct((512, 4096), F32)]
    if last:
        shapes.append(jax.ShapeDtypeStruct((BLOCK, 512), F32))
    return pl.pallas_call(
        last_kernel if last else first_kernel,
        grid_spec=pltpu.PrefetchScalarGridSpec(
            num_scalar_prefetch=1,
            grid=(1,),
            in_specs=[hbm] + [hbm, hbm] * last,
            out_specs=[hbm] + [hbm] * last,
            scratch_shapes=[
                pltpu.VMEM((2, 64, 16, 128), BF),
                pltpu.VMEM((1024, 128), F32),
                pltpu.VMEM((BLOCK, 512), F32),
                pltpu.SemaphoreType.DMA((3,)),
            ]
            * last
            + [
                pltpu.VMEM((8, 8, 16, 1024), BF),
                pltpu.VMEM((8, 128, 1024), F32),
                pltpu.SemaphoreType.DMA((8,)),
                pltpu.SemaphoreType.DMA((8,)),
            ],
        ),
        out_shape=shapes,
        input_output_aliases={3: 0} if last else {},
        cost_estimate=pl.CostEstimate(flops=10**6, bytes_accessed=6 * 10**6, transcendentals=0),
        name="write_last" if last else "write_first",
    )(half, rows, *([mine, whole] if last else []))


def exchange(x, axes):
    return lax.all_to_all(x, axes, 0, 0, tiled=True)


def across(x):
    return lax.ppermute(x, "c", [(0, 1), (1, 0)])


def along(x, step):
    return lax.ppermute(x, SEQ, [(n, n + step) for n in range(8) if 0 <= n + step < 8])


def above(x):
    return lax.ppermute(x, "zl", [(0, 1), (1, 0)])


def opposite(x):
    return lax.ppermute(x, ("zl", "c"), [(n, 3 - n) for n in range(4)])


def on_device(streams, short_filter, long_filter, skip_gain, out_weight, out_grad):
    scale = 1.0 / math.sqrt(16 * 2048)
    core = lax.axis_index("c").astype(jnp.int32)
    side = lax.axis_index("zl").astype(jnp.int32)
    seq = lax.axis_index(SEQ).astype(jnp.int32)
    grad = out_grad[0]

    def quarter(c, z):
        return lax.dynamic_slice(grad, (0, 1024 * (2 * c + z)), (BLOCK, 1024))

    grads = (
        above(quarter(core, 1 - side)),
        across(quarter(1 - core, side)),
        opposite(quarter(1 - core, 1 - side)),
    )
    short = short_filter
    packed, grad_mixed, gate_out = pack(streams[:, 0], grad, out_weight, long_filter, short)
    got = exchange(packed, SEQ)
    edge = along(streams[0, 0, BLOCK - 8 :], 1)
    later = along(grad_mixed[:8], -1)
    place = jnp.stack([seq, side])
    gain = skip_gain.reshape(1, 512)
    sent = conv(place, got, short, gain)
    sent, got, grads, edge, later = lax.optimization_barrier((sent, got, grads, edge, later))
    lags_own, lags = lag_sums(place, got, short, gain)
    back = exchange(sent, SEQ)
    back, lags_own, lags = lax.optimization_barrier((back, lags_own, lags))
    m00, joined = unpack_mixed(back, gate_out, edge, short, lags)
    m01, m10 = above(joined), across(m00)
    mixed = (m00, m01, m10, across(m01[:, :512]))
    part = partial((2 * core + side)[None], mixed, grad, grads, lags_own)
    part, m00, back = lax.optimization_barrier((part, m00, back))
    part = exchange(part, MOST)
    layer_out = jnp.dot(m00, out_weight, preferred_element_type=F32).astype(BF)
    part, m00, layer_out = lax.optimization_barrier((part, m00, layer_out))
    rows, back = lax.optimization_barrier((reduce(part, scale), back))
    mine = exchange(rows, CHIPS)
    grad_streams = unpack_grads(back, grad_mixed, later, short)
    mine, grad_streams = lax.optimization_barrier((mine, grad_streams))
    theirs = across(mine)
    grad_weight = write_half(core[None], mine)[0]
    grad_weight, grad_filter = write_half(1 - core[None], theirs, mine, grad_weight)
    return layer_out[None], grad_streams[:, None], grad_filter, grad_weight


def solution(mesh):
    fine = Mesh(
        mesh.devices.reshape(2, 2, 2, 2, 4, 2), ("zh", "zl", "yh", "c", "x", "yl")
    )
    dp = ("zh", "zl", "yh", "c")
    placed = (P(None, dp, SEQ, None), P(), P(SEQ, None), P(), P(), P(dp, SEQ, None))
    return jax.shard_map(
        on_device,
        mesh=fine,
        in_specs=placed,
        out_specs=(P(dp, SEQ, None), P(None, dp, SEQ, None), P(SEQ, None), P()),
        check_vma=False,
    )
```

```python
import functools
import math

import jax
import jax.numpy as jnp
import numpy as np
from jax import lax
from jax.experimental import pallas as pl
from jax.experimental.pallas import tpu as pltpu
from jax.sharding import Mesh, PartitionSpec as P

BF = jnp.bfloat16
F32 = jnp.float32
BLOCK = 256
HALF = 64
SENT_ROWS = BLOCK + 16
KEEP_OUT = 63 * 2**20
SEQ = ("x", "yl")
MOST = ("zh", "yh") + SEQ
DEPTH = ("zh", "zl", "yh")
CHIPS = DEPTH + SEQ


@functools.lru_cache(maxsize=None)
def tables():
    order = np.concatenate([np.arange(0, BLOCK, 2), np.arange(1, BLOCK, 2)])
    angle = np.pi * ((2 * order[:, None] + 1) * np.arange(BLOCK)[None, :] % 1024) / 512.0
    ahead = np.concatenate([np.cos(angle), -np.sin(angle)], axis=0)
    back = ahead.T / BLOCK

    def two(table):
        table = table.astype(np.float32)
        high = table.astype(jnp.bfloat16)
        return high, (table - high.astype(np.float32)).astype(jnp.bfloat16)

    return two(ahead) + two(back)


def mm(a, b):
    return jnp.dot(a, b, preferred_element_type=F32)


def low_lanes(rows):
    return lax.broadcasted_iota(jnp.int32, (rows, 128), 1) < HALF


def turned(x):
    return pltpu.roll(x, HALF, 1)


def pack_kernel(streams, out_grad, weight, filt, short, packed, grad, gate_out, pad):
    step = pl.program_id(0)
    low, low16 = low_lanes(BLOCK), low_lanes(16)

    @pl.when(step == 0)
    def _():
        grad[...] = jnp.zeros_like(grad)

    grad[...] += lax.dot_general(
        out_grad[...], weight[...], (((1,), (1,)), ((), ())), preferred_element_type=F32
    )

    for q in range(4):

        @pl.when(step == q)
        def _(q=q):
            lanes = slice(128 * q, 128 * q + 128)
            a, b = streams[1, :, lanes].astype(F32), streams[2, :, lanes].astype(F32)
            packed[2 * q, 0:BLOCK, 0:128] = jnp.where(low, a, turned(b)).astype(BF)
            packed[2 * q + 1, 0:BLOCK, 0:128] = jnp.where(low, turned(a), b).astype(BF)
            pad[0:8] = jnp.zeros((8, 128), F32)
            pad[8:] = streams[0, :, lanes].astype(F32)
            gate_out[:, lanes] = sum(
                short[0, j : j + 1, lanes] * pad[8 - j : 8 - j + BLOCK] for j in range(3)
            )

    @pl.when(step == pl.num_programs(0) - 1)
    def _():
        for q in range(4):
            lanes = slice(128 * q, 128 * q + 128)
            a, b = grad[:, lanes] * gate_out[:, lanes], filt[:, lanes]
            packed[2 * q, 0:BLOCK, 128:256] = jnp.where(low, a, turned(b)).astype(BF)
            packed[2 * q + 1, 0:BLOCK, 128:256] = jnp.where(low, turned(a), b).astype(BF)
            ends = streams[0, :, lanes].astype(F32)
            a = jnp.concatenate([ends[0:8], ends[BLOCK - 8 :]], axis=0)
            b = grad[0:16, lanes]
            packed[2 * q, BLOCK:, 0:128] = jnp.where(low16, a, turned(b)).astype(BF)
            packed[2 * q + 1, BLOCK:, 0:128] = jnp.where(low16, turned(a), b).astype(BF)
            packed[2 * q, BLOCK:, 128:256] = jnp.zeros((16, 128), BF)
            packed[2 * q + 1, BLOCK:, 128:256] = jnp.zeros((16, 128), BF)


def pack(streams, out_grad, weight, filt, short):
    steps = 4
    wide = out_grad.shape[1] // steps
    full = lambda *shape: pl.BlockSpec(shape, lambda k: (0,) * len(shape))
    return pl.pallas_call(
        pack_kernel,
        grid=(steps,),
        in_specs=[
            full(3, BLOCK, 512),
            pl.BlockSpec((BLOCK, wide), lambda k: (0, k)),
            pl.BlockSpec((512, wide), lambda k: (0, k)),
            full(BLOCK, 512),
            full(3, 3, 512),
        ],
        out_specs=[full(8, SENT_ROWS, 256), full(BLOCK, 512), full(BLOCK, 512)],
        out_shape=[
            jax.ShapeDtypeStruct((8, SENT_ROWS, 256), BF),
            jax.ShapeDtypeStruct((BLOCK, 512), F32),
            jax.ShapeDtypeStruct((BLOCK, 512), F32),
        ],
        scratch_shapes=[pltpu.VMEM((8 + BLOCK, 128), F32)],
        name="pack",
    )(streams, out_grad, weight, filt, short)


def split(x):
    high = x.astype(BF)
    return high, (x - high.astype(F32)).astype(BF)


def apply(table_h, table_l, high, rest):
    return mm(table_h[...], high) + mm(table_h[...], rest) + mm(table_l[...], high)


def weights(place, short, skip):
    low1 = low_lanes(1)
    odd = place[0] % 2 == 1
    taps = jnp.concatenate([short[n] for n in range(3)], axis=0)
    taps = jnp.where(odd, turned(taps), taps)
    taps_up = turned(taps)
    gain = skip[...]
    gain = jnp.where(odd, turned(gain), gain)
    gain = jnp.where(low1, gain, turned(gain))

    def pair(first, second):
        def row(table, i, j):
            if i is None:
                return jnp.full((1, 128), 1.0 if j == 0 else 0.0, F32)
            return table[3 * i + j : 3 * i + j + 1]

        return [
            jnp.where(low1, row(taps, first, j), row(taps_up, second, j)) for j in range(3)
        ]

    return pair, gain


def prepare(got, pair, pad, prod, gates=None):
    taps = pair(1, 2)
    low = low_lanes(BLOCK)
    pad[0:8] = jnp.zeros((8, 128), F32)

    def load(b, carry):
        rows = pl.ds(pl.multiple_of(8 + BLOCK * b, 8), BLOCK)
        pad[rows] = got[b, 0:BLOCK, 0:128].astype(F32)
        return carry

    lax.fori_loop(0, 8, load, 0)
    for b in range(8):
        start = 8 + BLOCK * b
        s = sum(taps[j] * pad[start - j : start - j + BLOCK] for j in range(3))
        if gates is not None:
            gates[b] = s
        prod[b] = jnp.where(low, s * turned(s), turned(got[b, 0:BLOCK, 128:256].astype(F32)))
    low8 = low_lanes(8)
    gate = pair(0, None)
    for b in range(8):
        ends = got[b, BLOCK:, 0:128].astype(F32)
        first = got[b - 1, BLOCK:, 0:128].astype(F32)[8:] if b else jnp.zeros((8, 128), F32)
        pad[0:8] = first
        pad[8:16] = ends[0:8]
        out = sum(gate[j] * pad[8 - j : 16 - j] for j in range(3))
        prod[b, 0:8] = jnp.where(low8, prod[b, 0:8], turned(out) * ends[0:8])


def spectra(prod, ahead_h, ahead_l, spec):
    low = low_lanes(BLOCK)
    sigma = jnp.where(low, 1.0, -1.0)

    def transform(n, carry):
        x = jnp.concatenate(
            [jnp.where(low, prod[b], prod[7 - b]) for b in (2 * n, 2 * n + 1)], axis=1
        )
        out = apply(ahead_h, ahead_l, *split(x))
        for t in range(2):
            spec[2 * n + t, 0:BLOCK] = out[:BLOCK, 128 * t : 128 * t + 128]
            spec[2 * n + t, BLOCK:] = out[BLOCK:, 128 * t : 128 * t + 128] * sigma
        return carry

    lax.fori_loop(0, 4, transform, 0)


def over_bins(spec, use):
    for sign, base in ((1.0, 0), (-1.0, 128)):

        def step(n, carry, sign=sign, base=base):
            re = pl.ds(pl.multiple_of(base + 8 * n, 8), 8)
            im = pl.ds(pl.multiple_of(BLOCK + base + 8 * n, 8), 8)
            own = [(spec[j, re], spec[j, im]) for j in range(8)]
            both = [own[0]]
            for j in range(1, 8):
                both.append(
                    (own[j][0] - sign * own[j - 1][1], own[j][1] + sign * own[j - 1][0])
                )
            use(re, im, own, both)
            return carry

        lax.fori_loop(0, 16, step, 0)


def summed(pairs):
    first = True
    for (ar, ai), (br, bi) in pairs:
        pr = ar * br - ai * bi
        pi = ar * bi + ai * br
        tr, ti = (pr, pi) if first else (tr + pr, ti + pi)
        first = False
    return tr, ti


def flipped(x, sign):
    return jnp.concatenate([x[0:BLOCK], x[BLOCK:] * sign], axis=0)


def conv_kernel(
    place, got, short, skip, ahead_h, ahead_l, back_h, back_l,
    sent,
    pad, prod, gates, spec, fspec, res, time, after,
):
    low = low_lanes(BLOCK)
    sigma = jnp.where(low, 1.0, -1.0)
    pair, gain = weights(place, short, skip)

    def filters(n, carry):
        def blocks(b):
            x, y = (got[n, 0:BLOCK, 128:256].astype(F32) for n in (b, b + 1))
            return jnp.where(low, turned(x), y).astype(BF)

        f = jnp.concatenate([blocks(4 * n), blocks(4 * n + 2)], axis=1)
        out = mm(ahead_h[...], f) + mm(ahead_l[...], f)
        low512 = low_lanes(512)
        for t in range(2):
            x = out[:, 128 * t : 128 * t + 128]
            y = turned(x)
            fspec[4 * n + 2 * t] = jnp.where(low512, x, y)
            fspec[4 * n + 2 * t + 1] = jnp.where(low512, y, x)
        return carry

    lax.fori_loop(0, 2, filters, 0)
    prepare(got, pair, pad, prod, gates)
    spectra(prod, ahead_h, ahead_l, spec)

    def multiply(re, im, own, both):
        filt = [(fspec[m, re], fspec[m, im]) for m in range(8)]
        for i in range(8):
            tr, ti = summed([(filt[m], both[i - m]) for m in range(i + 1)])
            res[i, re] = tr
            res[i, im] = ti

    over_bins(spec, multiply)

    def invert(n, carry):
        x = jnp.concatenate([flipped(res[b], sigma) for b in (2 * n, 2 * n + 1)], axis=1)
        out = apply(back_h, back_l, *split(x))
        time[2 * n] = out[:, :128]
        time[2 * n + 1] = out[:, 128:]
        return carry

    lax.fori_loop(0, 4, invert, 0)

    low128 = low_lanes(128)

    def gate(b, carry):
        t = jnp.where(low, time[b], time[7 - b]) + gain * prod[b]
        rows = pl.ds(pl.multiple_of(BLOCK * b, 8), BLOCK)
        after[rows] = jnp.where(low, turned(t), t) * turned(gates[b])
        sent[b, BLOCK:384] = jnp.where(low128, t[0:128], turned(t[128:256])).astype(BF)
        return carry

    lax.fori_loop(0, 8, gate, 0)
    low8 = low_lanes(8)
    for b in range(8):
        if b < 7:
            t = jnp.where(low8, time[b + 1, 0:8], time[6 - b, 0:8]) + gain * prod[b + 1, 0:8]
        else:
            t = jnp.zeros((8, 128), F32)
        sent[b, 384:400] = jnp.concatenate([t, t], axis=0).astype(BF)
    after[8 * BLOCK :] = jnp.zeros((8, 128), F32)
    taps = pair(1, 2)
    for b in range(8):
        start = BLOCK * b
        y = sum(taps[j] * after[start + j : start + j + BLOCK] for j in range(3))
        sent[b, 0:BLOCK] = y.astype(BF)


def lag_kernel(
    place, got, short, skip, ahead_h, ahead_l, back_h, back_l,
    lags, lags_z,
    pad, prod, spec, lres, rows,
):
    pair, _ = weights(place, short, skip)
    prepare(got, pair, pad, prod)
    spectra(prod, ahead_h, ahead_l, spec)
    zero = jnp.zeros((8, 128), F32)
    low8 = low_lanes(8)

    def multiply(re, im, own, both):
        grads, shifted = [], []
        for i in range(8):
            grads.append(
                tuple(jnp.where(low8, turned(own[7 - i][k]), own[7 - i][k]) for k in range(2))
            )
            before = both[i - 1] if i else (zero, zero)
            shifted.append(
                tuple(jnp.where(low8, before[k], turned(both[i][k])) for k in range(2))
            )
        for a in range(4):
            tr, ti = summed([(grads[i], shifted[i - 2 * a]) for i in range(2 * a, 8)])
            lres[a, re] = tr
            lres[a, im] = ti

    over_bins(spec, multiply)

    def invert(n, carry):
        x = jnp.concatenate([flipped(lres[a], -1.0) for a in (2 * n, 2 * n + 1)], axis=1)
        out = apply(back_h, back_l, *split(x))
        for t in range(2):
            for k in range(4):
                there = pl.ds(8 * n + 4 * t + k, 64, stride=16)
                rows[there, :] = out[64 * k : 64 * k + 64, 128 * t : 128 * t + 128]
        return carry

    for n in range(2):
        invert(n, 0)
    for z in range(2):
        for ref, side in ((lags, place[1]), (lags_z, 1 - place[1])):
            part = rows[pl.ds(pl.multiple_of(512 * z + 256 * side, 256), 256), :]
            ref[16 * z : 16 * z + 16] = part.reshape(16, 16, 128).astype(BF)


def on_channels(kernel, name, inputs, in_shapes, outputs, scratch, cost):
    full = lambda *shape: pl.BlockSpec(shape, lambda n, p: (0,) * len(shape))
    return pl.pallas_call(
        kernel,
        grid_spec=pltpu.PrefetchScalarGridSpec(
            num_scalar_prefetch=1,
            grid=(1,),
            in_specs=[
                full(8, SENT_ROWS, 256),
                pl.BlockSpec((3, 3, 128), lambda n, p: (0, 0, p[0] // 2)),
                pl.BlockSpec((1, 128), lambda n, p: (0, p[0] // 2)),
            ]
            + [full(*shape) for shape in in_shapes],
            out_specs=[full(*shape) for shape, _ in outputs],
            scratch_shapes=[
                pltpu.VMEM(shape, dtype)
                for shape, dtype in [((8 + 8 * BLOCK, 128), F32)] + scratch
            ],
        ),
        out_shape=[jax.ShapeDtypeStruct(shape, dtype) for shape, dtype in outputs],
        cost_estimate=cost,
        name=name,
    )(*inputs)


TABLES = [(512, BLOCK), (512, BLOCK), (BLOCK, 512), (BLOCK, 512)]
BLOCKS = ((8, BLOCK, 128), F32)
BINS = ((8, 512, 128), F32)


def spent(flops):
    return pl.CostEstimate(flops=flops, bytes_accessed=3 * 10**6, transcendentals=0)


def conv(place, got, short, skip):
    inputs = (place, got, short, skip, *(jnp.asarray(t) for t in tables()))
    outputs = [((8, 400, 128), BF)]
    scratch = [BLOCKS, BLOCKS, BINS, BINS, BINS, BLOCKS, ((8 * BLOCK + 8, 128), F32)]
    return on_channels(conv_kernel, "conv", inputs, TABLES, outputs, scratch, None)[0]


def lag_sums(place, got, short, skip):
    inputs = (place, got, short, skip, *(jnp.asarray(t) for t in tables()))
    outputs = [((32, 16, 128), BF)] * 2
    scratch = [BLOCKS, BINS, ((4, 512, 128), F32), ((1024, 128), F32)]
    cost = spent(2 * 10**9)
    return on_channels(lag_kernel, "lag_sums", inputs, TABLES, outputs, scratch, cost)


def convolved(got, q, start, low128):
    there = slice(start, start + 128)
    a, b = got[2 * q, there].astype(F32), got[2 * q + 1, there].astype(F32)
    return jnp.where(low128, a, turned(b)), jnp.where(low128, turned(a), b)


def mixed_kernel(got, gate_out, edge, short, lags, mixed, joined, pad):
    low128 = low_lanes(128)
    pad[0:8] = edge[...].astype(F32)
    pad[8:] = jnp.zeros((8, 512), F32)
    more = sum(short[0, j : j + 1] * pad[8 - j : 16 - j] for j in (1, 2))
    for q in range(4):
        lanes = slice(128 * q, 128 * q + 128)
        first, second = convolved(got, q, 0, low128)
        gate = gate_out[0:128, lanes]
        gate = jnp.concatenate([gate[0:8] + more[:, lanes], gate[8:]], axis=0)
        for ref in (mixed, joined):
            ref[0:128, lanes] = (gate * first).astype(BF)
            ref[128:256, lanes] = (gate_out[128:256, lanes] * second).astype(BF)
    for n in range(32):
        start, lane = 16 * (n % 16), 512 + 128 * (n // 16)
        joined[start : start + 16, lane : lane + 128] = lags[n]


def unpack_mixed(got, gate_out, edge, short, lags):
    full = lambda *shape: pl.BlockSpec(shape, lambda n: (0,) * len(shape))
    return pl.pallas_call(
        mixed_kernel,
        grid=(1,),
        in_specs=[
            pl.BlockSpec((8, 128, 128), lambda n: (0, 2, 0)),
            full(BLOCK, 512),
            full(8, 512),
            full(3, 3, 512),
            full(32, 16, 128),
        ],
        out_specs=[full(BLOCK, 512), full(BLOCK, 768)],
        out_shape=[
            jax.ShapeDtypeStruct((BLOCK, 512), BF),
            jax.ShapeDtypeStruct((BLOCK, 768), BF),
        ],
        scratch_shapes=[pltpu.VMEM((16, 512), F32)],
        compiler_params=pltpu.CompilerParams(vmem_limit_bytes=KEEP_OUT),
        name="unpack_mixed",
    )(got, gate_out, edge, short, lags)


def grads_kernel(got, grad, later, short, grads, pad):
    low, low128, low8 = low_lanes(BLOCK), low_lanes(128), low_lanes(8)
    for q in range(4):
        lanes = slice(128 * q, 128 * q + 128)
        first, second = convolved(got, q, BLOCK, low128)
        pad[0:128, lanes] = grad[0:128, lanes] * first
        pad[128:256, lanes] = grad[128:256, lanes] * second
        a, b = (got[2 * q + n, 384:400].astype(F32)[0:8] for n in range(2))
        pad[256:264, lanes] = later[:, lanes] * jnp.where(low8, a, turned(b))
        a, b = got[2 * q, 0:BLOCK].astype(F32), got[2 * q + 1, 0:BLOCK].astype(F32)
        grads[1, :, lanes] = jnp.where(low, a, turned(b)).astype(BF)
        grads[2, :, lanes] = jnp.where(low, turned(a), b).astype(BF)
        grads[0, :, lanes] = sum(
            short[0, j : j + 1, lanes] * pad[j : j + BLOCK, lanes] for j in range(3)
        ).astype(BF)


def unpack_grads(got, grad, later, short):
    return pl.pallas_call(
        grads_kernel,
        out_shape=jax.ShapeDtypeStruct((3, BLOCK, 512), BF),
        scratch_shapes=[pltpu.VMEM((BLOCK + 8, 512), F32)],
        cost_estimate=pl.CostEstimate(flops=10**6, bytes_accessed=2 * 10**6, transcendentals=0),
        compiler_params=pltpu.CompilerParams(vmem_limit_bytes=KEEP_OUT),
        name="unpack_grads",
    )(got, grad, later, short)


def partial_kernel(place, m00, m01, m10, m11, g00, g01, g10, g11, lags, packed):
    def term(mixed, grad):
        return lax.dot_general(
            mixed[:, 0:512], grad[...], (((0,), (0,)), ((), ())), preferred_element_type=F32
        )

    part = term(m00, g00) + term(m01, g01) + term(m10, g10) + term(m11, g11)
    part = part.astype(BF)
    for n in range(32):
        packed[n, :, 0:1024] = part[16 * n : 16 * n + 16]
        start, lane = 16 * (n % 16), 512 + 128 * (n // 16)
        lag_z = m01[start : start + 16, lane : lane + 128]
        lag = lags[n].astype(F32) + lag_z.astype(F32)
        packed[n, :, 1024:1152] = lag.astype(BF)


def partial(place, mixed, grad, grads, lags):
    full = lambda *shape: pl.BlockSpec(shape, lambda n, p: (0,) * len(shape))
    return pl.pallas_call(
        partial_kernel,
        grid_spec=pltpu.PrefetchScalarGridSpec(
            num_scalar_prefetch=1,
            grid=(1,),
            in_specs=[full(BLOCK, 512), full(BLOCK, 768), full(BLOCK, 512), full(BLOCK, 512)]
            + [pl.BlockSpec((BLOCK, 1024), lambda n, p: (0, p[0]))]
            + [full(BLOCK, 1024)] * 3
            + [full(32, 16, 128)],
            out_specs=full(32, 16, 1152),
        ),
        out_shape=jax.ShapeDtypeStruct((32, 16, 1152), BF),
        name="partial",
    )(place, *mixed, grad, *grads, lags)


def reduce_kernel(scale, got, shared, held, lags, wide, in_sems, out_sems):
    copies = [
        pltpu.make_async_copy(
            got.at[8 * k : 8 * k + 8], held.at[8 * k : 8 * k + 8], in_sems.at[k]
        )
        for k in range(4)
    ]
    for copy in copies:
        copy.start()
    total = jnp.zeros((16, 1024), F32)
    sums = [jnp.zeros((16, 128), F32) for _ in range(8)]
    for k in range(4):
        copies[k].wait()
        for s in range(8):
            total = total + held[8 * k + s, :, 0:1024].astype(F32)
            sums[s] = sums[s] + held[8 * k + s, :, 1024:1152].astype(F32)
    total = (total * scale).astype(BF)
    low = low_lanes(16)
    for q in range(4):
        a, b = sums[2 * q] * scale, sums[2 * q + 1] * scale
        sides = (jnp.where(low, turned(a), b), jnp.where(low, a, turned(b)))
        for s in range(8):
            start = 4 * (s // 2)
            lags[s, 4 * q : 4 * q + 4] = sides[s % 2][start : start + 4]
    for s in range(8):
        wide[s, :, 0:1024] = total
        wide[s, :, 1024:1152] = lags[s].astype(BF)
    copies = [
        pltpu.make_async_copy(wide, shared.at[8 * k : 8 * k + 8], out_sems.at[k])
        for k in range(8)
    ]
    for copy in copies:
        copy.start()
    for copy in copies:
        copy.wait()


def reduce(got, scale):
    return pl.pallas_call(
        functools.partial(reduce_kernel, scale),
        in_specs=[pl.BlockSpec(memory_space=pltpu.HBM)],
        out_specs=pl.BlockSpec(memory_space=pltpu.HBM),
        out_shape=jax.ShapeDtypeStruct((64, 16, 1152), BF),
        scratch_shapes=[
            pltpu.VMEM((32, 16, 1152), BF),
            pltpu.VMEM((8, 16, 128), F32),
            pltpu.VMEM((8, 16, 1152), BF),
            pltpu.SemaphoreType.DMA((4,)),
            pltpu.SemaphoreType.DMA((8,)),
        ],
        compiler_params=pltpu.CompilerParams(vmem_limit_bytes=KEEP_OUT),
        name="reduce",
    )(got)


def start_writes(place, rows, grad_weight, held, wide, in_sems, out_sems, more=()):
    reads = [
        pltpu.make_async_copy(
            rows.at[8 * n : 8 * n + 8, :, 0:1024], held.at[n], in_sems.at[n]
        )
        for n in range(8)
    ]
    for copy in reads + list(more):
        copy.start()
    copies = []
    for n in range(8):
        reads[n].wait()
        zh, zl, yh = n // 4, n // 2 % 2, n % 2
        for k in range(8):
            wide[n, 16 * k : 16 * k + 16] = held[n, k].astype(F32)
        there = slice(128 * (2 * zh + yh), 128 * (2 * zh + yh) + 128)
        lanes = pl.ds(pl.multiple_of(2048 * place[0] + 1024 * zl, 1024), 1024)
        copies.append(
            pltpu.make_async_copy(wide.at[n], grad_weight.at[there, lanes], out_sems.at[n])
        )
        copies[-1].start()
    return copies


def first_kernel(place, rows, grad_weight, *scratch):
    for copy in start_writes(place, rows, grad_weight, *scratch):
        copy.wait()


def last_kernel(
    place, rows, mine, whole, grad_weight, grad_filter, lags, sums, filt, lag_sems, *scratch
):
    reads = [
        pltpu.make_async_copy(src.at[:, :, 1024:1152], lags.at[n], lag_sems.at[n])
        for n, src in enumerate((rows, mine))
    ]
    copies = start_writes(place, rows, grad_weight, *scratch, more=reads)
    for copy in reads:
        copy.wait()
    sums[...] = (lags[0].astype(F32) + lags[1].astype(F32)).reshape(1024, 128)
    for q in range(4):
        for k in range(4):
            part = sums[pl.ds(4 * q + k, 64, stride=16), :]
            filt[64 * k : 64 * k + 64, 128 * q : 128 * q + 128] = part
    copies.append(pltpu.make_async_copy(filt, grad_filter, lag_sems.at[2]))
    copies[-1].start()
    for copy in copies:
        copy.wait()


def write_half(half, rows, mine=None, whole=None):
    last = whole is not None
    hbm = pl.BlockSpec(memory_space=pltpu.HBM)
    shapes = [jax.ShapeDtypeStruct((512, 4096), F32)]
    if last:
        shapes.append(jax.ShapeDtypeStruct((BLOCK, 512), F32))
    return pl.pallas_call(
        last_kernel if last else first_kernel,
        grid_spec=pltpu.PrefetchScalarGridSpec(
            num_scalar_prefetch=1,
            grid=(1,),
            in_specs=[hbm] + [hbm, hbm] * last,
            out_specs=[hbm] + [hbm] * last,
            scratch_shapes=[
                pltpu.VMEM((2, 64, 16, 128), BF),
                pltpu.VMEM((1024, 128), F32),
                pltpu.VMEM((BLOCK, 512), F32),
                pltpu.SemaphoreType.DMA((3,)),
            ]
            * last
            + [
                pltpu.VMEM((8, 8, 16, 1024), BF),
                pltpu.VMEM((8, 128, 1024), F32),
                pltpu.SemaphoreType.DMA((8,)),
                pltpu.SemaphoreType.DMA((8,)),
            ],
        ),
        out_shape=shapes,
        input_output_aliases={3: 0} if last else {},
        cost_estimate=pl.CostEstimate(flops=10**6, bytes_accessed=6 * 10**6, transcendentals=0),
        compiler_params=pltpu.CompilerParams(vmem_limit_bytes=KEEP_OUT),
        name="write_last" if last else "write_first",
    )(half, rows, *([mine, whole] if last else []))


def exchange(x, axes):
    return lax.all_to_all(x, axes, 0, 0, tiled=True)


def across(x):
    return lax.ppermute(x, "c", [(0, 1), (1, 0)])


def along(x, step):
    return lax.ppermute(x, SEQ, [(n, n + step) for n in range(8) if 0 <= n + step < 8])


def above(x):
    return lax.ppermute(x, "zl", [(0, 1), (1, 0)])


def opposite(x):
    return lax.ppermute(x, ("zl", "c"), [(n, 3 - n) for n in range(4)])


def on_device(streams, short_filter, long_filter, skip_gain, out_weight, out_grad):
    scale = 1.0 / math.sqrt(16 * 2048)
    core = lax.axis_index("c").astype(jnp.int32)
    side = lax.axis_index("zl").astype(jnp.int32)
    seq = lax.axis_index(SEQ).astype(jnp.int32)
    grad = out_grad[0]

    def quarter(c, z):
        return lax.dynamic_slice(grad, (0, 1024 * (2 * c + z)), (BLOCK, 1024))

    grads = (
        above(quarter(core, 1 - side)),
        across(quarter(1 - core, side)),
        opposite(quarter(1 - core, 1 - side)),
    )
    short = short_filter
    packed, grad_mixed, gate_out = pack(streams[:, 0], grad, out_weight, long_filter, short)
    got = exchange(packed, SEQ)
    edge = along(streams[0, 0, BLOCK - 8 :], 1)
    later = along(grad_mixed[:8], -1)
    place = jnp.stack([seq, side])
    gain = skip_gain.reshape(1, 512)
    sent = conv(place, got, short, gain)
    sent, got, grads, edge, later = lax.optimization_barrier((sent, got, grads, edge, later))
    lags_own, lags = lag_sums(place, got, short, gain)
    back = exchange(sent, SEQ)
    back, lags_own, lags = lax.optimization_barrier((back, lags_own, lags))
    m00, joined = unpack_mixed(back, gate_out, edge, short, lags)
    m01, m10 = above(joined), across(m00)
    mixed = (m00, m01, m10, across(m01[:, :512]))
    part = partial((2 * core + side)[None], mixed, grad, grads, lags_own)
    part, m00, back = lax.optimization_barrier((part, m00, back))
    part = exchange(part, MOST)
    layer_out = jnp.dot(m00, out_weight, preferred_element_type=F32).astype(BF)
    part, m00, layer_out = lax.optimization_barrier((part, m00, layer_out))
    rows, back = lax.optimization_barrier((reduce(part, scale), back))
    mine = exchange(rows, CHIPS)
    grad_streams = unpack_grads(back, grad_mixed, later, short)
    mine, grad_streams = lax.optimization_barrier((mine, grad_streams))
    theirs = across(mine)
    grad_weight = write_half(core[None], mine)[0]
    grad_weight, grad_filter = write_half(1 - core[None], theirs, mine, grad_weight)
    return layer_out[None], grad_streams[:, None], grad_filter, grad_weight


def solution(mesh):
    fine = Mesh(
        mesh.devices.reshape(2, 2, 2, 2, 4, 2), ("zh", "zl", "yh", "c", "x", "yl")
    )
    dp = ("zh", "zl", "yh", "c")
    placed = (P(None, dp, SEQ, None), P(), P(SEQ, None), P(), P(), P(dp, SEQ, None))
    return jax.shard_map(
        on_device,
        mesh=fine,
        in_specs=placed,
        out_specs=(P(dp, SEQ, None), P(None, dp, SEQ, None), P(SEQ, None), P()),
        check_vma=False,
    )
```

```python
import functools
import math

import jax
import jax.numpy as jnp
import numpy as np
from jax import lax
from jax.experimental import pallas as pl
from jax.experimental.pallas import tpu as pltpu
from jax.sharding import Mesh, PartitionSpec as P

BF = jnp.bfloat16
F32 = jnp.float32
BLOCK = 256
HALF = 64
SENT_ROWS = BLOCK + 16
KEEP_OUT = 63 * 2**20
SEQ = ("x", "yl")
MOST = ("zh", "yh") + SEQ
DEPTH = ("zh", "zl", "yh")
CHIPS = DEPTH + SEQ


@functools.lru_cache(maxsize=None)
def tables():
    order = np.concatenate([np.arange(0, BLOCK, 2), np.arange(1, BLOCK, 2)])
    angle = np.pi * ((2 * order[:, None] + 1) * np.arange(BLOCK)[None, :] % 1024) / 512.0
    ahead = np.concatenate([np.cos(angle), -np.sin(angle)], axis=0)
    back = ahead.T / BLOCK

    def two(table):
        table = table.astype(np.float32)
        high = table.astype(jnp.bfloat16)
        return high, (table - high.astype(np.float32)).astype(jnp.bfloat16)

    return two(ahead) + two(back)


def mm(a, b):
    return jnp.dot(a, b, preferred_element_type=F32)


def low_lanes(rows):
    return lax.broadcasted_iota(jnp.int32, (rows, 128), 1) < HALF


def turned(x):
    return pltpu.roll(x, HALF, 1)


def pack_kernel(streams, out_grad, weight, filt, short, packed, grad, gate_out, pad):
    step = pl.program_id(0)
    low, low16 = low_lanes(BLOCK), low_lanes(16)

    @pl.when(step == 0)
    def _():
        grad[...] = jnp.zeros_like(grad)

    grad[...] += lax.dot_general(
        out_grad[...], weight[...], (((1,), (1,)), ((), ())), preferred_element_type=F32
    )

    for q in range(4):

        @pl.when(step == q)
        def _(q=q):
            lanes = slice(128 * q, 128 * q + 128)
            a, b = streams[1, :, lanes].astype(F32), streams[2, :, lanes].astype(F32)
            packed[2 * q, 0:BLOCK, 0:128] = jnp.where(low, a, turned(b)).astype(BF)
            packed[2 * q + 1, 0:BLOCK, 0:128] = jnp.where(low, turned(a), b).astype(BF)
            pad[0:8] = jnp.zeros((8, 128), F32)
            pad[8:] = streams[0, :, lanes].astype(F32)
            gate_out[:, lanes] = sum(
                short[0, j : j + 1, lanes] * pad[8 - j : 8 - j + BLOCK] for j in range(3)
            )

    @pl.when(step == pl.num_programs(0) - 1)
    def _():
        for q in range(4):
            lanes = slice(128 * q, 128 * q + 128)
            a, b = grad[:, lanes] * gate_out[:, lanes], filt[:, lanes]
            packed[2 * q, 0:BLOCK, 128:256] = jnp.where(low, a, turned(b)).astype(BF)
            packed[2 * q + 1, 0:BLOCK, 128:256] = jnp.where(low, turned(a), b).astype(BF)
            ends = streams[0, :, lanes].astype(F32)
            a = jnp.concatenate([ends[0:8], ends[BLOCK - 8 :]], axis=0)
            b = grad[0:16, lanes]
            packed[2 * q, BLOCK:, 0:128] = jnp.where(low16, a, turned(b)).astype(BF)
            packed[2 * q + 1, BLOCK:, 0:128] = jnp.where(low16, turned(a), b).astype(BF)
            packed[2 * q, BLOCK:, 128:256] = jnp.zeros((16, 128), BF)
            packed[2 * q + 1, BLOCK:, 128:256] = jnp.zeros((16, 128), BF)


def pack(streams, out_grad, weight, filt, short):
    steps = 4
    wide = out_grad.shape[1] // steps
    full = lambda *shape: pl.BlockSpec(shape, lambda k: (0,) * len(shape))
    return pl.pallas_call(
        pack_kernel,
        grid=(steps,),
        in_specs=[
            full(3, BLOCK, 512),
            pl.BlockSpec((BLOCK, wide), lambda k: (0, k)),
            pl.BlockSpec((512, wide), lambda k: (0, k)),
            full(BLOCK, 512),
            full(3, 3, 512),
        ],
        out_specs=[full(8, SENT_ROWS, 256), full(BLOCK, 512), full(BLOCK, 512)],
        out_shape=[
            jax.ShapeDtypeStruct((8, SENT_ROWS, 256), BF),
            jax.ShapeDtypeStruct((BLOCK, 512), F32),
            jax.ShapeDtypeStruct((BLOCK, 512), F32),
        ],
        scratch_shapes=[pltpu.VMEM((8 + BLOCK, 128), F32)],
        name="pack",
    )(streams, out_grad, weight, filt, short)


def split(x):
    high = x.astype(BF)
    return high, (x - high.astype(F32)).astype(BF)


def apply(table_h, table_l, high, rest):
    return mm(table_h[...], high) + mm(table_h[...], rest) + mm(table_l[...], high)


def weights(place, short, skip):
    low1 = low_lanes(1)
    odd = place[0] % 2 == 1
    taps = jnp.concatenate([short[n] for n in range(3)], axis=0)
    taps = jnp.where(odd, turned(taps), taps)
    taps_up = turned(taps)
    gain = skip[...]
    gain = jnp.where(odd, turned(gain), gain)
    gain = jnp.where(low1, gain, turned(gain))

    def pair(first, second):
        def row(table, i, j):
            if i is None:
                return jnp.full((1, 128), 1.0 if j == 0 else 0.0, F32)
            return table[3 * i + j : 3 * i + j + 1]

        return [
            jnp.where(low1, row(taps, first, j), row(taps_up, second, j)) for j in range(3)
        ]

    return pair, gain


def prepare(got, pair, pad, prod, gates=None):
    taps = pair(1, 2)
    low = low_lanes(BLOCK)
    pad[0:8] = jnp.zeros((8, 128), F32)

    def load(b, carry):
        rows = pl.ds(pl.multiple_of(8 + BLOCK * b, 8), BLOCK)
        pad[rows] = got[b, 0:BLOCK, 0:128].astype(F32)
        return carry

    lax.fori_loop(0, 8, load, 0)
    for b in range(8):
        start = 8 + BLOCK * b
        s = sum(taps[j] * pad[start - j : start - j + BLOCK] for j in range(3))
        if gates is not None:
            gates[b] = s
        prod[b] = jnp.where(low, s * turned(s), turned(got[b, 0:BLOCK, 128:256].astype(F32)))
    low8 = low_lanes(8)
    gate = pair(0, None)
    for b in range(8):
        ends = got[b, BLOCK:, 0:128].astype(F32)
        first = got[b - 1, BLOCK:, 0:128].astype(F32)[8:] if b else jnp.zeros((8, 128), F32)
        pad[0:8] = first
        pad[8:16] = ends[0:8]
        out = sum(gate[j] * pad[8 - j : 16 - j] for j in range(3))
        prod[b, 0:8] = jnp.where(low8, prod[b, 0:8], turned(out) * ends[0:8])


def spectra(prod, ahead_h, ahead_l, spec):
    low = low_lanes(BLOCK)
    sigma = jnp.where(low, 1.0, -1.0)

    def transform(n, carry):
        x = jnp.concatenate(
            [jnp.where(low, prod[b], prod[7 - b]) for b in (2 * n, 2 * n + 1)], axis=1
        )
        out = apply(ahead_h, ahead_l, *split(x))
        for t in range(2):
            spec[2 * n + t, 0:BLOCK] = out[:BLOCK, 128 * t : 128 * t + 128]
            spec[2 * n + t, BLOCK:] = out[BLOCK:, 128 * t : 128 * t + 128] * sigma
        return carry

    lax.fori_loop(0, 4, transform, 0)


def over_bins(spec, use):
    for sign, base in ((1.0, 0), (-1.0, 128)):

        def step(n, carry, sign=sign, base=base):
            re = pl.ds(pl.multiple_of(base + 8 * n, 8), 8)
            im = pl.ds(pl.multiple_of(BLOCK + base + 8 * n, 8), 8)
            own = [(spec[j, re], spec[j, im]) for j in range(8)]
            both = [own[0]]
            for j in range(1, 8):
                both.append(
                    (own[j][0] - sign * own[j - 1][1], own[j][1] + sign * own[j - 1][0])
                )
            use(re, im, own, both)
            return carry

        lax.fori_loop(0, 16, step, 0)


def summed(pairs):
    first = True
    for (ar, ai), (br, bi) in pairs:
        pr = ar * br - ai * bi
        pi = ar * bi + ai * br
        tr, ti = (pr, pi) if first else (tr + pr, ti + pi)
        first = False
    return tr, ti


def flipped(x, sign):
    return jnp.concatenate([x[0:BLOCK], x[BLOCK:] * sign], axis=0)


def conv_kernel(
    place, got, short, skip, ahead_h, ahead_l, back_h, back_l,
    sent,
    pad, prod, gates, spec, fspec, res, time, after,
):
    low = low_lanes(BLOCK)
    sigma = jnp.where(low, 1.0, -1.0)
    pair, gain = weights(place, short, skip)

    def filters(n, carry):
        def blocks(b):
            x, y = (got[n, 0:BLOCK, 128:256].astype(F32) for n in (b, b + 1))
            return jnp.where(low, turned(x), y).astype(BF)

        f = jnp.concatenate([blocks(4 * n), blocks(4 * n + 2)], axis=1)
        out = mm(ahead_h[...], f) + mm(ahead_l[...], f)
        low512 = low_lanes(512)
        for t in range(2):
            x = out[:, 128 * t : 128 * t + 128]
            y = turned(x)
            fspec[4 * n + 2 * t] = jnp.where(low512, x, y)
            fspec[4 * n + 2 * t + 1] = jnp.where(low512, y, x)
        return carry

    lax.fori_loop(0, 2, filters, 0)
    prepare(got, pair, pad, prod, gates)
    spectra(prod, ahead_h, ahead_l, spec)

    def multiply(re, im, own, both):
        filt = [(fspec[m, re], fspec[m, im]) for m in range(8)]
        for i in range(8):
            tr, ti = summed([(filt[m], both[i - m]) for m in range(i + 1)])
            res[i, re] = tr
            res[i, im] = ti

    over_bins(spec, multiply)

    def invert(n, carry):
        x = jnp.concatenate([flipped(res[b], sigma) for b in (2 * n, 2 * n + 1)], axis=1)
        out = apply(back_h, back_l, *split(x))
        time[2 * n] = out[:, :128]
        time[2 * n + 1] = out[:, 128:]
        return carry

    lax.fori_loop(0, 4, invert, 0)

    low128 = low_lanes(128)

    def gate(b, carry):
        t = jnp.where(low, time[b], time[7 - b]) + gain * prod[b]
        rows = pl.ds(pl.multiple_of(BLOCK * b, 8), BLOCK)
        after[rows] = jnp.where(low, turned(t), t) * turned(gates[b])
        sent[b, BLOCK:384] = jnp.where(low128, t[0:128], turned(t[128:256])).astype(BF)
        return carry

    lax.fori_loop(0, 8, gate, 0)
    low8 = low_lanes(8)
    for b in range(8):
        if b < 7:
            t = jnp.where(low8, time[b + 1, 0:8], time[6 - b, 0:8]) + gain * prod[b + 1, 0:8]
        else:
            t = jnp.zeros((8, 128), F32)
        sent[b, 384:400] = jnp.concatenate([t, t], axis=0).astype(BF)
    after[8 * BLOCK :] = jnp.zeros((8, 128), F32)
    taps = pair(1, 2)
    for b in range(8):
        start = BLOCK * b
        y = sum(taps[j] * after[start + j : start + j + BLOCK] for j in range(3))
        sent[b, 0:BLOCK] = y.astype(BF)


def lag_kernel(
    place, got, short, skip, ahead_h, ahead_l, back_h, back_l,
    lags, lags_z,
    pad, prod, spec, lres, rows,
):
    pair, _ = weights(place, short, skip)
    prepare(got, pair, pad, prod)
    spectra(prod, ahead_h, ahead_l, spec)
    zero = jnp.zeros((8, 128), F32)
    low8 = low_lanes(8)

    def multiply(re, im, own, both):
        grads, shifted = [], []
        for i in range(8):
            grads.append(
                tuple(jnp.where(low8, turned(own[7 - i][k]), own[7 - i][k]) for k in range(2))
            )
            before = both[i - 1] if i else (zero, zero)
            shifted.append(
                tuple(jnp.where(low8, before[k], turned(both[i][k])) for k in range(2))
            )
        for a in range(4):
            tr, ti = summed([(grads[i], shifted[i - 2 * a]) for i in range(2 * a, 8)])
            lres[a, re] = tr
            lres[a, im] = ti

    over_bins(spec, multiply)

    def invert(n, carry):
        x = jnp.concatenate([flipped(lres[a], -1.0) for a in (2 * n, 2 * n + 1)], axis=1)
        out = apply(back_h, back_l, *split(x))
        for t in range(2):
            for k in range(4):
                there = pl.ds(8 * n + 4 * t + k, 64, stride=16)
                rows[there, :] = out[64 * k : 64 * k + 64, 128 * t : 128 * t + 128]
        return carry

    for n in range(2):
        invert(n, 0)
    for z in range(2):
        for ref, side in ((lags, place[1]), (lags_z, 1 - place[1])):
            part = rows[pl.ds(pl.multiple_of(512 * z + 256 * side, 256), 256), :]
            ref[16 * z : 16 * z + 16] = part.reshape(16, 16, 128).astype(BF)


def on_channels(kernel, name, inputs, in_shapes, outputs, scratch, cost):
    full = lambda *shape: pl.BlockSpec(shape, lambda n, p: (0,) * len(shape))
    return pl.pallas_call(
        kernel,
        grid_spec=pltpu.PrefetchScalarGridSpec(
            num_scalar_prefetch=1,
            grid=(1,),
            in_specs=[
                full(8, SENT_ROWS, 256),
                pl.BlockSpec((3, 3, 128), lambda n, p: (0, 0, p[0] // 2)),
                pl.BlockSpec((1, 128), lambda n, p: (0, p[0] // 2)),
            ]
            + [full(*shape) for shape in in_shapes],
            out_specs=[full(*shape) for shape, _ in outputs],
            scratch_shapes=[
                pltpu.VMEM(shape, dtype)
                for shape, dtype in [((8 + 8 * BLOCK, 128), F32)] + scratch
            ],
        ),
        out_shape=[jax.ShapeDtypeStruct(shape, dtype) for shape, dtype in outputs],
        cost_estimate=cost,
        name=name,
    )(*inputs)


TABLES = [(512, BLOCK), (512, BLOCK), (BLOCK, 512), (BLOCK, 512)]
BLOCKS = ((8, BLOCK, 128), F32)
BINS = ((8, 512, 128), F32)


def spent(flops):
    return pl.CostEstimate(flops=flops, bytes_accessed=3 * 10**6, transcendentals=0)


def conv(place, got, short, skip):
    inputs = (place, got, short, skip, *(jnp.asarray(t) for t in tables()))
    outputs = [((8, 400, 128), BF)]
    scratch = [BLOCKS, BLOCKS, BINS, BINS, BINS, BLOCKS, ((8 * BLOCK + 8, 128), F32)]
    return on_channels(conv_kernel, "conv", inputs, TABLES, outputs, scratch, None)[0]


def lag_sums(place, got, short, skip):
    inputs = (place, got, short, skip, *(jnp.asarray(t) for t in tables()))
    outputs = [((32, 16, 128), BF)] * 2
    scratch = [BLOCKS, BINS, ((4, 512, 128), F32), ((1024, 128), F32)]
    cost = spent(2 * 10**9)
    return on_channels(lag_kernel, "lag_sums", inputs, TABLES, outputs, scratch, cost)


def convolved(got, q, start, low128):
    there = slice(start, start + 128)
    a, b = got[2 * q, there].astype(F32), got[2 * q + 1, there].astype(F32)
    return jnp.where(low128, a, turned(b)), jnp.where(low128, turned(a), b)


def mixed_kernel(got, gate_out, edge, short, lags, mixed, joined, pad):
    low128 = low_lanes(128)
    pad[0:8] = edge[...].astype(F32)
    pad[8:] = jnp.zeros((8, 512), F32)
    more = sum(short[0, j : j + 1] * pad[8 - j : 16 - j] for j in (1, 2))
    for q in range(4):
        lanes = slice(128 * q, 128 * q + 128)
        first, second = convolved(got, q, 0, low128)
        gate = gate_out[0:128, lanes]
        gate = jnp.concatenate([gate[0:8] + more[:, lanes], gate[8:]], axis=0)
        for ref in (mixed, joined):
            ref[0:128, lanes] = (gate * first).astype(BF)
            ref[128:256, lanes] = (gate_out[128:256, lanes] * second).astype(BF)
    for n in range(32):
        start, lane = 16 * (n % 16), 512 + 128 * (n // 16)
        joined[start : start + 16, lane : lane + 128] = lags[n]


def unpack_mixed(got, gate_out, edge, short, lags):
    full = lambda *shape: pl.BlockSpec(shape, lambda n: (0,) * len(shape))
    return pl.pallas_call(
        mixed_kernel,
        grid=(1,),
        in_specs=[
            pl.BlockSpec((8, 128, 128), lambda n: (0, 2, 0)),
            full(BLOCK, 512),
            full(8, 512),
            full(3, 3, 512),
            full(32, 16, 128),
        ],
        out_specs=[full(BLOCK, 512), full(BLOCK, 768)],
        out_shape=[
            jax.ShapeDtypeStruct((BLOCK, 512), BF),
            jax.ShapeDtypeStruct((BLOCK, 768), BF),
        ],
        scratch_shapes=[pltpu.VMEM((16, 512), F32)],
        name="unpack_mixed",
    )(got, gate_out, edge, short, lags)


def grads_kernel(got, grad, later, short, grads, pad):
    low, low128, low8 = low_lanes(BLOCK), low_lanes(128), low_lanes(8)
    for q in range(4):
        lanes = slice(128 * q, 128 * q + 128)
        first, second = convolved(got, q, BLOCK, low128)
        pad[0:128, lanes] = grad[0:128, lanes] * first
        pad[128:256, lanes] = grad[128:256, lanes] * second
        a, b = (got[2 * q + n, 384:400].astype(F32)[0:8] for n in range(2))
        pad[256:264, lanes] = later[:, lanes] * jnp.where(low8, a, turned(b))
        a, b = got[2 * q, 0:BLOCK].astype(F32), got[2 * q + 1, 0:BLOCK].astype(F32)
        grads[1, :, lanes] = jnp.where(low, a, turned(b)).astype(BF)
        grads[2, :, lanes] = jnp.where(low, turned(a), b).astype(BF)
        grads[0, :, lanes] = sum(
            short[0, j : j + 1, lanes] * pad[j : j + BLOCK, lanes] for j in range(3)
        ).astype(BF)


def unpack_grads(got, grad, later, short):
    return pl.pallas_call(
        grads_kernel,
        out_shape=jax.ShapeDtypeStruct((3, BLOCK, 512), BF),
        scratch_shapes=[pltpu.VMEM((BLOCK + 8, 512), F32)],
        cost_estimate=pl.CostEstimate(flops=10**6, bytes_accessed=2 * 10**6, transcendentals=0),
        name="unpack_grads",
    )(got, grad, later, short)


def partial_kernel(place, m00, m01, m10, m11, g00, g01, g10, g11, lags, packed):
    def term(mixed, grad):
        return lax.dot_general(
            mixed[:, 0:512], grad[...], (((0,), (0,)), ((), ())), preferred_element_type=F32
        )

    part = term(m00, g00) + term(m01, g01) + term(m10, g10) + term(m11, g11)
    part = part.astype(BF)
    for n in range(32):
        packed[n, :, 0:1024] = part[16 * n : 16 * n + 16]
        start, lane = 16 * (n % 16), 512 + 128 * (n // 16)
        lag_z = m01[start : start + 16, lane : lane + 128]
        lag = lags[n].astype(F32) + lag_z.astype(F32)
        packed[n, :, 1024:1152] = lag.astype(BF)


def partial(place, mixed, grad, grads, lags):
    full = lambda *shape: pl.BlockSpec(shape, lambda n, p: (0,) * len(shape))
    return pl.pallas_call(
        partial_kernel,
        grid_spec=pltpu.PrefetchScalarGridSpec(
            num_scalar_prefetch=1,
            grid=(1,),
            in_specs=[full(BLOCK, 512), full(BLOCK, 768), full(BLOCK, 512), full(BLOCK, 512)]
            + [pl.BlockSpec((BLOCK, 1024), lambda n, p: (0, p[0]))]
            + [full(BLOCK, 1024)] * 3
            + [full(32, 16, 128)],
            out_specs=full(32, 16, 1152),
        ),
        out_shape=jax.ShapeDtypeStruct((32, 16, 1152), BF),
        name="partial",
    )(place, *mixed, grad, *grads, lags)


def reduce_kernel(scale, got, shared, held, lags, wide, in_sems, out_sems):
    copies = [
        pltpu.make_async_copy(
            got.at[8 * k : 8 * k + 8], held.at[8 * k : 8 * k + 8], in_sems.at[k]
        )
        for k in range(4)
    ]
    for copy in copies:
        copy.start()
    total = jnp.zeros((16, 1024), F32)
    sums = [jnp.zeros((16, 128), F32) for _ in range(8)]
    for k in range(4):
        copies[k].wait()
        for s in range(8):
            total = total + held[8 * k + s, :, 0:1024].astype(F32)
            sums[s] = sums[s] + held[8 * k + s, :, 1024:1152].astype(F32)
    total = (total * scale).astype(BF)
    low = low_lanes(16)
    for q in range(4):
        a, b = sums[2 * q] * scale, sums[2 * q + 1] * scale
        sides = (jnp.where(low, turned(a), b), jnp.where(low, a, turned(b)))
        for s in range(8):
            start = 4 * (s // 2)
            lags[s, 4 * q : 4 * q + 4] = sides[s % 2][start : start + 4]
    for s in range(8):
        wide[s, :, 0:1024] = total
        wide[s, :, 1024:1152] = lags[s].astype(BF)
    copies = [
        pltpu.make_async_copy(wide, shared.at[8 * k : 8 * k + 8], out_sems.at[k])
        for k in range(8)
    ]
    for copy in copies:
        copy.start()
    for copy in copies:
        copy.wait()


def reduce(got, scale):
    return pl.pallas_call(
        functools.partial(reduce_kernel, scale),
        in_specs=[pl.BlockSpec(memory_space=pltpu.HBM)],
        out_specs=pl.BlockSpec(memory_space=pltpu.HBM),
        out_shape=jax.ShapeDtypeStruct((64, 16, 1152), BF),
        scratch_shapes=[
            pltpu.VMEM((32, 16, 1152), BF),
            pltpu.VMEM((8, 16, 128), F32),
            pltpu.VMEM((8, 16, 1152), BF),
            pltpu.SemaphoreType.DMA((4,)),
            pltpu.SemaphoreType.DMA((8,)),
        ],
        compiler_params=pltpu.CompilerParams(vmem_limit_bytes=KEEP_OUT),
        name="reduce",
    )(got)


def start_writes(place, rows, grad_weight, held, wide, in_sems, out_sems, more=()):
    reads = [
        pltpu.make_async_copy(
            rows.at[8 * n : 8 * n + 8, :, 0:1024], held.at[n], in_sems.at[n]
        )
        for n in range(8)
    ]
    for copy in reads + list(more):
        copy.start()
    copies = []
    for n in range(8):
        reads[n].wait()
        zh, zl, yh = n // 4, n // 2 % 2, n % 2
        for k in range(8):
            wide[n, 16 * k : 16 * k + 16] = held[n, k].astype(F32)
        there = slice(128 * (2 * zh + yh), 128 * (2 * zh + yh) + 128)
        lanes = pl.ds(pl.multiple_of(2048 * place[0] + 1024 * zl, 1024), 1024)
        copies.append(
            pltpu.make_async_copy(wide.at[n], grad_weight.at[there, lanes], out_sems.at[n])
        )
        copies[-1].start()
    return copies


def first_kernel(place, rows, grad_weight, *scratch):
    for copy in start_writes(place, rows, grad_weight, *scratch):
        copy.wait()


def last_kernel(
    place, rows, mine, whole, grad_weight, grad_filter, lags, sums, filt, lag_sems, *scratch
):
    reads = [
        pltpu.make_async_copy(src.at[:, :, 1024:1152], lags.at[n], lag_sems.at[n])
        for n, src in enumerate((rows, mine))
    ]
    copies = start_writes(place, rows, grad_weight, *scratch, more=reads)
    for copy in reads:
        copy.wait()
    sums[...] = (lags[0].astype(F32) + lags[1].astype(F32)).reshape(1024, 128)
    for q in range(4):
        for k in range(4):
            part = sums[pl.ds(4 * q + k, 64, stride=16), :]
            filt[64 * k : 64 * k + 64, 128 * q : 128 * q + 128] = part
    copies.append(pltpu.make_async_copy(filt, grad_filter, lag_sems.at[2]))
    copies[-1].start()
    for copy in copies:
        copy.wait()


def write_half(half, rows, mine=None, whole=None):
    last = whole is not None
    hbm = pl.BlockSpec(memory_space=pltpu.HBM)
    shapes = [jax.ShapeDtypeStruct((512, 4096), F32)]
    if last:
        shapes.append(jax.ShapeDtypeStruct((BLOCK, 512), F32))
    return pl.pallas_call(
        last_kernel if last else first_kernel,
        grid_spec=pltpu.PrefetchScalarGridSpec(
            num_scalar_prefetch=1,
            grid=(1,),
            in_specs=[hbm] + [hbm, hbm] * last,
            out_specs=[hbm] + [hbm] * last,
            scratch_shapes=[
                pltpu.VMEM((2, 64, 16, 128), BF),
                pltpu.VMEM((1024, 128), F32),
                pltpu.VMEM((BLOCK, 512), F32),
                pltpu.SemaphoreType.DMA((3,)),
            ]
            * last
            + [
                pltpu.VMEM((8, 8, 16, 1024), BF),
                pltpu.VMEM((8, 128, 1024), F32),
                pltpu.SemaphoreType.DMA((8,)),
                pltpu.SemaphoreType.DMA((8,)),
            ],
        ),
        out_shape=shapes,
        input_output_aliases={3: 0} if last else {},
        cost_estimate=pl.CostEstimate(flops=10**6, bytes_accessed=6 * 10**6, transcendentals=0),
        name="write_last" if last else "write_first",
    )(half, rows, *([mine, whole] if last else []))


def exchange(x, axes):
    return lax.all_to_all(x, axes, 0, 0, tiled=True)


def across(x):
    return lax.ppermute(x, "c", [(0, 1), (1, 0)])


def along(x, step):
    return lax.ppermute(x, SEQ, [(n, n + step) for n in range(8) if 0 <= n + step < 8])


def above(x):
    return lax.ppermute(x, "zl", [(0, 1), (1, 0)])


def opposite(x):
    return lax.ppermute(x, ("zl", "c"), [(n, 3 - n) for n in range(4)])


def on_device(streams, short_filter, long_filter, skip_gain, out_weight, out_grad):
    scale = 1.0 / math.sqrt(16 * 2048)
    core = lax.axis_index("c").astype(jnp.int32)
    side = lax.axis_index("zl").astype(jnp.int32)
    seq = lax.axis_index(SEQ).astype(jnp.int32)
    grad = out_grad[0]

    def quarter(c, z):
        return lax.dynamic_slice(grad, (0, 1024 * (2 * c + z)), (BLOCK, 1024))

    grads = (
        above(quarter(core, 1 - side)),
        across(quarter(1 - core, side)),
        opposite(quarter(1 - core, 1 - side)),
    )
    short = short_filter
    packed, grad_mixed, gate_out = pack(streams[:, 0], grad, out_weight, long_filter, short)
    got = exchange(packed, SEQ)
    edge = along(streams[0, 0, BLOCK - 8 :], 1)
    later = along(grad_mixed[:8], -1)
    place = jnp.stack([seq, side])
    gain = skip_gain.reshape(1, 512)
    sent = conv(place, got, short, gain)
    sent, got, grads, edge, later = lax.optimization_barrier((sent, got, grads, edge, later))
    lags_own, lags = lag_sums(place, got, short, gain)
    back = exchange(sent, SEQ)
    back, lags_own, lags = lax.optimization_barrier((back, lags_own, lags))
    m00, joined = unpack_mixed(back, gate_out, edge, short, lags)
    m01, m10 = above(joined), across(m00)
    mixed = (m00, m01, m10, across(m01[:, :512]))
    part = partial((2 * core + side)[None], mixed, grad, grads, lags_own)
    part, m00, back = lax.optimization_barrier((part, m00, back))
    part = exchange(part, MOST)
    layer_out = jnp.dot(m00, out_weight, preferred_element_type=F32).astype(BF)
    part, m00, layer_out = lax.optimization_barrier((part, m00, layer_out))
    rows, back = lax.optimization_barrier((reduce(part, scale), back))
    mine = exchange(rows, CHIPS)
    grad_streams = unpack_grads(back, grad_mixed, later, short)
    mine, grad_streams = lax.optimization_barrier((mine, grad_streams))
    theirs = across(mine)
    grad_weight = write_half(core[None], mine)[0]
    grad_weight, grad_filter = write_half(1 - core[None], theirs, mine, grad_weight)
    return layer_out[None], grad_streams[:, None], grad_filter, grad_weight


def solution(mesh):
    fine = Mesh(
        mesh.devices.reshape(2, 2, 2, 2, 4, 2), ("zh", "zl", "yh", "c", "x", "yl")
    )
    dp = ("zh", "zl", "yh", "c")
    placed = (P(None, dp, SEQ, None), P(), P(SEQ, None), P(), P(), P(dp, SEQ, None))
    return jax.shard_map(
        on_device,
        mesh=fine,
        in_specs=placed,
        out_specs=(P(dp, SEQ, None), P(None, dp, SEQ, None), P(SEQ, None), P()),
        check_vma=False,
    )
```

```python
import functools
import math

import jax
import jax.numpy as jnp
import numpy as np
from jax import lax
from jax.experimental import pallas as pl
from jax.experimental.pallas import tpu as pltpu
from jax.sharding import Mesh, PartitionSpec as P

BF = jnp.bfloat16
F32 = jnp.float32
BLOCK = 256
HALF = 64
SENT_ROWS = BLOCK + 16
KEEP_OUT = 63 * 2**20
SEQ = ("x", "yl")
MOST = ("zh", "yh") + SEQ
DEPTH = ("zh", "zl", "yh")
CHIPS = DEPTH + SEQ


@functools.lru_cache(maxsize=None)
def tables():
    order = np.concatenate([np.arange(0, BLOCK, 2), np.arange(1, BLOCK, 2)])
    angle = np.pi * ((2 * order[:, None] + 1) * np.arange(BLOCK)[None, :] % 1024) / 512.0
    ahead = np.concatenate([np.cos(angle), -np.sin(angle)], axis=0)
    back = ahead.T / BLOCK

    def two(table):
        table = table.astype(np.float32)
        high = table.astype(jnp.bfloat16)
        return high, (table - high.astype(np.float32)).astype(jnp.bfloat16)

    return two(ahead) + two(back)


def mm(a, b):
    return jnp.dot(a, b, preferred_element_type=F32)


def low_lanes(rows):
    return lax.broadcasted_iota(jnp.int32, (rows, 128), 1) < HALF


def turned(x):
    return pltpu.roll(x, HALF, 1)


def pack_kernel(streams, out_grad, weight, filt, short, packed, grad, gate_out, pad):
    step = pl.program_id(0)
    low, low16 = low_lanes(BLOCK), low_lanes(16)

    @pl.when(step == 0)
    def _():
        grad[...] = jnp.zeros_like(grad)

    grad[...] += lax.dot_general(
        out_grad[...], weight[...], (((1,), (1,)), ((), ())), preferred_element_type=F32
    )

    for q in range(4):

        @pl.when(step == q)
        def _(q=q):
            lanes = slice(128 * q, 128 * q + 128)
            a, b = streams[1, :, lanes].astype(F32), streams[2, :, lanes].astype(F32)
            packed[2 * q, 0:BLOCK, 0:128] = jnp.where(low, a, turned(b)).astype(BF)
            packed[2 * q + 1, 0:BLOCK, 0:128] = jnp.where(low, turned(a), b).astype(BF)
            pad[0:8] = jnp.zeros((8, 128), F32)
            pad[8:] = streams[0, :, lanes].astype(F32)
            gate_out[:, lanes] = sum(
                short[0, j : j + 1, lanes] * pad[8 - j : 8 - j + BLOCK] for j in range(3)
            )

    @pl.when(step == pl.num_programs(0) - 1)
    def _():
        for q in range(4):
            lanes = slice(128 * q, 128 * q + 128)
            a, b = grad[:, lanes] * gate_out[:, lanes], filt[:, lanes]
            packed[2 * q, 0:BLOCK, 128:256] = jnp.where(low, a, turned(b)).astype(BF)
            packed[2 * q + 1, 0:BLOCK, 128:256] = jnp.where(low, turned(a), b).astype(BF)
            ends = streams[0, :, lanes].astype(F32)
            a = jnp.concatenate([ends[0:8], ends[BLOCK - 8 :]], axis=0)
            b = grad[0:16, lanes]
            packed[2 * q, BLOCK:, 0:128] = jnp.where(low16, a, turned(b)).astype(BF)
            packed[2 * q + 1, BLOCK:, 0:128] = jnp.where(low16, turned(a), b).astype(BF)
            packed[2 * q, BLOCK:, 128:256] = jnp.zeros((16, 128), BF)
            packed[2 * q + 1, BLOCK:, 128:256] = jnp.zeros((16, 128), BF)


def pack(streams, out_grad, weight, filt, short):
    steps = 4
    wide = out_grad.shape[1] // steps
    full = lambda *shape: pl.BlockSpec(shape, lambda k: (0,) * len(shape))
    return pl.pallas_call(
        pack_kernel,
        grid=(steps,),
        in_specs=[
            full(3, BLOCK, 512),
            pl.BlockSpec((BLOCK, wide), lambda k: (0, k)),
            pl.BlockSpec((512, wide), lambda k: (0, k)),
            full(BLOCK, 512),
            full(3, 3, 512),
        ],
        out_specs=[full(8, SENT_ROWS, 256), full(BLOCK, 512), full(BLOCK, 512)],
        out_shape=[
            jax.ShapeDtypeStruct((8, SENT_ROWS, 256), BF),
            jax.ShapeDtypeStruct((BLOCK, 512), F32),
            jax.ShapeDtypeStruct((BLOCK, 512), F32),
        ],
        scratch_shapes=[pltpu.VMEM((8 + BLOCK, 128), F32)],
        name="pack",
    )(streams, out_grad, weight, filt, short)


def split(x):
    high = x.astype(BF)
    return high, (x - high.astype(F32)).astype(BF)


def apply(table_h, table_l, high, rest):
    return mm(table_h[...], high) + mm(table_h[...], rest) + mm(table_l[...], high)


def weights(place, short, skip):
    low1 = low_lanes(1)
    odd = place[0] % 2 == 1
    taps = jnp.concatenate([short[n] for n in range(3)], axis=0)
    taps = jnp.where(odd, turned(taps), taps)
    taps_up = turned(taps)
    gain = skip[...]
    gain = jnp.where(odd, turned(gain), gain)
    gain = jnp.where(low1, gain, turned(gain))

    def pair(first, second):
        def row(table, i, j):
            if i is None:
                return jnp.full((1, 128), 1.0 if j == 0 else 0.0, F32)
            return table[3 * i + j : 3 * i + j + 1]

        return [
            jnp.where(low1, row(taps, first, j), row(taps_up, second, j)) for j in range(3)
        ]

    return pair, gain


def prepare(got, pair, pad, prod, gates=None):
    taps = pair(1, 2)
    low = low_lanes(BLOCK)
    pad[0:8] = jnp.zeros((8, 128), F32)

    def load(b, carry):
        rows = pl.ds(pl.multiple_of(8 + BLOCK * b, 8), BLOCK)
        pad[rows] = got[b, 0:BLOCK, 0:128].astype(F32)
        return carry

    lax.fori_loop(0, 8, load, 0)
    for b in range(8):
        start = 8 + BLOCK * b
        s = sum(taps[j] * pad[start - j : start - j + BLOCK] for j in range(3))
        if gates is not None:
            gates[b] = s
        prod[b] = jnp.where(low, s * turned(s), turned(got[b, 0:BLOCK, 128:256].astype(F32)))
    low8 = low_lanes(8)
    gate = pair(0, None)
    for b in range(8):
        ends = got[b, BLOCK:, 0:128].astype(F32)
        first = got[b - 1, BLOCK:, 0:128].astype(F32)[8:] if b else jnp.zeros((8, 128), F32)
        pad[0:8] = first
        pad[8:16] = ends[0:8]
        out = sum(gate[j] * pad[8 - j : 16 - j] for j in range(3))
        prod[b, 0:8] = jnp.where(low8, prod[b, 0:8], turned(out) * ends[0:8])


def spectra(prod, ahead_h, ahead_l, spec):
    low = low_lanes(BLOCK)
    sigma = jnp.where(low, 1.0, -1.0)

    def transform(n, carry):
        x = jnp.concatenate(
            [jnp.where(low, prod[b], prod[7 - b]) for b in (2 * n, 2 * n + 1)], axis=1
        )
        out = apply(ahead_h, ahead_l, *split(x))
        for t in range(2):
            spec[2 * n + t, 0:BLOCK] = out[:BLOCK, 128 * t : 128 * t + 128]
            spec[2 * n + t, BLOCK:] = out[BLOCK:, 128 * t : 128 * t + 128] * sigma
        return carry

    lax.fori_loop(0, 4, transform, 0)


def over_bins(spec, use):
    for sign, base in ((1.0, 0), (-1.0, 128)):

        def step(n, carry, sign=sign, base=base):
            re = pl.ds(pl.multiple_of(base + 8 * n, 8), 8)
            im = pl.ds(pl.multiple_of(BLOCK + base + 8 * n, 8), 8)
            own = [(spec[j, re], spec[j, im]) for j in range(8)]
            both = [own[0]]
            for j in range(1, 8):
                both.append(
                    (own[j][0] - sign * own[j - 1][1], own[j][1] + sign * own[j - 1][0])
                )
            use(re, im, own, both)
            return carry

        lax.fori_loop(0, 16, step, 0)


def summed(pairs):
    first = True
    for (ar, ai), (br, bi) in pairs:
        pr = ar * br - ai * bi
        pi = ar * bi + ai * br
        tr, ti = (pr, pi) if first else (tr + pr, ti + pi)
        first = False
    return tr, ti


def flipped(x, sign):
    return jnp.concatenate([x[0:BLOCK], x[BLOCK:] * sign], axis=0)


def conv_kernel(
    place, got, short, skip, ahead_h, ahead_l, back_h, back_l,
    sent,
    pad, prod, gates, spec, fspec, res, time, after,
):
    low = low_lanes(BLOCK)
    sigma = jnp.where(low, 1.0, -1.0)
    pair, gain = weights(place, short, skip)

    def filters(n, carry):
        def blocks(b):
            x, y = (got[n, 0:BLOCK, 128:256].astype(F32) for n in (b, b + 1))
            return jnp.where(low, turned(x), y).astype(BF)

        f = jnp.concatenate([blocks(4 * n), blocks(4 * n + 2)], axis=1)
        out = mm(ahead_h[...], f) + mm(ahead_l[...], f)
        low512 = low_lanes(512)
        for t in range(2):
            x = out[:, 128 * t : 128 * t + 128]
            y = turned(x)
            fspec[4 * n + 2 * t] = jnp.where(low512, x, y)
            fspec[4 * n + 2 * t + 1] = jnp.where(low512, y, x)
        return carry

    lax.fori_loop(0, 2, filters, 0)
    prepare(got, pair, pad, prod, gates)
    spectra(prod, ahead_h, ahead_l, spec)

    def multiply(re, im, own, both):
        filt = [(fspec[m, re], fspec[m, im]) for m in range(8)]
        for i in range(8):
            tr, ti = summed([(filt[m], both[i - m]) for m in range(i + 1)])
            res[i, re] = tr
            res[i, im] = ti

    over_bins(spec, multiply)

    def invert(n, carry):
        x = jnp.concatenate([flipped(res[b], sigma) for b in (2 * n, 2 * n + 1)], axis=1)
        out = apply(back_h, back_l, *split(x))
        time[2 * n] = out[:, :128]
        time[2 * n + 1] = out[:, 128:]
        return carry

    lax.fori_loop(0, 4, invert, 0)

    low128 = low_lanes(128)

    def gate(b, carry):
        t = jnp.where(low, time[b], time[7 - b]) + gain * prod[b]
        rows = pl.ds(pl.multiple_of(BLOCK * b, 8), BLOCK)
        after[rows] = jnp.where(low, turned(t), t) * turned(gates[b])
        sent[b, BLOCK:384] = jnp.where(low128, t[0:128], turned(t[128:256])).astype(BF)
        return carry

    lax.fori_loop(0, 8, gate, 0)
    low8 = low_lanes(8)
    for b in range(8):
        if b < 7:
            t = jnp.where(low8, time[b + 1, 0:8], time[6 - b, 0:8]) + gain * prod[b + 1, 0:8]
        else:
            t = jnp.zeros((8, 128), F32)
        sent[b, 384:400] = jnp.concatenate([t, t], axis=0).astype(BF)
    after[8 * BLOCK :] = jnp.zeros((8, 128), F32)
    taps = pair(1, 2)
    for b in range(8):
        start = BLOCK * b
        y = sum(taps[j] * after[start + j : start + j + BLOCK] for j in range(3))
        sent[b, 0:BLOCK] = y.astype(BF)


def lag_kernel(
    place, got, short, skip, ahead_h, ahead_l, back_h, back_l,
    lags, lags_z,
    pad, prod, spec, lres, rows,
):
    pair, _ = weights(place, short, skip)
    prepare(got, pair, pad, prod)
    spectra(prod, ahead_h, ahead_l, spec)
    zero = jnp.zeros((8, 128), F32)
    low8 = low_lanes(8)

    def multiply(re, im, own, both):
        grads, shifted = [], []
        for i in range(8):
            grads.append(
                tuple(jnp.where(low8, turned(own[7 - i][k]), own[7 - i][k]) for k in range(2))
            )
            before = both[i - 1] if i else (zero, zero)
            shifted.append(
                tuple(jnp.where(low8, before[k], turned(both[i][k])) for k in range(2))
            )
        for a in range(4):
            tr, ti = summed([(grads[i], shifted[i - 2 * a]) for i in range(2 * a, 8)])
            lres[a, re] = tr
            lres[a, im] = ti

    over_bins(spec, multiply)

    def invert(n, carry):
        x = jnp.concatenate([flipped(lres[a], -1.0) for a in (2 * n, 2 * n + 1)], axis=1)
        out = apply(back_h, back_l, *split(x))
        for t in range(2):
            for k in range(4):
                there = pl.ds(8 * n + 4 * t + k, 64, stride=16)
                rows[there, :] = out[64 * k : 64 * k + 64, 128 * t : 128 * t + 128]
        return carry

    for n in range(2):
        invert(n, 0)
    for z in range(2):
        for ref, side in ((lags, place[1]), (lags_z, 1 - place[1])):
            part = rows[pl.ds(pl.multiple_of(512 * z + 256 * side, 256), 256), :]
            ref[16 * z : 16 * z + 16] = part.reshape(16, 16, 128).astype(BF)


def on_channels(kernel, name, inputs, in_shapes, outputs, scratch, cost):
    full = lambda *shape: pl.BlockSpec(shape, lambda n, p: (0,) * len(shape))
    return pl.pallas_call(
        kernel,
        grid_spec=pltpu.PrefetchScalarGridSpec(
            num_scalar_prefetch=1,
            grid=(1,),
            in_specs=[
                full(8, SENT_ROWS, 256),
                pl.BlockSpec((3, 3, 128), lambda n, p: (0, 0, p[0] // 2)),
                pl.BlockSpec((1, 128), lambda n, p: (0, p[0] // 2)),
            ]
            + [full(*shape) for shape in in_shapes],
            out_specs=[full(*shape) for shape, _ in outputs],
            scratch_shapes=[
                pltpu.VMEM(shape, dtype)
                for shape, dtype in [((8 + 8 * BLOCK, 128), F32)] + scratch
            ],
        ),
        out_shape=[jax.ShapeDtypeStruct(shape, dtype) for shape, dtype in outputs],
        cost_estimate=cost,
        compiler_params=pltpu.CompilerParams(vmem_limit_bytes=KEEP_OUT if cost is None else None),
        name=name,
    )(*inputs)


TABLES = [(512, BLOCK), (512, BLOCK), (BLOCK, 512), (BLOCK, 512)]
BLOCKS = ((8, BLOCK, 128), F32)
BINS = ((8, 512, 128), F32)


def spent(flops):
    return pl.CostEstimate(flops=flops, bytes_accessed=3 * 10**6, transcendentals=0)


def conv(place, got, short, skip):
    inputs = (place, got, short, skip, *(jnp.asarray(t) for t in tables()))
    outputs = [((8, 400, 128), BF)]
    scratch = [BLOCKS, BLOCKS, BINS, BINS, BINS, BLOCKS, ((8 * BLOCK + 8, 128), F32)]
    return on_channels(conv_kernel, "conv", inputs, TABLES, outputs, scratch, None)[0]


def lag_sums(place, got, short, skip):
    inputs = (place, got, short, skip, *(jnp.asarray(t) for t in tables()))
    outputs = [((32, 16, 128), BF)] * 2
    scratch = [BLOCKS, BINS, ((4, 512, 128), F32), ((1024, 128), F32)]
    cost = spent(2 * 10**9)
    return on_channels(lag_kernel, "lag_sums", inputs, TABLES, outputs, scratch, cost)


def convolved(got, q, start, low128):
    there = slice(start, start + 128)
    a, b = got[2 * q, there].astype(F32), got[2 * q + 1, there].astype(F32)
    return jnp.where(low128, a, turned(b)), jnp.where(low128, turned(a), b)


def mixed_kernel(got, gate_out, edge, short, lags, mixed, joined, pad):
    low128 = low_lanes(128)
    pad[0:8] = edge[...].astype(F32)
    pad[8:] = jnp.zeros((8, 512), F32)
    more = sum(short[0, j : j + 1] * pad[8 - j : 16 - j] for j in (1, 2))
    for q in range(4):
        lanes = slice(128 * q, 128 * q + 128)
        first, second = convolved(got, q, 0, low128)
        gate = gate_out[0:128, lanes]
        gate = jnp.concatenate([gate[0:8] + more[:, lanes], gate[8:]], axis=0)
        for ref in (mixed, joined):
            ref[0:128, lanes] = (gate * first).astype(BF)
            ref[128:256, lanes] = (gate_out[128:256, lanes] * second).astype(BF)
    for n in range(32):
        start, lane = 16 * (n % 16), 512 + 128 * (n // 16)
        joined[start : start + 16, lane : lane + 128] = lags[n]


def unpack_mixed(got, gate_out, edge, short, lags):
    full = lambda *shape: pl.BlockSpec(shape, lambda n: (0,) * len(shape))
    return pl.pallas_call(
        mixed_kernel,
        grid=(1,),
        in_specs=[
            pl.BlockSpec((8, 128, 128), lambda n: (0, 2, 0)),
            full(BLOCK, 512),
            full(8, 512),
            full(3, 3, 512),
            full(32, 16, 128),
        ],
        out_specs=[full(BLOCK, 512), full(BLOCK, 768)],
        out_shape=[
            jax.ShapeDtypeStruct((BLOCK, 512), BF),
            jax.ShapeDtypeStruct((BLOCK, 768), BF),
        ],
        scratch_shapes=[pltpu.VMEM((16, 512), F32)],
        name="unpack_mixed",
    )(got, gate_out, edge, short, lags)


def grads_kernel(got, grad, later, short, grads, pad):
    low, low128, low8 = low_lanes(BLOCK), low_lanes(128), low_lanes(8)
    for q in range(4):
        lanes = slice(128 * q, 128 * q + 128)
        first, second = convolved(got, q, BLOCK, low128)
        pad[0:128, lanes] = grad[0:128, lanes] * first
        pad[128:256, lanes] = grad[128:256, lanes] * second
        a, b = (got[2 * q + n, 384:400].astype(F32)[0:8] for n in range(2))
        pad[256:264, lanes] = later[:, lanes] * jnp.where(low8, a, turned(b))
        a, b = got[2 * q, 0:BLOCK].astype(F32), got[2 * q + 1, 0:BLOCK].astype(F32)
        grads[1, :, lanes] = jnp.where(low, a, turned(b)).astype(BF)
        grads[2, :, lanes] = jnp.where(low, turned(a), b).astype(BF)
        grads[0, :, lanes] = sum(
            short[0, j : j + 1, lanes] * pad[j : j + BLOCK, lanes] for j in range(3)
        ).astype(BF)


def unpack_grads(got, grad, later, short):
    return pl.pallas_call(
        grads_kernel,
        out_shape=jax.ShapeDtypeStruct((3, BLOCK, 512), BF),
        scratch_shapes=[pltpu.VMEM((BLOCK + 8, 512), F32)],
        cost_estimate=pl.CostEstimate(flops=10**6, bytes_accessed=2 * 10**6, transcendentals=0),
        name="unpack_grads",
    )(got, grad, later, short)


def partial_kernel(place, m00, m01, m10, m11, g00, g01, g10, g11, lags, packed):
    def term(mixed, grad):
        return lax.dot_general(
            mixed[:, 0:512], grad[...], (((0,), (0,)), ((), ())), preferred_element_type=F32
        )

    part = term(m00, g00) + term(m01, g01) + term(m10, g10) + term(m11, g11)
    part = part.astype(BF)
    for n in range(32):
        packed[n, :, 0:1024] = part[16 * n : 16 * n + 16]
        start, lane = 16 * (n % 16), 512 + 128 * (n // 16)
        lag_z = m01[start : start + 16, lane : lane + 128]
        lag = lags[n].astype(F32) + lag_z.astype(F32)
        packed[n, :, 1024:1152] = lag.astype(BF)


def partial(place, mixed, grad, grads, lags):
    full = lambda *shape: pl.BlockSpec(shape, lambda n, p: (0,) * len(shape))
    return pl.pallas_call(
        partial_kernel,
        grid_spec=pltpu.PrefetchScalarGridSpec(
            num_scalar_prefetch=1,
            grid=(1,),
            in_specs=[full(BLOCK, 512), full(BLOCK, 768), full(BLOCK, 512), full(BLOCK, 512)]
            + [pl.BlockSpec((BLOCK, 1024), lambda n, p: (0, p[0]))]
            + [full(BLOCK, 1024)] * 3
            + [full(32, 16, 128)],
            out_specs=full(32, 16, 1152),
        ),
        out_shape=jax.ShapeDtypeStruct((32, 16, 1152), BF),
        name="partial",
    )(place, *mixed, grad, *grads, lags)


def reduce_kernel(scale, got, shared, held, lags, wide, in_sems, out_sems):
    copies = [
        pltpu.make_async_copy(
            got.at[8 * k : 8 * k + 8], held.at[8 * k : 8 * k + 8], in_sems.at[k]
        )
        for k in range(4)
    ]
    for copy in copies:
        copy.start()
    total = jnp.zeros((16, 1024), F32)
    sums = [jnp.zeros((16, 128), F32) for _ in range(8)]
    for k in range(4):
        copies[k].wait()
        for s in range(8):
            total = total + held[8 * k + s, :, 0:1024].astype(F32)
            sums[s] = sums[s] + held[8 * k + s, :, 1024:1152].astype(F32)
    total = (total * scale).astype(BF)
    low = low_lanes(16)
    for q in range(4):
        a, b = sums[2 * q] * scale, sums[2 * q + 1] * scale
        sides = (jnp.where(low, turned(a), b), jnp.where(low, a, turned(b)))
        for s in range(8):
            start = 4 * (s // 2)
            lags[s, 4 * q : 4 * q + 4] = sides[s % 2][start : start + 4]
    for s in range(8):
        wide[s, :, 0:1024] = total
        wide[s, :, 1024:1152] = lags[s].astype(BF)
    copies = [
        pltpu.make_async_copy(wide, shared.at[8 * k : 8 * k + 8], out_sems.at[k])
        for k in range(8)
    ]
    for copy in copies:
        copy.start()
    for copy in copies:
        copy.wait()


def reduce(got, scale):
    return pl.pallas_call(
        functools.partial(reduce_kernel, scale),
        in_specs=[pl.BlockSpec(memory_space=pltpu.HBM)],
        out_specs=pl.BlockSpec(memory_space=pltpu.HBM),
        out_shape=jax.ShapeDtypeStruct((64, 16, 1152), BF),
        scratch_shapes=[
            pltpu.VMEM((32, 16, 1152), BF),
            pltpu.VMEM((8, 16, 128), F32),
            pltpu.VMEM((8, 16, 1152), BF),
            pltpu.SemaphoreType.DMA((4,)),
            pltpu.SemaphoreType.DMA((8,)),
        ],
        compiler_params=pltpu.CompilerParams(vmem_limit_bytes=KEEP_OUT),
        name="reduce",
    )(got)


def start_writes(place, rows, grad_weight, held, wide, in_sems, out_sems, more=()):
    reads = [
        pltpu.make_async_copy(
            rows.at[8 * n : 8 * n + 8, :, 0:1024], held.at[n], in_sems.at[n]
        )
        for n in range(8)
    ]
    for copy in reads + list(more):
        copy.start()
    copies = []
    for n in range(8):
        reads[n].wait()
        zh, zl, yh = n // 4, n // 2 % 2, n % 2
        for k in range(8):
            wide[n, 16 * k : 16 * k + 16] = held[n, k].astype(F32)
        there = slice(128 * (2 * zh + yh), 128 * (2 * zh + yh) + 128)
        lanes = pl.ds(pl.multiple_of(2048 * place[0] + 1024 * zl, 1024), 1024)
        copies.append(
            pltpu.make_async_copy(wide.at[n], grad_weight.at[there, lanes], out_sems.at[n])
        )
        copies[-1].start()
    return copies


def first_kernel(place, rows, grad_weight, *scratch):
    for copy in start_writes(place, rows, grad_weight, *scratch):
        copy.wait()


def last_kernel(
    place, rows, mine, whole, grad_weight, grad_filter, lags, sums, filt, lag_sems, *scratch
):
    reads = [
        pltpu.make_async_copy(src.at[:, :, 1024:1152], lags.at[n], lag_sems.at[n])
        for n, src in enumerate((rows, mine))
    ]
    copies = start_writes(place, rows, grad_weight, *scratch, more=reads)
    for copy in reads:
        copy.wait()
    sums[...] = (lags[0].astype(F32) + lags[1].astype(F32)).reshape(1024, 128)
    for q in range(4):
        for k in range(4):
            part = sums[pl.ds(4 * q + k, 64, stride=16), :]
            filt[64 * k : 64 * k + 64, 128 * q : 128 * q + 128] = part
    copies.append(pltpu.make_async_copy(filt, grad_filter, lag_sems.at[2]))
    copies[-1].start()
    for copy in copies:
        copy.wait()


def write_half(half, rows, mine=None, whole=None):
    last = whole is not None
    hbm = pl.BlockSpec(memory_space=pltpu.HBM)
    shapes = [jax.ShapeDtypeStruct((512, 4096), F32)]
    if last:
        shapes.append(jax.ShapeDtypeStruct((BLOCK, 512), F32))
    return pl.pallas_call(
        last_kernel if last else first_kernel,
        grid_spec=pltpu.PrefetchScalarGridSpec(
            num_scalar_prefetch=1,
            grid=(1,),
            in_specs=[hbm] + [hbm, hbm] * last,
            out_specs=[hbm] + [hbm] * last,
            scratch_shapes=[
                pltpu.VMEM((2, 64, 16, 128), BF),
                pltpu.VMEM((1024, 128), F32),
                pltpu.VMEM((BLOCK, 512), F32),
                pltpu.SemaphoreType.DMA((3,)),
            ]
            * last
            + [
                pltpu.VMEM((8, 8, 16, 1024), BF),
                pltpu.VMEM((8, 128, 1024), F32),
                pltpu.SemaphoreType.DMA((8,)),
                pltpu.SemaphoreType.DMA((8,)),
            ],
        ),
        out_shape=shapes,
        input_output_aliases={3: 0} if last else {},
        cost_estimate=pl.CostEstimate(flops=10**6, bytes_accessed=6 * 10**6, transcendentals=0),
        name="write_last" if last else "write_first",
    )(half, rows, *([mine, whole] if last else []))


def exchange(x, axes):
    return lax.all_to_all(x, axes, 0, 0, tiled=True)


def across(x):
    return lax.ppermute(x, "c", [(0, 1), (1, 0)])


def along(x, step):
    return lax.ppermute(x, SEQ, [(n, n + step) for n in range(8) if 0 <= n + step < 8])


def above(x):
    return lax.ppermute(x, "zl", [(0, 1), (1, 0)])


def opposite(x):
    return lax.ppermute(x, ("zl", "c"), [(n, 3 - n) for n in range(4)])


def on_device(streams, short_filter, long_filter, skip_gain, out_weight, out_grad):
    scale = 1.0 / math.sqrt(16 * 2048)
    core = lax.axis_index("c").astype(jnp.int32)
    side = lax.axis_index("zl").astype(jnp.int32)
    seq = lax.axis_index(SEQ).astype(jnp.int32)
    grad = out_grad[0]

    def quarter(c, z):
        return lax.dynamic_slice(grad, (0, 1024 * (2 * c + z)), (BLOCK, 1024))

    grads = (
        above(quarter(core, 1 - side)),
        across(quarter(1 - core, side)),
        opposite(quarter(1 - core, 1 - side)),
    )
    short = short_filter
    packed, grad_mixed, gate_out = pack(streams[:, 0], grad, out_weight, long_filter, short)
    got = exchange(packed, SEQ)
    edge = along(streams[0, 0, BLOCK - 8 :], 1)
    later = along(grad_mixed[:8], -1)
    place = jnp.stack([seq, side])
    gain = skip_gain.reshape(1, 512)
    sent = conv(place, got, short, gain)
    sent, got, grads, edge, later = lax.optimization_barrier((sent, got, grads, edge, later))
    lags_own, lags = lag_sums(place, got, short, gain)
    back = exchange(sent, SEQ)
    back, lags_own, lags = lax.optimization_barrier((back, lags_own, lags))
    m00, joined = unpack_mixed(back, gate_out, edge, short, lags)
    m01, m10 = above(joined), across(m00)
    mixed = (m00, m01, m10, across(m01[:, :512]))
    part = partial((2 * core + side)[None], mixed, grad, grads, lags_own)
    part, m00, back = lax.optimization_barrier((part, m00, back))
    part = exchange(part, MOST)
    layer_out = jnp.dot(m00, out_weight, preferred_element_type=F32).astype(BF)
    part, m00, layer_out = lax.optimization_barrier((part, m00, layer_out))
    rows, back = lax.optimization_barrier((reduce(part, scale), back))
    mine = exchange(rows, CHIPS)
    grad_streams = unpack_grads(back, grad_mixed, later, short)
    mine, grad_streams = lax.optimization_barrier((mine, grad_streams))
    theirs = across(mine)
    grad_weight = write_half(core[None], mine)[0]
    grad_weight, grad_filter = write_half(1 - core[None], theirs, mine, grad_weight)
    return layer_out[None], grad_streams[:, None], grad_filter, grad_weight


def solution(mesh):
    fine = Mesh(
        mesh.devices.reshape(2, 2, 2, 2, 4, 2), ("zh", "zl", "yh", "c", "x", "yl")
    )
    dp = ("zh", "zl", "yh", "c")
    placed = (P(None, dp, SEQ, None), P(), P(SEQ, None), P(), P(), P(dp, SEQ, None))
    return jax.shard_map(
        on_device,
        mesh=fine,
        in_specs=placed,
        out_specs=(P(dp, SEQ, None), P(None, dp, SEQ, None), P(SEQ, None), P()),
        check_vma=False,
    )
```
